128 devices in a mesh: seq: 16 (over z, x), dp: 8 (over y, core).
Axes of the slice: x: 4, y: 4, z: 4, core: 2. Of those that a mesh axis runs over, the one named last changes fastest.
Arguments:
- query_input: bfloat16 [8, 8192, 2048], P('dp', 'seq'), may hold values from -300 to 300
- key_input: bfloat16 [8, 8192, 2048], P('dp', 'seq'), may hold values from -6 to 6
- value_input: bfloat16 [8, 8192, 2048], P('dp', 'seq'), may hold values from -6 to 6
- keep_blocks: int32 [8, 16], P('dp'), may hold values from 0 to 63, as said below
- dest_slots: int32 [8, 16], P('dp'), may hold values from 0 to 15, each once within a row
- proj_weights: bfloat16 [3, 2048, 2048], P(None, None, 'seq'), may hold values from -5 to 5
- cotangent: bfloat16 [8, 2048, 2048], P('dp', None, 'seq'), may hold values from -6 to 6
Outputs:
- window_out: bfloat16 [8, 8192, 2048], P('dp', 'seq')
- causal_out: bfloat16 [8, 2048, 2048], P('dp', None, 'seq')
- weight_grad: float32 [3, 2048, 2048], P(None, None, 'seq')
- row_grad: bfloat16 [8, 2048, 2048], P('dp', 'seq')
The draws below stay inside these ranges and needn't reach their ends.
Inputs may be any that keep to these rules, and one draw needn't show every extreme that they name: `keep_blocks`: each row lists 16 distinct block numbers in increasing order, block b covering positions b * 128 to b * 128 + 127. The 4 blocks on one index of seq contribute at most 2 kept blocks, and in every document some index of seq contributes exactly 2. `dest_slots`: each row is a permutation.
All inputs are finite; a program needn't handle non-finite values.
Results may differ from the reference program's by a relative error of at most 0.015.
Values may be sent and summed in bfloat16 or wider, within the bound.
A program may use at most 192 MiB of HBM per device.

```python
import jax
import jax.numpy as jnp
from jax import lax

H = 16
HEAD = 128
HD = 2048
WIN = 1024
BLK = 128
TOK_DEV = 512
TOKENS = 8192
DOCS = 8
KEPT = 16
MOST = 2
ROWS = 2048
HPD = 1
N_SEQ = 16


def key_field(key):
    base_field = jax.random.normal(jax.random.fold_in(key, 101), (DOCS, TOKENS, HD), jnp.float32)
    return jnp.clip(base_field, -6.0, 6.0)


def draw_key_input(key, part):
    return key_field(key).astype(jnp.bfloat16)


def draw_query_input(key, part):
    own_key = jax.random.fold_in(key, 202)
    base_field = 2.0 * jnp.clip(jax.random.normal(own_key, (DOCS, TOKENS, HD), jnp.float32), -6.0, 6.0)
    return base_field.astype(jnp.bfloat16)


def draw_proj_weights(key, part):
    base_field = jnp.clip(jax.random.normal(jax.random.fold_in(key, 303), (3, HD, HD), jnp.float32), -6.0, 6.0) * HD ** (-0.5)
    return base_field.astype(jnp.bfloat16)


def draw_keep_blocks(key, part):
    shards = TOKENS // TOK_DEV
    per_shard = TOK_DEV // BLK
    block_total = shards * per_shard

    def one_document(doc_index):
        doc_key = jax.random.fold_in(jax.random.fold_in(key, 404), doc_index)
        heavy_shard = jax.random.randint(jax.random.fold_in(doc_key, 1), (), 0, shards)
        shard_keys = jax.random.split(jax.random.fold_in(doc_key, 2), shards)
        block_ranks = jax.vmap(lambda shard_key: jax.random.permutation(shard_key, per_shard))(shard_keys).reshape(block_total)
        random_order = jax.random.permutation(jax.random.fold_in(doc_key, 3), block_total)
        owner_shard = jnp.arange(block_total) // per_shard
        candidate = block_ranks < MOST
        priority = jnp.where(candidate & (owner_shard == heavy_shard), block_ranks, jnp.where(candidate & (owner_shard != heavy_shard), MOST + random_order, MOST + block_total + jnp.arange(block_total)))
        picked = jnp.argsort(priority, stable=True)[:KEPT]
        return jnp.sort(picked).astype(jnp.int32)
    return jax.vmap(one_document)(jnp.arange(DOCS))


def levels(key, dims, cuts, smallest, high):
    def one(axis_at, parts):
        heights = jax.random.uniform(jax.random.fold_in(jax.random.fold_in(key, 6), axis_at), (parts,), jnp.float32, smallest / len(cuts), high / len(cuts))
        return jnp.repeat(jnp.exp(heights), dims[axis_at] // parts).reshape((-1,) + (1,) * (len(dims) - axis_at - 1))

    factor_of = one(*cuts[0])
    for cut in cuts[1:]:
        factor_of = factor_of * one(*cut)
    return factor_of


def gaussian(stream_key, extent, scale, bound, cuts=(), held_as=jnp.bfloat16):
    level = levels(stream_key, extent, cuts, -0.22, 0.18) if cuts else 1.0
    values = jax.random.normal(stream_key, extent, jnp.float32) * scale * level
    return jnp.minimum(jnp.maximum(values, -bound), bound).astype(held_as)


def setup_inputs(seed: int = 0) -> dict:
    keys = jax.random.split(jax.random.key(seed), 8)
    return {
        "query_input": draw_query_input(jax.random.fold_in(keys[7], 71), 0),
        "key_input": draw_key_input(jax.random.fold_in(keys[7], 71), 0),
        "value_input": gaussian(keys[2], (DOCS, TOKENS, HD), 1.0, 6.0, ((0, 8), (1, 16))),
        "keep_blocks": draw_keep_blocks(jax.random.fold_in(keys[7], 71), 0),
        "dest_slots": jax.vmap(lambda own: jax.random.permutation(own, KEPT))(jax.random.split(keys[4], DOCS)).reshape((DOCS, KEPT)).astype(jnp.int32),
        "proj_weights": draw_proj_weights(jax.random.fold_in(keys[7], 71), 0),
        "cotangent": gaussian(keys[6], (DOCS, ROWS, HD), 1.0, 6.0, ((0, 8), (2, 16))),
    }


def band_mask(row_count, shard_index):
    reach_rows = WIN - 1
    row_ids = jnp.arange(row_count)[:, None]
    col_ids = jnp.arange(row_count + reach_rows)[None, :]
    return (col_ids >= row_ids) & (col_ids <= row_ids + reach_rows) & (col_ids + shard_index * row_count >= reach_rows)

def window_head(query_rows, key_rows, value_rows, allowed):
    score_scale = HEAD ** (-0.5)
    scores = lax.dot_general(query_rows, key_rows, (((1,), (1,)), ((), ())), preferred_element_type=jnp.float32) * score_scale
    scores = jnp.where(allowed, scores, -1e+30)
    row_max = lax.optimization_barrier(jnp.max(scores, axis=1, keepdims=True))
    weight = jnp.where(allowed, jnp.exp(scores - row_max), 0.0)
    probabilities = (weight / lax.optimization_barrier(jnp.sum(weight, axis=1, keepdims=True))).astype(jnp.bfloat16)
    return jnp.dot(probabilities, value_rows, preferred_element_type=jnp.float32).astype(jnp.bfloat16)

def norm_rows(rows_in):
    values_f = rows_in.astype(jnp.float32)
    mean_square = lax.optimization_barrier(jnp.mean(values_f * values_f, axis=1, keepdims=True))
    return (values_f * lax.rsqrt(mean_square + 1e-06)).astype(jnp.bfloat16)

def global_head(query_rows, key_rows, value_rows, grad_rows, positions):
    row_count = query_rows.shape[0]
    block_rows = min(512, row_count)
    block_count = row_count // block_rows
    score_scale = HEAD ** (-0.5)

    def step_block(accumulators, block_index):
        key_acc, value_acc = accumulators
        start_row = (block_index * block_rows).astype(jnp.int32)
        query_block = lax.dynamic_slice_in_dim(query_rows, start_row, block_rows, 0)
        grad_block = lax.dynamic_slice_in_dim(grad_rows, start_row, block_rows, 0)
        place_block = lax.dynamic_slice_in_dim(positions, start_row, block_rows, 0)
        causal = positions[None, :] <= place_block[:, None]
        scores = lax.dot_general(query_block, key_rows, (((1,), (1,)), ((), ())), preferred_element_type=jnp.float32) * score_scale
        scores = jnp.where(causal, scores, -1e+30)
        row_max = lax.optimization_barrier(jnp.max(scores, axis=1, keepdims=True))
        weight = jnp.where(causal, jnp.exp(scores - row_max), 0.0)
        soft_weights = weight / lax.optimization_barrier(jnp.sum(weight, axis=1, keepdims=True))
        probabilities = soft_weights.astype(jnp.bfloat16)
        head_output = jnp.dot(probabilities, value_rows, preferred_element_type=jnp.float32).astype(jnp.bfloat16)
        d_probs = lax.dot_general(grad_block, value_rows, (((1,), (1,)), ((), ())), preferred_element_type=jnp.float32)
        value_acc = value_acc + lax.dot_general(probabilities, grad_block, (((0,), (0,)), ((), ())), preferred_element_type=jnp.float32)
        row_delta = lax.optimization_barrier(jnp.sum(soft_weights * d_probs, axis=1, keepdims=True))
        d_scores = (soft_weights * (d_probs - row_delta) * score_scale).astype(jnp.bfloat16)
        grad_query = jnp.dot(d_scores, key_rows, preferred_element_type=jnp.float32).astype(jnp.bfloat16)
        key_acc = key_acc + lax.dot_general(d_scores, query_block, (((0,), (0,)), ((), ())), preferred_element_type=jnp.float32)
        return ((key_acc, value_acc), (head_output, grad_query))
    zero_acc = jnp.zeros(key_rows.shape, jnp.float32)
    (key_acc, value_acc), (outputs, grad_queries) = lax.scan(step_block, (zero_acc, zero_acc), jnp.arange(block_count))
    head_width = query_rows.shape[1]
    return (outputs.reshape(row_count, head_width), grad_queries.reshape(row_count, head_width), key_acc.astype(jnp.bfloat16), value_acc.astype(jnp.bfloat16))

def compact_sources(keep_list, slot_list):
    order_inverse = jnp.argsort(slot_list).astype(jnp.int32)
    compact_ids = jnp.arange(keep_list.shape[0] * BLK, dtype=jnp.int32)
    kept_index = order_inverse[compact_ids // BLK]
    return (keep_list[kept_index] * BLK + compact_ids % BLK).astype(jnp.int32)

def regroup(stacked):
    return jnp.transpose(stacked, (1, 0, 2)).reshape(stacked.shape[1], stacked.shape[0] * stacked.shape[2])

def document(query_doc, key_doc, value_doc, keep_list, slot_list, proj_weights, grad_doc):
    zero_rows = jnp.zeros((WIN - 1, HD), key_doc.dtype)
    key_padded = jnp.concatenate([zero_rows, key_doc], axis=0)
    value_padded = jnp.concatenate([zero_rows, value_doc], axis=0)

    def head_window(head_index):
        column = (head_index * HEAD).astype(jnp.int32)
        query_head = lax.dynamic_slice_in_dim(query_doc, column, HEAD, 1)
        key_head = lax.dynamic_slice_in_dim(key_padded, column, HEAD, 1)
        value_head = lax.dynamic_slice_in_dim(value_padded, column, HEAD, 1)

        def block_window(block_index):
            start_row = (block_index * TOK_DEV).astype(jnp.int32)
            query_block = lax.dynamic_slice_in_dim(query_head, start_row, TOK_DEV, 0)
            key_block = lax.dynamic_slice_in_dim(key_head, start_row, TOK_DEV + WIN - 1, 0)
            value_block = lax.dynamic_slice_in_dim(value_head, start_row, TOK_DEV + WIN - 1, 0)
            return window_head(query_block, key_block, value_block, band_mask(TOK_DEV, block_index))
        return lax.map(block_window, jnp.arange(N_SEQ)).reshape(TOKENS, HEAD)
    window_out = regroup(lax.map(head_window, jnp.arange(H)))
    source = compact_sources(keep_list, slot_list)
    normed = norm_rows(window_out[source])
    q_rows = jnp.dot(normed, proj_weights[0], preferred_element_type=jnp.float32).astype(jnp.bfloat16)
    k_rows = jnp.dot(normed, proj_weights[1], preferred_element_type=jnp.float32).astype(jnp.bfloat16)
    v_rows = jnp.dot(normed, proj_weights[2], preferred_element_type=jnp.float32).astype(jnp.bfloat16)

    def head_causal(head_index):
        column = (head_index * HEAD).astype(jnp.int32)
        return global_head(lax.dynamic_slice_in_dim(q_rows, column, HEAD, 1), lax.dynamic_slice_in_dim(k_rows, column, HEAD, 1), lax.dynamic_slice_in_dim(v_rows, column, HEAD, 1), lax.dynamic_slice_in_dim(grad_doc, column, HEAD, 1), source)
    outputs, grad_query, grad_key, grad_value = lax.map(head_causal, jnp.arange(H))
    causal_out = regroup(outputs)
    grad_parts = (regroup(grad_query), regroup(grad_key), regroup(grad_value))
    weight_grads = jnp.stack([lax.dot_general(normed, part, (((0,), (0,)), ((), ())), preferred_element_type=jnp.float32) for part in grad_parts])
    group_width = HPD * HEAD

    def add_group(running_sum, group_index):
        column = (group_index * group_width).astype(jnp.int32)
        term = jnp.zeros((ROWS, HD), jnp.float32)
        for which_proj in range(3):
            grad_cols = lax.dynamic_slice_in_dim(grad_parts[which_proj], column, group_width, 1)
            weight_cols = lax.dynamic_slice_in_dim(proj_weights[which_proj], column, group_width, 1)
            term = term + lax.dot_general(grad_cols, weight_cols, (((1,), (1,)), ((), ())), preferred_element_type=jnp.float32)
        rounded = lax.optimization_barrier(term.astype(jnp.bfloat16))
        return (running_sum + rounded.astype(jnp.float32), None)
    row_sum, unused = lax.scan(add_group, jnp.zeros((ROWS, HD), jnp.float32), jnp.arange(N_SEQ))
    return (window_out, causal_out, weight_grads, row_sum.astype(jnp.bfloat16))

def reference(query_input, key_input, value_input, keep_blocks, dest_slots, proj_weights, cotangent):

    def per_document(running_sum, doc_items):
        query_doc, key_doc, value_doc, keep_list, slot_list, grad_doc = doc_items
        window_out, causal_out, weight_grads, row_grad = document(query_doc, key_doc, value_doc, keep_list, slot_list, proj_weights, grad_doc)
        return (running_sum + weight_grads, (window_out, causal_out, row_grad))
    start_sum = jnp.zeros((3, HD, HD), jnp.float32)
    weight_grad, (window_out, causal_out, row_grad) = lax.scan(per_document, start_sum, (query_input, key_input, value_input, keep_blocks, dest_slots, cotangent))
    return (window_out, causal_out, weight_grad, row_grad)
```

```python
import functools

import jax
import jax.numpy as jnp
from jax import lax
from jax.experimental import pallas as pl
from jax.experimental.pallas import tpu as pltpu
from jax.sharding import PartitionSpec as P

HEAD = 128
BLK = 128
SEQ = "seq"
MESH = pl.DeviceIdType.MESH
SCALE = HEAD ** (-0.5)
LOG2E = 1.4426950408889634
SCALE2 = SCALE * LOG2E
LOW = -1e30
NT = (((1,), (1,)), ((), ()))
BF16 = jnp.bfloat16
F32 = jnp.float32
VMEM_LIMIT = 56 * 1024 * 1024


def window_part(query, key, value_t, bias):
    scores = lax.dot_general(key, query, NT, preferred_element_type=F32)
    if bias is not None:
        scores = scores + bias
    top = jnp.max(scores, axis=0, keepdims=True)
    weight = jnp.exp2((scores - top) * SCALE2)
    total = jnp.sum(weight, axis=0, keepdims=True)
    out = jnp.dot(value_t, weight.astype(BF16), preferred_element_type=F32)
    return out / total, top * SCALE2 + jnp.log2(total)


def merged(out_a, lse_a, out_b, lse_b):
    top = jnp.maximum(lse_a, lse_b)
    weight_a = jnp.exp2(lse_a - top)
    weight_b = jnp.exp2(lse_b - top)
    total = weight_a + weight_b
    return out_a * (weight_a / total) + out_b * (weight_b / total), top + jnp.log2(total)


def window_kernel(
    chunks, per_chunk, sel, q_in, k_in, v_in, out,
    q_own, q_one, q_two, v_t, o_own, l_own, o_snd2, l_snd2, o_got2, l_got2, o_snd1, l_snd1, o_got1, l_got1,
    bias_own, bias_two, send_sem, recv_sem,
):
    shard = lax.axis_index(SEQ)
    count = lax.axis_size(SEQ)
    right = lax.rem(shard + 1, count)
    left = lax.rem(shard + count - 1, count)
    width = per_chunk * HEAD
    rows = q_own.shape[1]
    picks = rows // BLK

    def copy(which, c, src, dst, target):
        return pltpu.make_async_remote_copy(
            src_ref=src.at[c], dst_ref=dst.at[c],
            send_sem=send_sem.at[which, c], recv_sem=recv_sem.at[which, c],
            device_id={SEQ: target}, device_id_type=MESH,
        )

    def hop_one(c):
        return copy(0, c, q_own, q_one, left)

    def hop_two(c):
        return copy(1, c, q_one, q_two, left)

    def back_two(c):
        return (copy(2, c, o_snd2, o_got2, right), copy(3, c, l_snd2, l_got2, right))

    def back_one(c):
        return (copy(4, c, o_snd1, o_got1, right), copy(5, c, l_snd1, l_got1, right))

    barrier = pltpu.get_barrier_semaphore()
    for neighbour in (left, right):
        pl.semaphore_signal(barrier, inc=1, device_id={SEQ: neighbour}, device_id_type=MESH)

    for a in range(picks):
        block = q_in[sel[a]]
        for c in range(chunks):
            q_own[c, a * BLK : (a + 1) * BLK, :] = block[:, c * width : (c + 1) * width]
    pl.semaphore_wait(barrier, 2)
    for c in range(chunks):
        hop_one(c).start()

    lane = lax.broadcasted_iota(jnp.int32, (1, rows), 1)
    key_at = lax.broadcasted_iota(jnp.int32, bias_own.shape, 0)
    for base, ref in ((0, bias_own), (2 * picks, bias_two)):
        place = lane
        for a in range(picks):
            place = jnp.where(lane // BLK == a, (lane - a * BLK) + sel[base + a] * BLK, place)
        seen = (key_at <= place) if base == 0 else (key_at > place)
        ref[...] = jnp.where(seen, 0.0, LOW)

    def head_of(c, h):
        return pl.ds(pl.multiple_of(c * width + h * HEAD, HEAD), HEAD)

    def spread(row):
        return jnp.broadcast_to(row, (8 // per_chunk, rows))

    def lse_rows(h):
        return slice(h * (8 // per_chunk), (h + 1) * (8 // per_chunk))

    def own_part(c, carry):
        hop_one(c).wait_recv()
        hop_two(c).start()
        for h in range(per_chunk):
            cols = head_of(c, h)
            value_t = v_in[:, cols].T
            v_t[cols, :] = value_t
            part, lse = window_part(
                q_own[c, :, h * HEAD : (h + 1) * HEAD], k_in[:, cols], value_t, bias_own[...]
            )
            o_own[c, h * HEAD : (h + 1) * HEAD, :] = part
            l_own[c, lse_rows(h), :] = spread(lse)
        return carry

    lax.fori_loop(0, chunks, own_part, 0)

    def step(t, carry):
        @pl.when(t < chunks)
        def _():
            c = t
            hop_two(c).wait_recv()
            for h in range(per_chunk):
                cols = head_of(c, h)
                part, lse = window_part(
                    q_two[c, :, h * HEAD : (h + 1) * HEAD], k_in[:, cols], v_t[cols, :], bias_two[...]
                )
                o_snd2[c, h * HEAD : (h + 1) * HEAD, :] = part.astype(BF16)
                l_snd2[c, lse_rows(h), :] = spread(lse)
            for one in back_two(c):
                one.start()

        @pl.when((t >= 1) & (t <= chunks))
        def _():
            c = t - 1
            parts = []
            for h in range(per_chunk):
                cols = head_of(c, h)
                parts.append(
                    window_part(q_one[c, :, h * HEAD : (h + 1) * HEAD], k_in[:, cols], v_t[cols, :], None)
                )
            for one in back_two(c):
                one.wait_recv()
            for h in range(per_chunk):
                part, lse = parts[h]
                lse_in = jnp.where(shard == 0, LOW, l_got2[c, h * (8 // per_chunk) : h * (8 // per_chunk) + 1, :])
                part, lse = merged(part, lse, o_got2[c, h * HEAD : (h + 1) * HEAD, :].astype(F32), lse_in)
                o_snd1[c, h * HEAD : (h + 1) * HEAD, :] = part.astype(BF16)
                l_snd1[c, lse_rows(h), :] = spread(lse)
            for one in back_one(c):
                one.start()

        @pl.when(t >= 2)
        def _():
            c = t - 2
            for one in back_one(c):
                one.wait_recv()
            for h in range(per_chunk):
                first = h * (8 // per_chunk)
                lse_in = jnp.where(shard == 0, LOW, l_got1[c, first : first + 1, :])
                part, lse = merged(
                    o_own[c, h * HEAD : (h + 1) * HEAD, :], l_own[c, first : first + 1, :],
                    o_got1[c, h * HEAD : (h + 1) * HEAD, :].astype(F32), lse_in,
                )
                final = part.T.astype(BF16)
                for a in range(picks):
                    out[a, :, head_of(c, h)] = final[a * BLK : (a + 1) * BLK, :]

        return carry

    lax.fori_loop(0, chunks + 2, step, 0)

    def drain(c, carry):
        hop_one(c).wait_send()
        hop_two(c).wait_send()
        for one in back_two(c) + back_one(c):
            one.wait_send()
        return carry

    lax.fori_loop(0, chunks, drain, 0)


def window(sel, query, key, value, part, parts, per_chunk, ident):
    blocks, _, full = query.shape
    tok = key.shape[0]
    cols = full // parts
    chunks = cols // HEAD // per_chunk
    width = per_chunk * HEAD
    rows = sel.shape[0] // 3 * BLK
    out_t = (chunks, width, rows)
    lse_t = (chunks, 8, rows)
    return pl.pallas_call(
        functools.partial(window_kernel, chunks, per_chunk),
        out_shape=jax.ShapeDtypeStruct((rows // BLK, BLK, cols), BF16),
        grid=(1,),
        in_specs=[
            pl.BlockSpec(memory_space=pltpu.SMEM),
            pl.BlockSpec((blocks, BLK, cols), lambda g: (0, 0, part)),
            pl.BlockSpec((tok, cols), lambda g: (0, part)),
            pl.BlockSpec((tok, cols), lambda g: (0, part)),
        ],
        out_specs=pl.BlockSpec((rows // BLK, BLK, cols), lambda g: (0, 0, 0)),
        scratch_shapes=[
            pltpu.VMEM((chunks, rows, width), BF16),
            pltpu.VMEM((chunks, rows, width), BF16),
            pltpu.VMEM((chunks, rows, width), BF16),
            pltpu.VMEM((cols, tok), BF16),
            pltpu.VMEM(out_t, F32),
            pltpu.VMEM(lse_t, F32),
            pltpu.VMEM(out_t, BF16),
            pltpu.VMEM(lse_t, F32),
            pltpu.VMEM(out_t, BF16),
            pltpu.VMEM(lse_t, F32),
            pltpu.VMEM(out_t, BF16),
            pltpu.VMEM(lse_t, F32),
            pltpu.VMEM(out_t, BF16),
            pltpu.VMEM(lse_t, F32),
            pltpu.VMEM((tok, rows), F32),
            pltpu.VMEM((tok, rows), F32),
            pltpu.SemaphoreType.DMA((6, chunks)),
            pltpu.SemaphoreType.DMA((6, chunks)),
        ],
        compiler_params=pltpu.CompilerParams(
            collective_id=ident, has_side_effects=True, vmem_limit_bytes=VMEM_LIMIT
        ),
        cost_estimate=pl.CostEstimate(
            flops=12 * rows * tok * cols, bytes_accessed=16 * 1024 * 1024 * cols // full, transcendentals=0
        ),
        name=f"window_{ident}",
    )(sel, query, key, value)


def project_kernel(index, a0, a1, b0, b1, weights, normed, projected):
    half = a0.shape[2]
    eps_width = 2 * half
    pieces = []
    for low, high in ((a0, b0), (a1, b1)):
        x0 = low[0].astype(F32)
        x1 = high[0].astype(F32)
        mean = (
            jnp.sum(x0 * x0, axis=1, keepdims=True) + jnp.sum(x1 * x1, axis=1, keepdims=True)
        ) * (1.0 / eps_width)
        inv = lax.rsqrt(mean + 1e-06)
        pieces.append(((x0 * inv).astype(BF16), (x1 * inv).astype(BF16)))
    n0 = jnp.concatenate([pieces[0][0], pieces[1][0]], axis=0)
    n1 = jnp.concatenate([pieces[0][1], pieces[1][1]], axis=0)
    normed[:, :half] = n0
    normed[:, half:] = n1
    projected[...] = (
        jnp.dot(n0, weights[:half, :], preferred_element_type=F32)
        + jnp.dot(n1, weights[half:, :], preferred_element_type=F32)
    ).astype(BF16)


def project(index, low, high, weights):
    kept = index.shape[0]
    half = low.shape[2]
    local = weights.shape[1]
    block = (1, BLK, half)
    return pl.pallas_call(
        project_kernel,
        out_shape=(
            jax.ShapeDtypeStruct((kept * BLK, 2 * half), BF16),
            jax.ShapeDtypeStruct((kept * BLK, local), BF16),
        ),
        grid_spec=pltpu.PrefetchScalarGridSpec(
            num_scalar_prefetch=1,
            grid=(kept // 2,),
            in_specs=[
                pl.BlockSpec(block, lambda g, idx: (idx[2 * g], 0, 0)),
                pl.BlockSpec(block, lambda g, idx: (idx[2 * g + 1], 0, 0)),
                pl.BlockSpec(block, lambda g, idx: (idx[2 * g], 0, 0)),
                pl.BlockSpec(block, lambda g, idx: (idx[2 * g + 1], 0, 0)),
                pl.BlockSpec((2 * half, local), lambda g, idx: (0, 0)),
            ],
            out_specs=[
                pl.BlockSpec((2 * BLK, 2 * half), lambda g, idx: (g, 0)),
                pl.BlockSpec((2 * BLK, local), lambda g, idx: (g, 0)),
            ],
        ),
        compiler_params=pltpu.CompilerParams(vmem_limit_bytes=VMEM_LIMIT),
        name="project",
    )(index, low, low, high, high, weights)


QB = 256
KB = 512


def causal_kernel(dest, qkv, cot, out, d_all, d_all_t, v_t, k_t, do_own, do_t, p_buf, dk_acc, dv_acc, dq_t):
    kept = dest.shape[0]
    total_rows = qkv.shape[0]
    for j in range(kept):
        do_own[j * BLK : (j + 1) * BLK, :] = cot[pl.ds(pl.multiple_of(dest[j] * BLK, BLK), BLK), :]

    def prepare(c, carry):
        at = pl.ds(pl.multiple_of(c * QB, QB), QB)
        k_t[:, at] = qkv[at, HEAD : 2 * HEAD].T
        v_t[:, at] = qkv[at, 2 * HEAD : 3 * HEAD].T
        do_t[:, at] = do_own[at, :].T
        return carry

    lax.fori_loop(0, total_rows // QB, prepare, 0)
    dk_acc[...] = jnp.zeros_like(dk_acc)
    dv_acc[...] = jnp.zeros_like(dv_acc)
    key_at = lax.broadcasted_iota(jnp.int32, (KB, QB), 0)
    row_at = lax.broadcasted_iota(jnp.int32, (KB, QB), 1)

    for i in range(total_rows // QB):
        rows = slice(i * QB, (i + 1) * QB)
        chunks = (i + 1) * QB // KB + (1 if (i + 1) * QB % KB else 0)
        q_i = qkv[rows, :HEAD]
        do_i = do_own[rows, :]

        def scores_of(c, masked):
            keys = pl.ds(pl.multiple_of(c * KB, KB), KB)
            scores = lax.dot_general(qkv[keys, HEAD : 2 * HEAD], q_i, NT, preferred_element_type=F32)
            if masked:
                scores = jnp.where(key_at <= row_at + (i * QB - (chunks - 1) * KB), scores, LOW)
            p_buf[keys, :] = scores
            return jnp.max(scores, axis=0, keepdims=True)

        top = scores_of(chunks - 1, True)
        if chunks > 1:
            top = lax.fori_loop(0, chunks - 1, lambda c, m: jnp.maximum(m, scores_of(c, False)), top)

        def weigh(c, carry):
            total, acc = carry
            keys = pl.ds(pl.multiple_of(c * KB, KB), KB)
            weight = jnp.exp2((p_buf[keys, :] - top) * SCALE2)
            p_buf[keys, :] = weight
            total = total + jnp.sum(weight, axis=0, keepdims=True)
            acc = acc + jnp.dot(v_t[:, keys], weight.astype(BF16), preferred_element_type=F32)
            return total, acc

        total, acc = lax.fori_loop(
            0, chunks, weigh, (jnp.zeros((1, QB), F32), jnp.zeros((HEAD, QB), F32))
        )
        inv = 1.0 / total
        o_t = acc * inv
        delta = jnp.sum(o_t * do_t[:, rows].astype(F32), axis=0, keepdims=True)
        o_i = o_t.T.astype(BF16)
        for b in range(QB // BLK):
            slot = dest[i * (QB // BLK) + b]
            out[pl.ds(pl.multiple_of(slot * BLK, BLK), BLK), :] = o_i[b * BLK : (b + 1) * BLK, :]

        def back(c, acc):
            keys = pl.ds(pl.multiple_of(c * KB, KB), KB)
            soft = p_buf[keys, :] * inv
            dv_acc[keys, :] += jnp.dot(soft.astype(BF16), do_i, preferred_element_type=F32)
            d_probs = lax.dot_general(qkv[keys, 2 * HEAD :], do_i, NT, preferred_element_type=F32)
            d_scores = (soft * (d_probs - delta) * SCALE).astype(BF16)
            dk_acc[keys, :] += jnp.dot(d_scores, q_i, preferred_element_type=F32)
            return acc + jnp.dot(k_t[:, keys], d_scores, preferred_element_type=F32)

        dq_t[:, rows] = lax.fori_loop(0, chunks, back, jnp.zeros((HEAD, QB), F32))

    def finish(c, carry):
        at = pl.ds(pl.multiple_of(c * QB, QB), QB)
        d_q = dq_t[:, at]
        d_all_t[:HEAD, at] = d_q.astype(BF16)
        d_all[at, :HEAD] = d_q.T.astype(BF16)
        for which, acc in ((1, dk_acc), (2, dv_acc)):
            value = acc[at, :]
            d_all[at, which * HEAD : (which + 1) * HEAD] = value.astype(BF16)
            d_all_t[which * HEAD : (which + 1) * HEAD, at] = value.T.astype(BF16)
        return carry

    lax.fori_loop(0, total_rows // QB, finish, 0)


def causal(dest, qkv, cot):
    total_rows, local = qkv.shape
    vmem = pl.BlockSpec(memory_space=pltpu.VMEM)
    return pl.pallas_call(
        causal_kernel,
        out_shape=(
            jax.ShapeDtypeStruct((total_rows, HEAD), BF16),
            jax.ShapeDtypeStruct((total_rows, local), BF16),
            jax.ShapeDtypeStruct((local, total_rows), BF16),
        ),
        in_specs=[pl.BlockSpec(memory_space=pltpu.SMEM), vmem, vmem],
        out_specs=[vmem, vmem, vmem],
        scratch_shapes=[
            pltpu.VMEM((HEAD, total_rows), BF16),
            pltpu.VMEM((HEAD, total_rows), BF16),
            pltpu.VMEM((total_rows, HEAD), BF16),
            pltpu.VMEM((HEAD, total_rows), BF16),
            pltpu.VMEM((total_rows, QB), F32),
            pltpu.VMEM((total_rows, HEAD), F32),
            pltpu.VMEM((total_rows, HEAD), F32),
            pltpu.VMEM((HEAD, total_rows), F32),
        ],
        compiler_params=pltpu.CompilerParams(vmem_limit_bytes=VMEM_LIMIT),
        name="causal",
    )(dest, qkv, cot)


def term_kernel(dest, d_all, weights, out):
    value = lax.dot_general(d_all[...], weights[...], NT, preferred_element_type=F32).astype(BF16)
    for j in range(value.shape[0] // BLK):
        out[pl.ds(pl.multiple_of(dest[j] * BLK, BLK), BLK), :] = value[j * BLK : (j + 1) * BLK, :]


def term(dest, d_all, weights, step=256):
    total_rows, local = d_all.shape
    full = weights.shape[0]
    return pl.pallas_call(
        term_kernel,
        out_shape=jax.ShapeDtypeStruct((total_rows, full), BF16),
        grid=(full // step,),
        in_specs=[
            pl.BlockSpec(memory_space=pltpu.SMEM),
            pl.BlockSpec((total_rows, local), lambda g: (0, 0)),
            pl.BlockSpec((step, local), lambda g: (g, 0)),
        ],
        out_specs=pl.BlockSpec((total_rows, step), lambda g: (0, g)),
        compiler_params=pltpu.CompilerParams(vmem_limit_bytes=VMEM_LIMIT),
        name="term",
    )(dest, d_all, weights)


def weight_grad_kernel(d_t, normed, out):
    value = jnp.dot(d_t[...], normed[...], preferred_element_type=F32)
    for at in range(3):
        out[at] = value[at * HEAD : (at + 1) * HEAD, :].T.astype(BF16)


def weight_grad(d_t, normed, step=256):
    local, total_rows = d_t.shape
    full = normed.shape[1]
    return pl.pallas_call(
        weight_grad_kernel,
        out_shape=jax.ShapeDtypeStruct((3, full, HEAD), BF16),
        grid=(full // step,),
        in_specs=[
            pl.BlockSpec((local, total_rows), lambda g: (0, 0)),
            pl.BlockSpec((total_rows, step), lambda g: (0, g)),
        ],
        out_specs=pl.BlockSpec((3, step, HEAD), lambda g: (0, g, 0)),
        compiler_params=pltpu.CompilerParams(vmem_limit_bytes=VMEM_LIMIT),
        name="weight_grad",
    )(d_t, normed)


def assemble_kernel(table, low, high, rest, out):
    first = table[3 * pl.program_id(0)] == 1

    @pl.when(first)
    def _():
        half = low.shape[2]
        out[:, :half] = low[0]
        out[:, half:] = high[0]

    @pl.when(jnp.logical_not(first))
    def _():
        out[...] = rest[0]


def assemble(table, low, high, rest):
    blocks = 2 * low.shape[0]
    half = low.shape[2]
    return pl.pallas_call(
        assemble_kernel,
        out_shape=jax.ShapeDtypeStruct((blocks * BLK, 2 * half), BF16),
        grid_spec=pltpu.PrefetchScalarGridSpec(
            num_scalar_prefetch=1,
            grid=(blocks,),
            in_specs=[
                pl.BlockSpec((1, BLK, half), lambda g, t: (t[3 * g + 1], 0, 0)),
                pl.BlockSpec((1, BLK, half), lambda g, t: (t[3 * g + 1], 0, 0)),
                pl.BlockSpec((1, BLK, 2 * half), lambda g, t: (t[3 * g + 2], 0, 0)),
            ],
            out_specs=pl.BlockSpec((BLK, 2 * half), lambda g, t: (g, 0)),
        ),
        name="assemble",
    )(table, low, high, rest)


def shards(query_input, key_input, value_input, keep_blocks, dest_slots, proj_weights, cotangent):
    tok, full = query_input.shape[1:]
    per_shard = tok // BLK
    shard = lax.axis_index(SEQ)
    count = lax.axis_size(SEQ)
    half_blocks = per_shard // 2
    query = query_input.reshape(per_shard, BLK, full)
    key = key_input[0]
    value = value_input[0]
    keep = keep_blocks[0]
    dest = dest_slots[0]

    kept = jnp.any(
        keep[None, None, :] == jnp.arange(count * per_shard).reshape(count, per_shard)[:, :, None], axis=2
    )
    order_key = jnp.where(kept, 0, per_shard) + jnp.arange(per_shard)[None, :]
    rank = jnp.sum(order_key[:, None, :] < order_key[:, :, None], axis=2).astype(jnp.int32)
    order = jnp.sum(
        jnp.where(
            rank[:, None, :] == jnp.arange(per_shard)[None, :, None], jnp.arange(per_shard)[None, None, :], 0
        ),
        axis=2,
    ).astype(jnp.int32)
    wrapped = jnp.concatenate([order, order[:2]], axis=0)
    near = lax.dynamic_slice_in_dim(wrapped, shard, 3, 0)
    sel_first = near[:, :half_blocks].reshape(-1)
    sel_rest = near[:, half_blocks:].reshape(-1)
    own_rank = lax.dynamic_slice_in_dim(rank, shard, 1, 0)[0]
    in_first = (own_rank < half_blocks).astype(jnp.int32)
    at = own_rank % half_blocks
    table = jnp.stack([in_first, at * in_first, at * (1 - in_first)], axis=1).reshape(-1)
    keep_shard = keep // per_shard
    before = jnp.sum((keep_shard[None, :] == keep_shard[:, None]) & (keep[None, :] < keep[:, None]), axis=1)
    packed = (keep_shard * half_blocks + before).astype(jnp.int32)
    weights = jnp.concatenate([proj_weights[0], proj_weights[1], proj_weights[2]], axis=1)

    low = window(sel_first, query, key, value, 0, 2, 2, 0)
    low_all = lax.all_gather(low, SEQ, axis=0, tiled=True)
    high = window(sel_first, query, key, value, 1, 2, 2, 1)
    high_all = lax.all_gather(high, SEQ, axis=0, tiled=True)

    normed, qkv = project(packed, low_all, high_all, weights)
    causal_out, d_all, d_all_t = causal(dest, qkv, cotangent[0])
    terms = term(dest, d_all, weights)
    row_grad = lax.psum_scatter(terms, SEQ, scatter_dimension=0, tiled=True)
    grads = weight_grad(d_all_t, normed)
    grads = lax.psum(grads, "dp").astype(F32)
    sel_late, terms = lax.optimization_barrier((sel_rest, d_all))
    rest = window(sel_late, query, key, value, 0, 1, 2, 2)
    window_out = assemble(table, low, high, rest)
    return (window_out[None], causal_out[None], grads, row_grad[None])


def solution(mesh):
    return jax.shard_map(
        shards,
        mesh=mesh,
        in_specs=(
            P("dp", "seq", None),
            P("dp", "seq", None),
            P("dp", "seq", None),
            P("dp", None),
            P("dp", None),
            P(None, None, "seq"),
            P("dp", None, "seq"),
        ),
        out_specs=(
            P("dp", "seq", None),
            P("dp", None, "seq"),
            P(None, None, "seq"),
            P("dp", "seq", None),
        ),
        check_vma=False,
    )
```

```python
import functools

import jax
import jax.numpy as jnp
from jax import lax
from jax.experimental import pallas as pl
from jax.experimental.pallas import tpu as pltpu
from jax.sharding import PartitionSpec as P

HEAD = 128
BLK = 128
SEQ = "seq"
MESH = pl.DeviceIdType.MESH
SCALE = HEAD ** (-0.5)
LOG2E = 1.4426950408889634
SCALE2 = SCALE * LOG2E
LOW = -1e30
NT = (((1,), (1,)), ((), ()))
BF16 = jnp.bfloat16
F32 = jnp.float32
VMEM_LIMIT = 56 * 1024 * 1024


def window_part(query, key, value_t, bias):
    scores = lax.dot_general(key, query, NT, preferred_element_type=F32)
    if bias is not None:
        scores = scores + bias
    top = jnp.max(scores, axis=0, keepdims=True)
    weight = jnp.exp2((scores - top) * SCALE2)
    total = jnp.sum(weight, axis=0, keepdims=True)
    out = jnp.dot(value_t, weight.astype(BF16), preferred_element_type=F32)
    return out / total, top * SCALE2 + jnp.log2(total)


def merged(out_a, lse_a, out_b, lse_b):
    top = jnp.maximum(lse_a, lse_b)
    weight_a = jnp.exp2(lse_a - top)
    weight_b = jnp.exp2(lse_b - top)
    total = weight_a + weight_b
    return out_a * (weight_a / total) + out_b * (weight_b / total), top + jnp.log2(total)


def window_kernel(
    chunks, per_chunk, sel, q_in, k_in, v_in, out,
    q_own, q_one, q_two, v_t, o_own, l_own, o_snd2, l_snd2, o_got2, l_got2, o_snd1, l_snd1, o_got1, l_got1,
    bias_own, bias_two, send_sem, recv_sem,
):
    shard = lax.axis_index(SEQ)
    count = lax.axis_size(SEQ)
    right = lax.rem(shard + 1, count)
    left = lax.rem(shard + count - 1, count)
    right_two = lax.rem(shard + 2, count)
    left_two = lax.rem(shard + count - 2, count)
    width = per_chunk * HEAD
    rows = q_own.shape[1]
    picks = rows // BLK

    def copy(which, c, src, dst, target):
        return pltpu.make_async_remote_copy(
            src_ref=src.at[c], dst_ref=dst.at[c],
            send_sem=send_sem.at[which, c], recv_sem=recv_sem.at[which, c],
            device_id={SEQ: target}, device_id_type=MESH,
        )

    def hop_one(c):
        return copy(0, c, q_own, q_one, left)

    def hop_two(c):
        return copy(1, c, q_own, q_two, left_two)

    def back_two(c):
        return (copy(2, c, o_snd2, o_got2, right), copy(3, c, l_snd2, l_got2, right))

    def back_one(c):
        return (copy(4, c, o_snd1, o_got1, right), copy(5, c, l_snd1, l_got1, right))

    barrier = pltpu.get_barrier_semaphore()
    for neighbour in (left, right, left_two, right_two):
        pl.semaphore_signal(barrier, inc=1, device_id={SEQ: neighbour}, device_id_type=MESH)

    for a in range(picks):
        block = q_in[sel[a]]
        for c in range(chunks):
            q_own[c, a * BLK : (a + 1) * BLK, :] = block[:, c * width : (c + 1) * width]
    pl.semaphore_wait(barrier, 4)

    def send(c, carry):
        hop_two(c).start()
        hop_one(c).start()
        return carry

    lax.fori_loop(0, chunks, send, 0)

    lane = lax.broadcasted_iota(jnp.int32, (1, rows), 1)
    key_at = lax.broadcasted_iota(jnp.int32, bias_own.shape, 0)
    for base, ref in ((0, bias_own), (2 * picks, bias_two)):
        place = lane
        for a in range(picks):
            place = jnp.where(lane // BLK == a, (lane - a * BLK) + sel[base + a] * BLK, place)
        seen = (key_at <= place) if base == 0 else (key_at > place)
        ref[...] = jnp.where(seen, 0.0, LOW)

    def head_of(c, h):
        return pl.ds(pl.multiple_of(c * width + h * HEAD, HEAD), HEAD)

    def spread(row):
        return jnp.broadcast_to(row, (8 // per_chunk, rows))

    def lse_rows(h):
        return slice(h * (8 // per_chunk), (h + 1) * (8 // per_chunk))

    def own_part(c, carry):
        for h in range(per_chunk):
            cols = head_of(c, h)
            value_t = v_in[:, cols].T
            v_t[cols, :] = value_t
            part, lse = window_part(
                q_own[c, :, h * HEAD : (h + 1) * HEAD], k_in[:, cols], value_t, bias_own[...]
            )
            o_own[c, h * HEAD : (h + 1) * HEAD, :] = part
            l_own[c, lse_rows(h), :] = spread(lse)
        return carry

    lax.fori_loop(0, chunks, own_part, 0)

    def step(t, carry):
        @pl.when(t < chunks)
        def _():
            c = t
            hop_two(c).wait_recv()
            for h in range(per_chunk):
                cols = head_of(c, h)
                part, lse = window_part(
                    q_two[c, :, h * HEAD : (h + 1) * HEAD], k_in[:, cols], v_t[cols, :], bias_two[...]
                )
                o_snd2[c, h * HEAD : (h + 1) * HEAD, :] = part.astype(BF16)
                l_snd2[c, lse_rows(h), :] = spread(lse)
            for one in back_two(c):
                one.start()

        @pl.when((t >= 1) & (t <= chunks))
        def _():
            c = t - 1
            hop_one(c).wait_recv()
            parts = []
            for h in range(per_chunk):
                cols = head_of(c, h)
                parts.append(
                    window_part(q_one[c, :, h * HEAD : (h + 1) * HEAD], k_in[:, cols], v_t[cols, :], None)
                )
            for one in back_two(c):
                one.wait_recv()
            for h in range(per_chunk):
                part, lse = parts[h]
                lse_in = jnp.where(shard == 0, LOW, l_got2[c, h * (8 // per_chunk) : h * (8 // per_chunk) + 1, :])
                part, lse = merged(part, lse, o_got2[c, h * HEAD : (h + 1) * HEAD, :].astype(F32), lse_in)
                o_snd1[c, h * HEAD : (h + 1) * HEAD, :] = part.astype(BF16)
                l_snd1[c, lse_rows(h), :] = spread(lse)
            for one in back_one(c):
                one.start()

        @pl.when(t >= 2)
        def _():
            c = t - 2
            for one in back_one(c):
                one.wait_recv()
            for h in range(per_chunk):
                first = h * (8 // per_chunk)
                lse_in = jnp.where(shard == 0, LOW, l_got1[c, first : first + 1, :])
                part, lse = merged(
                    o_own[c, h * HEAD : (h + 1) * HEAD, :], l_own[c, first : first + 1, :],
                    o_got1[c, h * HEAD : (h + 1) * HEAD, :].astype(F32), lse_in,
                )
                final = part.T.astype(BF16)
                for a in range(picks):
                    out[a * BLK : (a + 1) * BLK, head_of(c, h)] = final[a * BLK : (a + 1) * BLK, :]

        return carry

    lax.fori_loop(0, chunks + 2, step, 0)

    def drain(c, carry):
        hop_one(c).wait_send()
        hop_two(c).wait_send()
        for one in back_two(c) + back_one(c):
            one.wait_send()
        return carry

    lax.fori_loop(0, chunks, drain, 0)


def window(sel, query, key, value, part, parts, per_chunk, ident):
    blocks, _, full = query.shape
    tok = key.shape[0]
    cols = full // parts
    chunks = cols // HEAD // per_chunk
    width = per_chunk * HEAD
    rows = sel.shape[0] // 3 * BLK
    out_t = (chunks, width, rows)
    lse_t = (chunks, 8, rows)
    return pl.pallas_call(
        functools.partial(window_kernel, chunks, per_chunk),
        out_shape=jax.ShapeDtypeStruct((rows, cols), BF16),
        grid=(1,),
        in_specs=[
            pl.BlockSpec(memory_space=pltpu.SMEM),
            pl.BlockSpec((blocks, BLK, cols), lambda g: (0, 0, part)),
            pl.BlockSpec((tok, cols), lambda g: (0, part)),
            pl.BlockSpec((tok, cols), lambda g: (0, part)),
        ],
        out_specs=pl.BlockSpec((rows, cols), lambda g: (0, 0)),
        scratch_shapes=[
            pltpu.VMEM((chunks, rows, width), BF16),
            pltpu.VMEM((chunks, rows, width), BF16),
            pltpu.VMEM((chunks, rows, width), BF16),
            pltpu.VMEM((cols, tok), BF16),
            pltpu.VMEM(out_t, F32),
            pltpu.VMEM(lse_t, F32),
            pltpu.VMEM(out_t, BF16),
            pltpu.VMEM(lse_t, F32),
            pltpu.VMEM(out_t, BF16),
            pltpu.VMEM(lse_t, F32),
            pltpu.VMEM(out_t, BF16),
            pltpu.VMEM(lse_t, F32),
            pltpu.VMEM(out_t, BF16),
            pltpu.VMEM(lse_t, F32),
            pltpu.VMEM((tok, rows), F32),
            pltpu.VMEM((tok, rows), F32),
            pltpu.SemaphoreType.DMA((6, chunks)),
            pltpu.SemaphoreType.DMA((6, chunks)),
        ],
        compiler_params=pltpu.CompilerParams(
            collective_id=ident, has_side_effects=True, vmem_limit_bytes=VMEM_LIMIT
        ),
        cost_estimate=pl.CostEstimate(
            flops=12 * rows * tok * cols, bytes_accessed=16 * 1024 * 1024 * cols // full, transcendentals=0
        ),
        name=f"window_{ident}",
    )(sel, query, key, value)


def project_kernel(index, first, second, weights, normed, projected):
    for at, block in enumerate((first, second)):
        x = block[...].astype(F32)
        mean = jnp.sum(x * x, axis=1, keepdims=True) * (1.0 / x.shape[1])
        normed[at * BLK : (at + 1) * BLK, :] = (x * lax.rsqrt(mean + 1e-06)).astype(BF16)
    projected[...] = jnp.dot(normed[...], weights[...], preferred_element_type=F32).astype(BF16)


def project(index, rows, weights):
    kept = index.shape[0]
    full, local = weights.shape
    return pl.pallas_call(
        project_kernel,
        out_shape=(
            jax.ShapeDtypeStruct((kept * BLK, full), BF16),
            jax.ShapeDtypeStruct((kept * BLK, local), BF16),
        ),
        grid_spec=pltpu.PrefetchScalarGridSpec(
            num_scalar_prefetch=1,
            grid=(kept // 2,),
            in_specs=[
                pl.BlockSpec((BLK, full), lambda g, idx: (idx[2 * g], 0)),
                pl.BlockSpec((BLK, full), lambda g, idx: (idx[2 * g + 1], 0)),
                pl.BlockSpec((full, local), lambda g, idx: (0, 0)),
            ],
            out_specs=[
                pl.BlockSpec((2 * BLK, full), lambda g, idx: (g, 0)),
                pl.BlockSpec((2 * BLK, local), lambda g, idx: (g, 0)),
            ],
        ),
        compiler_params=pltpu.CompilerParams(vmem_limit_bytes=VMEM_LIMIT),
        name="project",
    )(index, rows, rows, weights)


QB = 256
KB = 512


def causal_kernel(dest, qkv, cot, out, d_all, d_all_t, v_t, k_t, do_own, do_t, p_buf, dk_acc, dv_acc, dq_t):
    kept = dest.shape[0]
    total_rows = qkv.shape[0]
    for j in range(kept):
        do_own[j * BLK : (j + 1) * BLK, :] = cot[pl.ds(pl.multiple_of(dest[j] * BLK, BLK), BLK), :]

    def prepare(c, carry):
        at = pl.ds(pl.multiple_of(c * QB, QB), QB)
        k_t[:, at] = qkv[at, HEAD : 2 * HEAD].T
        v_t[:, at] = qkv[at, 2 * HEAD : 3 * HEAD].T
        do_t[:, at] = do_own[at, :].T
        return carry

    lax.fori_loop(0, total_rows // QB, prepare, 0)
    dk_acc[...] = jnp.zeros_like(dk_acc)
    dv_acc[...] = jnp.zeros_like(dv_acc)
    key_at = lax.broadcasted_iota(jnp.int32, (KB, QB), 0)
    row_at = lax.broadcasted_iota(jnp.int32, (KB, QB), 1)

    for i in range(total_rows // QB):
        rows = slice(i * QB, (i + 1) * QB)
        chunks = (i + 1) * QB // KB + (1 if (i + 1) * QB % KB else 0)
        q_i = qkv[rows, :HEAD]
        do_i = do_own[rows, :]

        def scores_of(c, masked):
            keys = pl.ds(pl.multiple_of(c * KB, KB), KB)
            scores = lax.dot_general(qkv[keys, HEAD : 2 * HEAD], q_i, NT, preferred_element_type=F32)
            if masked:
                scores = jnp.where(key_at <= row_at + (i * QB - (chunks - 1) * KB), scores, LOW)
            p_buf[keys, :] = scores
            return jnp.max(scores, axis=0, keepdims=True)

        top = scores_of(chunks - 1, True)
        if chunks > 1:
            top = lax.fori_loop(0, chunks - 1, lambda c, m: jnp.maximum(m, scores_of(c, False)), top)

        def weigh(c, carry):
            total, acc = carry
            keys = pl.ds(pl.multiple_of(c * KB, KB), KB)
            weight = jnp.exp2((p_buf[keys, :] - top) * SCALE2)
            p_buf[keys, :] = weight
            total = total + jnp.sum(weight, axis=0, keepdims=True)
            acc = acc + jnp.dot(v_t[:, keys], weight.astype(BF16), preferred_element_type=F32)
            return total, acc

        total, acc = lax.fori_loop(
            0, chunks, weigh, (jnp.zeros((1, QB), F32), jnp.zeros((HEAD, QB), F32))
        )
        inv = 1.0 / total
        o_t = acc * inv
        delta = jnp.sum(o_t * do_t[:, rows].astype(F32), axis=0, keepdims=True)
        o_i = o_t.T.astype(BF16)
        for b in range(QB // BLK):
            slot = dest[i * (QB // BLK) + b]
            out[pl.ds(pl.multiple_of(slot * BLK, BLK), BLK), :] = o_i[b * BLK : (b + 1) * BLK, :]

        def back(c, acc):
            keys = pl.ds(pl.multiple_of(c * KB, KB), KB)
            soft = p_buf[keys, :] * inv
            dv_acc[keys, :] += jnp.dot(soft.astype(BF16), do_i, preferred_element_type=F32)
            d_probs = lax.dot_general(qkv[keys, 2 * HEAD :], do_i, NT, preferred_element_type=F32)
            d_scores = (soft * (d_probs - delta) * SCALE).astype(BF16)
            dk_acc[keys, :] += jnp.dot(d_scores, q_i, preferred_element_type=F32)
            return acc + jnp.dot(k_t[:, keys], d_scores, preferred_element_type=F32)

        dq_t[:, rows] = lax.fori_loop(0, chunks, back, jnp.zeros((HEAD, QB), F32))

    def finish(c, carry):
        at = pl.ds(pl.multiple_of(c * QB, QB), QB)
        d_q = dq_t[:, at]
        d_all_t[:HEAD, at] = d_q.astype(BF16)
        d_all[at, :HEAD] = d_q.T.astype(BF16)
        for which, acc in ((1, dk_acc), (2, dv_acc)):
            value = acc[at, :]
            d_all[at, which * HEAD : (which + 1) * HEAD] = value.astype(BF16)
            d_all_t[which * HEAD : (which + 1) * HEAD, at] = value.T.astype(BF16)
        return carry

    lax.fori_loop(0, total_rows // QB, finish, 0)


def causal(dest, qkv, cot):
    total_rows, local = qkv.shape
    vmem = pl.BlockSpec(memory_space=pltpu.VMEM)
    return pl.pallas_call(
        causal_kernel,
        out_shape=(
            jax.ShapeDtypeStruct((total_rows, HEAD), BF16),
            jax.ShapeDtypeStruct((total_rows, local), BF16),
            jax.ShapeDtypeStruct((local, total_rows), BF16),
        ),
        in_specs=[pl.BlockSpec(memory_space=pltpu.SMEM), vmem, vmem],
        out_specs=[vmem, vmem, vmem],
        scratch_shapes=[
            pltpu.VMEM((HEAD, total_rows), BF16),
            pltpu.VMEM((HEAD, total_rows), BF16),
            pltpu.VMEM((total_rows, HEAD), BF16),
            pltpu.VMEM((HEAD, total_rows), BF16),
            pltpu.VMEM((total_rows, QB), F32),
            pltpu.VMEM((total_rows, HEAD), F32),
            pltpu.VMEM((total_rows, HEAD), F32),
            pltpu.VMEM((HEAD, total_rows), F32),
        ],
        compiler_params=pltpu.CompilerParams(vmem_limit_bytes=VMEM_LIMIT),
        name="causal",
    )(dest, qkv, cot)


SIDE = 4


def scatter_kernel(
    slot_at, d_all, weights, out, terms, got1, snd2, got2, sums, last1, lasts2, last2,
    send1, recv1, send2, recv2, send3, recv3, send4, recv4,
):
    shard = lax.axis_index(SEQ)
    row, col = shard // SIDE, lax.rem(shard, SIDE)
    wide = out.shape[1] // 2
    part = wide // 2
    place = ((row, col), (col, row))
    halves = (slice(0, part), slice(part, wide))

    def turn(at, by):
        return lax.rem(at + by + SIDE, SIDE)

    def slot(h, a, b):
        return a * SIDE + b if h == 0 else b * SIDE + a

    barrier = pltpu.get_barrier_semaphore()
    for by in (1, -1):
        for h in range(2):
            a, b = place[h]
            pl.semaphore_signal(
                barrier, inc=1, device_id={SEQ: slot(h, turn(a, by), b)}, device_id_type=MESH
            )

    def group(h, a):
        slots = [jnp.where(h == 0, a * SIDE + s, s * SIDE + a) for s in range(SIDE)]
        rows = jnp.concatenate([d_all[slot_at[one]] for one in slots], axis=0)
        cols = pl.ds(pl.multiple_of(h * wide, wide), wide)
        value = lax.dot_general(rows, weights[cols, :], NT, preferred_element_type=F32).astype(BF16)
        for s in range(SIDE):
            terms[h, a, s] = value[s * BLK : (s + 1) * BLK, :]

    def first_send(h, d, s):
        a, b = place[h]
        return pltpu.make_async_remote_copy(
            src_ref=terms.at[h, turn(a, 2), s, :, halves[d]], dst_ref=got1.at[h, d, s],
            send_sem=send1.at[h, d, s], recv_sem=recv1.at[h, d, s],
            device_id={SEQ: slot(h, turn(a, 1 - 2 * d), b)}, device_id_type=MESH,
        )

    def second_send(h, d, s):
        a, b = place[h]
        return pltpu.make_async_remote_copy(
            src_ref=snd2.at[h, d, s], dst_ref=got2.at[h, d, s],
            send_sem=send2.at[h, d, s], recv_sem=recv2.at[h, d, s],
            device_id={SEQ: slot(h, turn(a, 1 - 2 * d), b)}, device_id_type=MESH,
        )

    def third_send(h, d):
        a, b = place[h]
        return pltpu.make_async_remote_copy(
            src_ref=sums.at[h, turn(b, 2), :, halves[d]], dst_ref=last1.at[h, d],
            send_sem=send3.at[h, d], recv_sem=recv3.at[h, d],
            device_id={SEQ: slot(h, a, turn(b, 1 - 2 * d))}, device_id_type=MESH,
        )

    def fourth_send(h, d):
        a, b = place[h]
        return pltpu.make_async_remote_copy(
            src_ref=lasts2.at[h, d], dst_ref=last2.at[h, d],
            send_sem=send4.at[h, d], recv_sem=recv4.at[h, d],
            device_id={SEQ: slot(h, a, turn(b, 1 - 2 * d))}, device_id_type=MESH,
        )

    def group_far(h, carry):
        group(h, turn(jnp.where(h == 0, row, col), 2))
        return carry

    def group_rest(g, carry):
        h, which = lax.rem(g, 2), g // 2
        by = jnp.where(which == 0, 1, jnp.where(which == 1, SIDE - 1, 0))
        group(h, turn(jnp.where(h == 0, row, col), by))
        return carry

    lax.fori_loop(0, 2, group_far, 0)
    pl.semaphore_wait(barrier, 4)
    for k in (2, 1, 3, 0):
        for h in range(2):
            s = turn(place[h][1], k)
            for d in range(2):
                first_send(h, d, s).start()
    lax.fori_loop(0, 6, group_rest, 0)
    for k in (2, 1, 3, 0):
        for h in range(2):
            a, b = place[h]
            s = turn(b, k)
            for d in range(2):
                first_send(h, d, s).wait_recv()
                near = turn(a, 1 - 2 * d)
                other = halves[1 - d]
                snd2[h, d, s, :, other] = terms[h, near, s, :, other]
                snd2[h, d, s, :, halves[d]] = (
                    terms[h, near, s, :, halves[d]].astype(F32) + got1[h, d, s].astype(F32)
                ).astype(BF16)
                second_send(h, d, s).start()
    for k in (2, 1, 3, 0):
        for h in range(2):
            a, b = place[h]
            s = turn(b, k)
            for d in range(2):
                second_send(h, d, s).wait_recv()
            total = (
                terms[h, a, s].astype(F32) + got2[h, 0, s].astype(F32) + got2[h, 1, s].astype(F32)
            )
            if k != 0:
                sums[h, s] = total.astype(BF16)
            if k == 2:
                for d in range(2):
                    third_send(h, d).start()
            elif k != 0:
                d = 0 if k == 1 else 1
                third_send(h, d).wait_recv()
                other = halves[1 - d]
                lasts2[h, d, :, other] = sums[h, s, :, other]
                lasts2[h, d, :, halves[d]] = (total[:, halves[d]] + last1[h, d].astype(F32)).astype(BF16)
                fourth_send(h, d).start()
            else:
                for d in range(2):
                    fourth_send(h, d).wait_recv()
                out[:, h * wide : (h + 1) * wide] = (
                    total + last2[h, 0].astype(F32) + last2[h, 1].astype(F32)
                ).astype(BF16)
    for h in range(2):
        for d in range(2):
            for s in range(SIDE):
                first_send(h, d, s).wait_send()
                second_send(h, d, s).wait_send()
            third_send(h, d).wait_send()
            fourth_send(h, d).wait_send()


def scatter_terms(slot_at, d_all, weights, ident):
    blocks, _, local = d_all.shape
    full = weights.shape[0]
    wide = full // 2
    part = wide // 2
    vmem = pl.BlockSpec(memory_space=pltpu.VMEM)
    four = pltpu.SemaphoreType.DMA((2, 2, SIDE))
    two = pltpu.SemaphoreType.DMA((2, 2))
    return pl.pallas_call(
        scatter_kernel,
        out_shape=jax.ShapeDtypeStruct((BLK, full), BF16),
        in_specs=[pl.BlockSpec(memory_space=pltpu.SMEM), vmem, vmem],
        out_specs=vmem,
        scratch_shapes=[
            pltpu.VMEM((2, SIDE, SIDE, BLK, wide), BF16),
            pltpu.VMEM((2, 2, SIDE, BLK, part), BF16),
            pltpu.VMEM((2, 2, SIDE, BLK, wide), BF16),
            pltpu.VMEM((2, 2, SIDE, BLK, wide), BF16),
            pltpu.VMEM((2, SIDE, BLK, wide), BF16),
            pltpu.VMEM((2, 2, BLK, part), BF16),
            pltpu.VMEM((2, 2, BLK, wide), BF16),
            pltpu.VMEM((2, 2, BLK, wide), BF16),
            four, four, four, four, two, two, two, two,
        ],
        compiler_params=pltpu.CompilerParams(
            collective_id=ident, has_side_effects=True, vmem_limit_bytes=VMEM_LIMIT
        ),
        cost_estimate=pl.CostEstimate(
            flops=2 * blocks * BLK * local * full, bytes_accessed=100 * 1024 * 1024, transcendentals=0
        ),
        name="scatter_terms",
    )(slot_at, d_all, weights)


def weight_grad_kernel(d_t, normed, out):
    value = jnp.dot(d_t[...], normed[...], preferred_element_type=F32)
    for at in range(3):
        out[at] = value[at * HEAD : (at + 1) * HEAD, :].T.astype(BF16)


def weight_grad(d_t, normed, step=256):
    local, total_rows = d_t.shape
    full = normed.shape[1]
    return pl.pallas_call(
        weight_grad_kernel,
        out_shape=jax.ShapeDtypeStruct((3, full, HEAD), BF16),
        grid=(full // step,),
        in_specs=[
            pl.BlockSpec((local, total_rows), lambda g: (0, 0)),
            pl.BlockSpec((total_rows, step), lambda g: (0, g)),
        ],
        out_specs=pl.BlockSpec((3, step, HEAD), lambda g: (0, g, 0)),
        compiler_params=pltpu.CompilerParams(vmem_limit_bytes=VMEM_LIMIT),
        name="weight_grad",
    )(d_t, normed)


def assemble_kernel(table, head, rest, out):
    first = table[3 * pl.program_id(0)] == 1

    @pl.when(first)
    def _():
        out[...] = head[...]

    @pl.when(jnp.logical_not(first))
    def _():
        out[...] = rest[...]


def assemble(table, head, rest):
    rows, full = head.shape
    return pl.pallas_call(
        assemble_kernel,
        out_shape=jax.ShapeDtypeStruct((2 * rows, full), BF16),
        grid_spec=pltpu.PrefetchScalarGridSpec(
            num_scalar_prefetch=1,
            grid=(2 * rows // BLK,),
            in_specs=[
                pl.BlockSpec((BLK, full), lambda g, t: (t[3 * g + 1], 0)),
                pl.BlockSpec((BLK, full), lambda g, t: (t[3 * g + 2], 0)),
            ],
            out_specs=pl.BlockSpec((BLK, full), lambda g, t: (g, 0)),
        ),
        name="assemble",
    )(table, head, rest)


def shards(query_input, key_input, value_input, keep_blocks, dest_slots, proj_weights, cotangent):
    tok, full = query_input.shape[1:]
    per_shard = tok // BLK
    shard = lax.axis_index(SEQ)
    count = lax.axis_size(SEQ)
    half_blocks = per_shard // 2
    query = query_input.reshape(per_shard, BLK, full)
    key = key_input[0]
    value = value_input[0]
    keep = keep_blocks[0]
    dest = dest_slots[0]

    kept = jnp.any(
        keep[None, None, :] == jnp.arange(count * per_shard).reshape(count, per_shard)[:, :, None], axis=2
    )
    order_key = jnp.where(kept, 0, per_shard) + jnp.arange(per_shard)[None, :]
    rank = jnp.sum(order_key[:, None, :] < order_key[:, :, None], axis=2).astype(jnp.int32)
    order = jnp.sum(
        jnp.where(
            rank[:, None, :] == jnp.arange(per_shard)[None, :, None], jnp.arange(per_shard)[None, None, :], 0
        ),
        axis=2,
    ).astype(jnp.int32)
    wrapped = jnp.concatenate([order, order[:2]], axis=0)
    near = lax.dynamic_slice_in_dim(wrapped, shard, 3, 0)
    sel_first = near[:, :half_blocks].reshape(-1)
    sel_rest = near[:, half_blocks:].reshape(-1)
    own_rank = lax.dynamic_slice_in_dim(rank, shard, 1, 0)[0]
    in_first = (own_rank < half_blocks).astype(jnp.int32)
    at = own_rank % half_blocks
    table = jnp.stack([in_first, at * in_first, at * (1 - in_first)], axis=1).reshape(-1)
    keep_shard = keep // per_shard
    before = jnp.sum((keep_shard[None, :] == keep_shard[:, None]) & (keep[None, :] < keep[:, None]), axis=1)
    packed = (keep_shard * half_blocks + before).astype(jnp.int32)
    weights = jnp.concatenate([proj_weights[0], proj_weights[1], proj_weights[2]], axis=1)

    slot_at = jnp.sum(
        jnp.where(dest[None, :] == jnp.arange(dest.shape[0])[:, None], jnp.arange(dest.shape[0])[None, :], 0),
        axis=1,
    ).astype(jnp.int32)

    first = window(sel_first, query, key, value, 0, 1, 2, 0)
    gathered = lax.all_gather(first, SEQ, axis=0, tiled=True)
    sel_late, _ = lax.optimization_barrier((sel_rest, first))
    rest = window(sel_late, query, key, value, 0, 1, 2, 1)
    window_out = assemble(table, first, rest)

    packed_late, _ = lax.optimization_barrier((packed, rest))
    normed, qkv = project(packed_late, gathered, weights)
    causal_out, d_all, d_all_t = causal(dest, qkv, cotangent[0])
    local_grads = weight_grad(d_all_t, normed)
    grads = lax.psum(local_grads, "dp").astype(F32)
    slot_late, _ = lax.optimization_barrier((slot_at, local_grads))
    row_grad = scatter_terms(slot_late, d_all.reshape(dest.shape[0], BLK, -1), weights, 2)
    return (window_out[None], causal_out[None], grads, row_grad[None])


def solution(mesh):
    return jax.shard_map(
        shards,
        mesh=mesh,
        in_specs=(
            P("dp", "seq", None),
            P("dp", "seq", None),
            P("dp", "seq", None),
            P("dp", None),
            P("dp", None),
            P(None, None, "seq"),
            P("dp", None, "seq"),
        ),
        out_specs=(
            P("dp", "seq", None),
            P("dp", None, "seq"),
            P(None, None, "seq"),
            P("dp", "seq", None),
        ),
        check_vma=False,
    )
```

```python
import functools

import jax
import jax.numpy as jnp
from jax import lax
from jax.experimental import pallas as pl
from jax.experimental.pallas import tpu as pltpu
from jax.sharding import PartitionSpec as P

HEAD = 128
BLK = 128
SEQ = "seq"
MESH = pl.DeviceIdType.MESH
SCALE = HEAD ** (-0.5)
LOG2E = 1.4426950408889634
SCALE2 = SCALE * LOG2E
LOW = -1e30
NT = (((1,), (1,)), ((), ()))
BF16 = jnp.bfloat16
F32 = jnp.float32
VMEM_LIMIT = 56 * 1024 * 1024


def window_part(query, key, value_t, bias):
    scores = lax.dot_general(key, query, NT, preferred_element_type=F32)
    if bias is not None:
        scores = scores + bias
    top = jnp.max(scores, axis=0, keepdims=True)
    weight = jnp.exp2((scores - top) * SCALE2)
    total = jnp.sum(weight, axis=0, keepdims=True)
    out = jnp.dot(value_t, weight.astype(BF16), preferred_element_type=F32)
    return out / total, top * SCALE2 + jnp.log2(total)


def merged(out_a, lse_a, out_b, lse_b):
    top = jnp.maximum(lse_a, lse_b)
    weight_a = jnp.exp2(lse_a - top)
    weight_b = jnp.exp2(lse_b - top)
    total = weight_a + weight_b
    return out_a * (weight_a / total) + out_b * (weight_b / total), top + jnp.log2(total)


class Flow:
    def __init__(self, sel, q_in, k_in, v_in, out, scratch):
        (
            self.q_own, self.q_one, self.q_two, self.v_t, self.o_own, self.l_own, self.o_snd2, self.l_snd2,
            self.o_got2, self.l_got2, self.o_snd1, self.l_snd1, self.o_got1, self.l_got1,
            self.bias_own, self.bias_two, self.send_sem, self.recv_sem,
        ) = scratch
        self.sel, self.q_in, self.k_in, self.v_in, self.out = sel, q_in, k_in, v_in, out
        self.chunks, self.rows, self.width = self.q_own.shape
        self.per_chunk = self.width // HEAD
        self.lse_step = 8 // self.per_chunk
        self.shard = lax.axis_index(SEQ)
        count = lax.axis_size(SEQ)
        self.right = lax.rem(self.shard + 1, count)
        self.left = lax.rem(self.shard + count - 1, count)

    def copy(self, which, c, src, dst, target):
        return pltpu.make_async_remote_copy(
            src_ref=src.at[c], dst_ref=dst.at[c],
            send_sem=self.send_sem.at[which, c], recv_sem=self.recv_sem.at[which, c],
            device_id={SEQ: target}, device_id_type=MESH,
        )

    def hop_one(self, c):
        return self.copy(0, c, self.q_own, self.q_one, self.left)

    def hop_two(self, c):
        return self.copy(1, c, self.q_one, self.q_two, self.left)

    def back_two(self, c):
        return (
            self.copy(2, c, self.o_snd2, self.o_got2, self.right),
            self.copy(3, c, self.l_snd2, self.l_got2, self.right),
        )

    def back_one(self, c):
        return (
            self.copy(4, c, self.o_snd1, self.o_got1, self.right),
            self.copy(5, c, self.l_snd1, self.l_got1, self.right),
        )

    def begin(self, ahead):
        barrier = pltpu.get_barrier_semaphore()
        for neighbour in (self.left, self.right):
            pl.semaphore_signal(barrier, inc=1, device_id={SEQ: neighbour}, device_id_type=MESH)
        picks = self.rows // BLK
        for a in range(picks):
            block = self.q_in[self.sel[a]]
            for c in range(self.chunks):
                self.q_own[c, a * BLK : (a + 1) * BLK, :] = block[:, c * self.width : (c + 1) * self.width]
        pl.semaphore_wait(barrier, 2)
        for c in range(ahead):
            self.hop_one(c).start()
        self.ahead = ahead
        lane = lax.broadcasted_iota(jnp.int32, (1, self.rows), 1)
        key_at = lax.broadcasted_iota(jnp.int32, self.bias_own.shape, 0)
        for base, ref in ((0, self.bias_own), (2 * picks, self.bias_two)):
            place = lane
            for a in range(picks):
                place = jnp.where(lane // BLK == a, (lane - a * BLK) + self.sel[base + a] * BLK, place)
            seen = (key_at <= place) if base == 0 else (key_at > place)
            ref[...] = jnp.where(seen, 0.0, LOW)

    def cols(self, c, h):
        return pl.ds(pl.multiple_of(c * self.width + h * HEAD, HEAD), HEAD)

    def lse_at(self, h):
        return slice(h * self.lse_step, (h + 1) * self.lse_step)

    def spread(self, row):
        return jnp.broadcast_to(row, (self.lse_step, self.rows))

    def head(self, h):
        return slice(h * HEAD, (h + 1) * HEAD)

    def pump(self, c):
        self.hop_one(c).wait_recv()
        self.hop_two(c).start()

        @pl.when(c + self.ahead < self.chunks)
        def _():
            self.hop_one(c + self.ahead).start()

    def own(self, c):
        for h in range(self.per_chunk):
            cols = self.cols(c, h)
            value_t = self.v_in[:, cols].T
            self.v_t[cols, :] = value_t
            part, lse = window_part(
                self.q_own[c, :, self.head(h)], self.k_in[:, cols], value_t, self.bias_own[...]
            )
            self.o_own[c, self.head(h), :] = part
            self.l_own[c, self.lse_at(h), :] = self.spread(lse)

    def two(self, c):
        self.hop_two(c).wait_recv()
        for h in range(self.per_chunk):
            cols = self.cols(c, h)
            part, lse = window_part(
                self.q_two[c, :, self.head(h)], self.k_in[:, cols], self.v_t[cols, :], self.bias_two[...]
            )
            self.o_snd2[c, self.head(h), :] = part.astype(BF16)
            self.l_snd2[c, self.lse_at(h), :] = self.spread(lse)
        for each in self.back_two(c):
            each.start()

    def incoming(self, got, h, c):
        first = h * self.lse_step
        return jnp.where(self.shard == 0, LOW, got[c, first : first + 1, :])

    def one(self, c):
        parts = []
        for h in range(self.per_chunk):
            cols = self.cols(c, h)
            parts.append(
                window_part(self.q_one[c, :, self.head(h)], self.k_in[:, cols], self.v_t[cols, :], None)
            )
        for each in self.back_two(c):
            each.wait_recv()
        for h in range(self.per_chunk):
            part, lse = merged(
                *parts[h], self.o_got2[c, self.head(h), :].astype(F32), self.incoming(self.l_got2, h, c)
            )
            self.o_snd1[c, self.head(h), :] = part.astype(BF16)
            self.l_snd1[c, self.lse_at(h), :] = self.spread(lse)
        for each in self.back_one(c):
            each.start()

    def final(self, c):
        for each in self.back_one(c):
            each.wait_recv()
        for h in range(self.per_chunk):
            first = h * self.lse_step
            part, _ = merged(
                self.o_own[c, self.head(h), :], self.l_own[c, first : first + 1, :],
                self.o_got1[c, self.head(h), :].astype(F32), self.incoming(self.l_got1, h, c),
            )
            self.out[:, self.cols(c, h)] = part.T.astype(BF16)

    def step(self, t):
        @pl.when(t < self.chunks)
        def _():
            self.pump(t)
            self.own(t)

        @pl.when((t >= 1) & (t <= self.chunks))
        def _():
            self.two(t - 1)

        @pl.when((t >= 2) & (t <= self.chunks + 1))
        def _():
            self.one(t - 2)

        @pl.when(t >= 3)
        def _():
            self.final(t - 3)

    def drain(self):
        def body(c, carry):
            self.hop_one(c).wait_send()
            self.hop_two(c).wait_send()
            for each in self.back_two(c) + self.back_one(c):
                each.wait_send()
            return carry

        lax.fori_loop(0, self.chunks, body, 0)

    @staticmethod
    def scratch(rows, tok, full, per_chunk):
        width = per_chunk * HEAD
        chunks = full // width
        queries = pltpu.VMEM((chunks, rows, width), BF16)
        outs = pltpu.VMEM((chunks, width, rows), BF16)
        lses = pltpu.VMEM((chunks, 8, rows), F32)
        return [
            queries, queries, queries, pltpu.VMEM((full, tok), BF16), pltpu.VMEM((chunks, width, rows), F32), lses,
            outs, lses, outs, lses, outs, lses, outs, lses,
            pltpu.VMEM((tok, rows), F32), pltpu.VMEM((tok, rows), F32),
            pltpu.SemaphoreType.DMA((6, chunks)), pltpu.SemaphoreType.DMA((6, chunks)),
        ]


def window_kernel(sel, q_in, k_in, v_in, out, *scratch):
    flow = Flow(sel, q_in, k_in, v_in, out, scratch)
    flow.begin(2)

    def step(t, carry):
        flow.step(t)
        return carry

    lax.fori_loop(0, flow.chunks + 3, step, 0)
    flow.drain()


def window(sel, query, key, value, per_chunk, ident):
    tok, full = key.shape
    rows = sel.shape[0] // 3 * BLK
    vmem = pl.BlockSpec(memory_space=pltpu.VMEM)
    return pl.pallas_call(
        window_kernel,
        out_shape=jax.ShapeDtypeStruct((rows, full), BF16),
        in_specs=[pl.BlockSpec(memory_space=pltpu.SMEM), vmem, vmem, vmem],
        out_specs=vmem,
        scratch_shapes=Flow.scratch(rows, tok, full, per_chunk),
        compiler_params=pltpu.CompilerParams(
            collective_id=ident, has_side_effects=True, vmem_limit_bytes=VMEM_LIMIT
        ),
        cost_estimate=pl.CostEstimate(
            flops=12 * rows * tok * full, bytes_accessed=16 * 1024 * 1024, transcendentals=0
        ),
        name="window",
    )(sel, query, key, value)


def project_kernel(index, first, second, weights, normed, projected):
    for at, block in enumerate((first, second)):
        x = block[...].astype(F32)
        mean = jnp.sum(x * x, axis=1, keepdims=True) * (1.0 / x.shape[1])
        normed[at * BLK : (at + 1) * BLK, :] = (x * lax.rsqrt(mean + 1e-06)).astype(BF16)
    projected[...] = jnp.dot(normed[...], weights[...], preferred_element_type=F32).astype(BF16)


def project(index, rows, weights):
    kept = index.shape[0]
    full, local = weights.shape
    return pl.pallas_call(
        project_kernel,
        out_shape=(
            jax.ShapeDtypeStruct((kept * BLK, full), BF16),
            jax.ShapeDtypeStruct((kept * BLK, local), BF16),
        ),
        grid_spec=pltpu.PrefetchScalarGridSpec(
            num_scalar_prefetch=1,
            grid=(kept // 2,),
            in_specs=[
                pl.BlockSpec((BLK, full), lambda g, idx: (idx[2 * g], 0)),
                pl.BlockSpec((BLK, full), lambda g, idx: (idx[2 * g + 1], 0)),
                pl.BlockSpec((full, local), lambda g, idx: (0, 0)),
            ],
            out_specs=[
                pl.BlockSpec((2 * BLK, full), lambda g, idx: (g, 0)),
                pl.BlockSpec((2 * BLK, local), lambda g, idx: (g, 0)),
            ],
        ),
        compiler_params=pltpu.CompilerParams(vmem_limit_bytes=VMEM_LIMIT),
        name="project",
    )(index, rows, rows, weights)


QB = 256
KB = 512


def causal_kernel(
    dest, sel, qkv, cot, normed, q_in, k_in, v_in, out, d_all, grads, rest,
    rows_in, rows_sem, d_all_t, v_t, k_t, do_own, do_t, p_buf, dk_acc, dv_acc, dq_t, *scratch,
):
    kept = dest.shape[0]
    total_rows = qkv.shape[0]
    blocks = total_rows // QB
    rows_copy = pltpu.make_async_copy(normed, rows_in, rows_sem)
    rows_copy.start()
    flow = Flow(sel, q_in, k_in, v_in, rest, scratch)
    flow.begin(2)

    for j in range(kept):
        do_own[j * BLK : (j + 1) * BLK, :] = cot[dest[j]]

    def prepare(c, carry):
        at = pl.ds(pl.multiple_of(c * QB, QB), QB)
        k_t[:, at] = qkv[at, HEAD : 2 * HEAD].T
        v_t[:, at] = qkv[at, 2 * HEAD : 3 * HEAD].T
        do_t[:, at] = do_own[at, :].T
        return carry

    lax.fori_loop(0, blocks, prepare, 0)
    dk_acc[...] = jnp.zeros_like(dk_acc)
    dv_acc[...] = jnp.zeros_like(dv_acc)

    def query_block(i):
        rows = pl.ds(pl.multiple_of(i * QB, QB), QB)
        chunks = (i * QB + QB + KB - 1) // KB
        q_i = qkv[rows, :HEAD]
        do_i = do_own[rows, :]

        def scores_of(c, masked):
            keys = pl.ds(pl.multiple_of(c * KB, KB), KB)
            scores = lax.dot_general(qkv[keys, HEAD : 2 * HEAD], q_i, NT, preferred_element_type=F32)
            if masked:
                key_at = lax.broadcasted_iota(jnp.int32, (KB, QB), 0)
                row_at = lax.broadcasted_iota(jnp.int32, (KB, QB), 1)
                scores = jnp.where(key_at - row_at <= i * QB - (chunks - 1) * KB, scores, LOW)
            p_buf[keys, :] = scores
            return jnp.max(scores, axis=0, keepdims=True)

        top = lax.fori_loop(
            0, chunks - 1, lambda c, m: jnp.maximum(m, scores_of(c, False)), scores_of(chunks - 1, True)
        )

        def weigh(c, carry):
            total, acc = carry
            keys = pl.ds(pl.multiple_of(c * KB, KB), KB)
            weight = jnp.exp2((p_buf[keys, :] - top) * SCALE2)
            p_buf[keys, :] = weight
            total = total + jnp.sum(weight, axis=0, keepdims=True)
            acc = acc + jnp.dot(v_t[:, keys], weight.astype(BF16), preferred_element_type=F32)
            return total, acc

        total, acc = lax.fori_loop(
            0, chunks, weigh, (jnp.zeros((1, QB), F32), jnp.zeros((HEAD, QB), F32))
        )
        inv = 1.0 / total
        o_t = acc * inv
        delta = jnp.sum(o_t * do_t[:, rows].astype(F32), axis=0, keepdims=True)
        out[rows, :] = o_t.T.astype(BF16)

        def back(c, acc):
            keys = pl.ds(pl.multiple_of(c * KB, KB), KB)
            soft = p_buf[keys, :] * inv
            dv_acc[keys, :] += jnp.dot(soft.astype(BF16), do_i, preferred_element_type=F32)
            d_probs = lax.dot_general(qkv[keys, 2 * HEAD :], do_i, NT, preferred_element_type=F32)
            d_scores = (soft * (d_probs - delta) * SCALE).astype(BF16)
            dk_acc[keys, :] += jnp.dot(d_scores, q_i, preferred_element_type=F32)
            return acc + jnp.dot(k_t[:, keys], d_scores, preferred_element_type=F32)

        dq_t[:, rows] = lax.fori_loop(0, chunks, back, jnp.zeros((HEAD, QB), F32))

    def finish(c, carry):
        at = pl.ds(pl.multiple_of(c * QB, QB), QB)
        d_q = dq_t[:, at]
        d_all_t[:HEAD, at] = d_q.astype(BF16)
        d_all[at, :HEAD] = d_q.T.astype(BF16)
        for which, acc in ((1, dk_acc), (2, dv_acc)):
            value = acc[at, :]
            d_all[at, which * HEAD : (which + 1) * HEAD] = value.astype(BF16)
            d_all_t[which * HEAD : (which + 1) * HEAD, at] = value.T.astype(BF16)
        return carry

    def weight_block(g, carry):
        at = pl.ds(pl.multiple_of(g * QB, QB), QB)
        value = jnp.dot(d_all_t[...], rows_in[:, at], preferred_element_type=F32)
        for which in range(3):
            grads[which, at, :] = value[which * HEAD : (which + 1) * HEAD, :].T.astype(BF16)
        return carry

    col_blocks = rows_in.shape[1] // QB
    share = (col_blocks + 2) // 3

    def step(t, carry):
        flow.step(t)

        @pl.when(t < blocks)
        def _():
            query_block(blocks - 1 - t)

        @pl.when(t == blocks)
        def _():
            lax.fori_loop(0, blocks, finish, 0)
            rows_copy.wait()

        @pl.when(t >= blocks)
        def _():
            low = (t - blocks) * share
            lax.fori_loop(low, jnp.minimum(low + share, col_blocks), weight_block, 0)

        return carry

    lax.fori_loop(0, blocks + 3, step, 0)
    flow.drain()


def causal(dest, sel, qkv, cot, normed, query, key, value, per_chunk, ident):
    total_rows, local = qkv.shape
    tok, full = key.shape
    rows = sel.shape[0] // 3 * BLK
    vmem = pl.BlockSpec(memory_space=pltpu.VMEM)
    smem = pl.BlockSpec(memory_space=pltpu.SMEM)
    return pl.pallas_call(
        causal_kernel,
        out_shape=(
            jax.ShapeDtypeStruct((total_rows, HEAD), BF16),
            jax.ShapeDtypeStruct((total_rows, local), BF16),
            jax.ShapeDtypeStruct((3, full, HEAD), BF16),
            jax.ShapeDtypeStruct((rows, full), BF16),
        ),
        in_specs=[smem, smem, vmem, vmem, pl.BlockSpec(memory_space=pl.ANY), vmem, vmem, vmem],
        out_specs=[vmem, vmem, vmem, vmem],
        scratch_shapes=[
            pltpu.VMEM((total_rows, full), BF16),
            pltpu.SemaphoreType.DMA,
            pltpu.VMEM((local, total_rows), BF16),
            pltpu.VMEM((HEAD, total_rows), BF16),
            pltpu.VMEM((HEAD, total_rows), BF16),
            pltpu.VMEM((total_rows, HEAD), BF16),
            pltpu.VMEM((HEAD, total_rows), BF16),
            pltpu.VMEM((total_rows, QB), F32),
            pltpu.VMEM((total_rows, HEAD), F32),
            pltpu.VMEM((total_rows, HEAD), F32),
            pltpu.VMEM((HEAD, total_rows), F32),
            *Flow.scratch(rows, tok, full, per_chunk),
        ],
        compiler_params=pltpu.CompilerParams(
            collective_id=ident, has_side_effects=True, vmem_limit_bytes=VMEM_LIMIT
        ),
        cost_estimate=pl.CostEstimate(
            flops=20 * 10**9, bytes_accessed=32 * 1024 * 1024, transcendentals=0
        ),
        name="causal",
    )(dest, sel, qkv, cot, normed, query, key, value)


SIDE = 4


def scatter_kernel(
    slot_at, d_all, weights, out, terms, got1, snd2, got2, sums, last1, lasts2, last2,
    send1, recv1, send2, recv2, send3, recv3, send4, recv4,
):
    shard = lax.axis_index(SEQ)
    row, col = shard // SIDE, lax.rem(shard, SIDE)
    wide = out.shape[1] // 2
    part = wide // 2
    place = ((row, col), (col, row))
    halves = (slice(0, part), slice(part, wide))

    def turn(at, by):
        return lax.rem(at + by + SIDE, SIDE)

    def slot(h, a, b):
        return a * SIDE + b if h == 0 else b * SIDE + a

    barrier = pltpu.get_barrier_semaphore()
    for by in (1, -1):
        for h in range(2):
            a, b = place[h]
            pl.semaphore_signal(
                barrier, inc=1, device_id={SEQ: slot(h, turn(a, by), b)}, device_id_type=MESH
            )

    def group(h, a):
        slots = [jnp.where(h == 0, a * SIDE + s, s * SIDE + a) for s in range(SIDE)]
        rows = jnp.concatenate([d_all[slot_at[one]] for one in slots], axis=0)
        cols = pl.ds(pl.multiple_of(h * wide, wide), wide)
        value = lax.dot_general(rows, weights[cols, :], NT, preferred_element_type=F32).astype(BF16)
        for s in range(SIDE):
            terms[h, a, s] = value[s * BLK : (s + 1) * BLK, :]

    def first_send(h, d, s):
        a, b = place[h]
        return pltpu.make_async_remote_copy(
            src_ref=terms.at[h, turn(a, 2), s, :, halves[d]], dst_ref=got1.at[h, d, s],
            send_sem=send1.at[h, d, s], recv_sem=recv1.at[h, d, s],
            device_id={SEQ: slot(h, turn(a, 1 - 2 * d), b)}, device_id_type=MESH,
        )

    def second_send(h, d, s):
        a, b = place[h]
        return pltpu.make_async_remote_copy(
            src_ref=snd2.at[h, d, s], dst_ref=got2.at[h, d, s],
            send_sem=send2.at[h, d, s], recv_sem=recv2.at[h, d, s],
            device_id={SEQ: slot(h, turn(a, 1 - 2 * d), b)}, device_id_type=MESH,
        )

    def third_send(h, d):
        a, b = place[h]
        return pltpu.make_async_remote_copy(
            src_ref=sums.at[h, turn(b, 2), :, halves[d]], dst_ref=last1.at[h, d],
            send_sem=send3.at[h, d], recv_sem=recv3.at[h, d],
            device_id={SEQ: slot(h, a, turn(b, 1 - 2 * d))}, device_id_type=MESH,
        )

    def fourth_send(h, d):
        a, b = place[h]
        return pltpu.make_async_remote_copy(
            src_ref=lasts2.at[h, d], dst_ref=last2.at[h, d],
            send_sem=send4.at[h, d], recv_sem=recv4.at[h, d],
            device_id={SEQ: slot(h, a, turn(b, 1 - 2 * d))}, device_id_type=MESH,
        )

    def group_far(h, carry):
        group(h, turn(jnp.where(h == 0, row, col), 2))
        return carry

    def group_rest(g, carry):
        h, which = lax.rem(g, 2), g // 2
        by = jnp.where(which == 0, 1, jnp.where(which == 1, SIDE - 1, 0))
        group(h, turn(jnp.where(h == 0, row, col), by))
        return carry

    lax.fori_loop(0, 2, group_far, 0)
    pl.semaphore_wait(barrier, 4)
    for k in (2, 1, 3, 0):
        for h in range(2):
            s = turn(place[h][1], k)
            for d in range(2):
                first_send(h, d, s).start()
    lax.fori_loop(0, 6, group_rest, 0)
    for k in (2, 1, 3, 0):
        for h in range(2):
            a, b = place[h]
            s = turn(b, k)
            for d in range(2):
                first_send(h, d, s).wait_recv()
                near = turn(a, 1 - 2 * d)
                other = halves[1 - d]
                snd2[h, d, s, :, other] = terms[h, near, s, :, other]
                snd2[h, d, s, :, halves[d]] = (
                    terms[h, near, s, :, halves[d]].astype(F32) + got1[h, d, s].astype(F32)
                ).astype(BF16)
                second_send(h, d, s).start()
    for k in (2, 1, 3, 0):
        for h in range(2):
            a, b = place[h]
            s = turn(b, k)
            for d in range(2):
                second_send(h, d, s).wait_recv()
            total = (
                terms[h, a, s].astype(F32) + got2[h, 0, s].astype(F32) + got2[h, 1, s].astype(F32)
            )
            if k != 0:
                sums[h, s] = total.astype(BF16)
            if k == 2:
                for d in range(2):
                    third_send(h, d).start()
            elif k != 0:
                d = 0 if k == 1 else 1
                third_send(h, d).wait_recv()
                other = halves[1 - d]
                lasts2[h, d, :, other] = sums[h, s, :, other]
                lasts2[h, d, :, halves[d]] = (total[:, halves[d]] + last1[h, d].astype(F32)).astype(BF16)
                fourth_send(h, d).start()
            else:
                for d in range(2):
                    fourth_send(h, d).wait_recv()
                out[:, h * wide : (h + 1) * wide] = (
                    total + last2[h, 0].astype(F32) + last2[h, 1].astype(F32)
                ).astype(BF16)
    for h in range(2):
        for d in range(2):
            for s in range(SIDE):
                first_send(h, d, s).wait_send()
                second_send(h, d, s).wait_send()
            third_send(h, d).wait_send()
            fourth_send(h, d).wait_send()


def scatter_terms(slot_at, d_all, weights, ident):
    blocks, _, local = d_all.shape
    full = weights.shape[0]
    wide = full // 2
    part = wide // 2
    vmem = pl.BlockSpec(memory_space=pltpu.VMEM)
    four = pltpu.SemaphoreType.DMA((2, 2, SIDE))
    two = pltpu.SemaphoreType.DMA((2, 2))
    return pl.pallas_call(
        scatter_kernel,
        out_shape=jax.ShapeDtypeStruct((BLK, full), BF16),
        in_specs=[pl.BlockSpec(memory_space=pltpu.SMEM), vmem, vmem],
        out_specs=vmem,
        scratch_shapes=[
            pltpu.VMEM((2, SIDE, SIDE, BLK, wide), BF16),
            pltpu.VMEM((2, 2, SIDE, BLK, part), BF16),
            pltpu.VMEM((2, 2, SIDE, BLK, wide), BF16),
            pltpu.VMEM((2, 2, SIDE, BLK, wide), BF16),
            pltpu.VMEM((2, SIDE, BLK, wide), BF16),
            pltpu.VMEM((2, 2, BLK, part), BF16),
            pltpu.VMEM((2, 2, BLK, wide), BF16),
            pltpu.VMEM((2, 2, BLK, wide), BF16),
            four, four, four, four, two, two, two, two,
        ],
        compiler_params=pltpu.CompilerParams(
            collective_id=ident, has_side_effects=True, vmem_limit_bytes=VMEM_LIMIT
        ),
        cost_estimate=pl.CostEstimate(
            flops=2 * blocks * BLK * local * full, bytes_accessed=100 * 1024 * 1024, transcendentals=0
        ),
        name="scatter_terms",
    )(slot_at, d_all, weights)


def assemble_kernel(table, head, rest, sorted_out, out, causal_out):
    kept = sorted_out.shape[0] // BLK
    first = table[kept + 3 * pl.program_id(0)] == 1

    @pl.when(pl.program_id(0) == 0)
    def _():
        for j in range(kept):
            causal_out[pl.ds(pl.multiple_of(table[j] * BLK, BLK), BLK), :] = sorted_out[j * BLK : (j + 1) * BLK, :]

    @pl.when(first)
    def _():
        out[...] = head[...]

    @pl.when(jnp.logical_not(first))
    def _():
        out[...] = rest[...]


def assemble(table, head, rest, sorted_out):
    rows, full = head.shape
    kept = sorted_out.shape[0] // BLK
    whole = pl.BlockSpec(sorted_out.shape, lambda g, t: (0, 0))
    return pl.pallas_call(
        assemble_kernel,
        out_shape=(
            jax.ShapeDtypeStruct((2 * rows, full), BF16),
            jax.ShapeDtypeStruct(sorted_out.shape, BF16),
        ),
        grid_spec=pltpu.PrefetchScalarGridSpec(
            num_scalar_prefetch=1,
            grid=(2 * rows // BLK,),
            in_specs=[
                pl.BlockSpec((BLK, full), lambda g, t: (t[kept + 3 * g + 1], 0)),
                pl.BlockSpec((BLK, full), lambda g, t: (t[kept + 3 * g + 2], 0)),
                whole,
            ],
            out_specs=[pl.BlockSpec((BLK, full), lambda g, t: (g, 0)), whole],
        ),
        name="assemble",
    )(table, head, rest, sorted_out)


def shards(query_input, key_input, value_input, keep_blocks, dest_slots, proj_weights, cotangent):
    tok, full = query_input.shape[1:]
    per_shard = tok // BLK
    shard = lax.axis_index(SEQ)
    count = lax.axis_size(SEQ)
    half_blocks = per_shard // 2
    query = query_input.reshape(per_shard, BLK, full)
    key = key_input[0]
    value = value_input[0]
    keep = keep_blocks[0]
    dest = dest_slots[0]

    kept = jnp.any(
        keep[None, None, :] == jnp.arange(count * per_shard).reshape(count, per_shard)[:, :, None], axis=2
    )
    order_key = jnp.where(kept, 0, per_shard) + jnp.arange(per_shard)[None, :]
    rank = jnp.sum(order_key[:, None, :] < order_key[:, :, None], axis=2).astype(jnp.int32)
    order = jnp.sum(
        jnp.where(
            rank[:, None, :] == jnp.arange(per_shard)[None, :, None], jnp.arange(per_shard)[None, None, :], 0
        ),
        axis=2,
    ).astype(jnp.int32)
    wrapped = jnp.concatenate([order, order[:2]], axis=0)
    near = lax.dynamic_slice_in_dim(wrapped, shard, 3, 0)
    sel_first = near[:, :half_blocks].reshape(-1)
    sel_rest = near[:, half_blocks:].reshape(-1)
    own_rank = lax.dynamic_slice_in_dim(rank, shard, 1, 0)[0]
    in_first = (own_rank < half_blocks).astype(jnp.int32)
    at = own_rank % half_blocks
    table = jnp.stack([in_first, at * in_first, at * (1 - in_first)], axis=1).reshape(-1)
    keep_shard = keep // per_shard
    before = jnp.sum((keep_shard[None, :] == keep_shard[:, None]) & (keep[None, :] < keep[:, None]), axis=1)
    packed = (keep_shard * half_blocks + before).astype(jnp.int32)
    weights = jnp.concatenate([proj_weights[0], proj_weights[1], proj_weights[2]], axis=1)

    slot_at = jnp.sum(
        jnp.where(dest[None, :] == jnp.arange(dest.shape[0])[:, None], jnp.arange(dest.shape[0])[None, :], 0),
        axis=1,
    ).astype(jnp.int32)

    first = window(sel_first, query, key, value, 2, 0)
    gathered = lax.all_gather(first, SEQ, axis=0, tiled=True)
    normed, qkv = project(packed, gathered, weights)
    sorted_out, d_all, local_grads, rest = causal(
        dest, sel_rest, qkv, cotangent.reshape(dest.shape[0], BLK, -1), normed, query, key, value, 2, 1
    )
    grads = lax.psum(local_grads, "dp").astype(F32)
    window_out, causal_out = assemble(jnp.concatenate([dest, table]), first, rest, sorted_out)
    row_grad = scatter_terms(slot_at, d_all.reshape(dest.shape[0], BLK, -1), weights, 2)
    return (window_out[None], causal_out[None], grads, row_grad[None])


def solution(mesh):
    return jax.shard_map(
        shards,
        mesh=mesh,
        in_specs=(
            P("dp", "seq", None),
            P("dp", "seq", None),
            P("dp", "seq", None),
            P("dp", None),
            P("dp", None),
            P(None, None, "seq"),
            P("dp", None, "seq"),
        ),
        out_specs=(
            P("dp", "seq", None),
            P("dp", None, "seq"),
            P(None, None, "seq"),
            P("dp", "seq", None),
        ),
        check_vma=False,
    )
```

```python
import functools

import jax
import jax.numpy as jnp
from jax import lax
from jax.experimental import pallas as pl
from jax.experimental.pallas import tpu as pltpu
from jax.sharding import PartitionSpec as P

HEAD = 128
BLK = 128
SEQ = "seq"
MESH = pl.DeviceIdType.MESH
SCALE = HEAD ** (-0.5)
LOG2E = 1.4426950408889634
SCALE2 = SCALE * LOG2E
LOW = -1e30
NT = (((1,), (1,)), ((), ()))
BF16 = jnp.bfloat16
F32 = jnp.float32
VMEM_LIMIT = 56 * 1024 * 1024


def window_part(query, key, value_t, bias):
    scores = lax.dot_general(key, query, NT, preferred_element_type=F32)
    if bias is not None:
        scores = scores + bias
    top = jnp.max(scores, axis=0, keepdims=True)
    weight = jnp.exp2((scores - top) * SCALE2)
    total = jnp.sum(weight, axis=0, keepdims=True)
    out = jnp.dot(value_t, weight.astype(BF16), preferred_element_type=F32)
    return out / total, top * SCALE2 + jnp.log2(total)


def merged(out_a, lse_a, out_b, lse_b):
    top = jnp.maximum(lse_a, lse_b)
    weight_a = jnp.exp2(lse_a - top)
    weight_b = jnp.exp2(lse_b - top)
    total = weight_a + weight_b
    return out_a * (weight_a / total) + out_b * (weight_b / total), top + jnp.log2(total)


class Flow:
    def __init__(self, sel, q_in, k_in, v_in, out, scratch):
        (
            self.q_own, self.q_one, self.q_two, self.v_t, self.o_own, self.l_own, self.o_snd2, self.l_snd2,
            self.o_got2, self.l_got2, self.o_snd1, self.l_snd1, self.o_got1, self.l_got1,
            self.bias_own, self.bias_two, self.send_sem, self.recv_sem,
        ) = scratch
        self.sel, self.q_in, self.k_in, self.v_in, self.out = sel, q_in, k_in, v_in, out
        self.chunks, self.rows, self.width = self.q_own.shape
        self.per_chunk = self.width // HEAD
        self.lse_step = 8 // self.per_chunk
        self.shard = lax.axis_index(SEQ)
        count = lax.axis_size(SEQ)
        self.right = lax.rem(self.shard + 1, count)
        self.left = lax.rem(self.shard + count - 1, count)

    def copy(self, which, c, src, dst, target):
        return pltpu.make_async_remote_copy(
            src_ref=src.at[c], dst_ref=dst.at[c],
            send_sem=self.send_sem.at[which, c], recv_sem=self.recv_sem.at[which, c],
            device_id={SEQ: target}, device_id_type=MESH,
        )

    def hop_one(self, c):
        return self.copy(0, c, self.q_own, self.q_one, self.left)

    def hop_two(self, c):
        return self.copy(1, c, self.q_one, self.q_two, self.left)

    def back_two(self, c):
        return (
            self.copy(2, c, self.o_snd2, self.o_got2, self.right),
            self.copy(3, c, self.l_snd2, self.l_got2, self.right),
        )

    def back_one(self, c):
        return (
            self.copy(4, c, self.o_snd1, self.o_got1, self.right),
            self.copy(5, c, self.l_snd1, self.l_got1, self.right),
        )

    def begin(self, ahead, others=()):
        barrier = pltpu.get_barrier_semaphore()
        greeted = (self.left, self.right, *others)
        for neighbour in greeted:
            pl.semaphore_signal(barrier, inc=1, device_id={SEQ: neighbour}, device_id_type=MESH)
        picks = self.rows // BLK
        for a in range(picks):
            block = self.q_in[self.sel[a]]
            for c in range(self.chunks):
                self.q_own[c, a * BLK : (a + 1) * BLK, :] = block[:, c * self.width : (c + 1) * self.width]
        pl.semaphore_wait(barrier, len(greeted))
        for c in range(ahead):
            self.hop_one(c).start()
        self.ahead = ahead
        lane = lax.broadcasted_iota(jnp.int32, (1, self.rows), 1)
        key_at = lax.broadcasted_iota(jnp.int32, self.bias_own.shape, 0)
        for base, ref in ((0, self.bias_own), (2 * picks, self.bias_two)):
            place = lane
            for a in range(picks):
                place = jnp.where(lane // BLK == a, (lane - a * BLK) + self.sel[base + a] * BLK, place)
            seen = (key_at <= place) if base == 0 else (key_at > place)
            ref[...] = jnp.where(seen, 0.0, LOW)

    def cols(self, c, h):
        return pl.ds(pl.multiple_of(c * self.width + h * HEAD, HEAD), HEAD)

    def lse_at(self, h):
        return slice(h * self.lse_step, (h + 1) * self.lse_step)

    def spread(self, row):
        return jnp.broadcast_to(row, (self.lse_step, self.rows))

    def head(self, h):
        return slice(h * HEAD, (h + 1) * HEAD)

    def pump(self, c):
        self.hop_one(c).wait_recv()
        self.hop_two(c).start()

        @pl.when(c + self.ahead < self.chunks)
        def _():
            self.hop_one(c + self.ahead).start()

    def own(self, c):
        for h in range(self.per_chunk):
            cols = self.cols(c, h)
            value_t = self.v_in[:, cols].T
            self.v_t[cols, :] = value_t
            part, lse = window_part(
                self.q_own[c, :, self.head(h)], self.k_in[:, cols], value_t, self.bias_own[...]
            )
            self.o_own[c, self.head(h), :] = part
            self.l_own[c, self.lse_at(h), :] = self.spread(lse)

    def two(self, c):
        self.hop_two(c).wait_recv()
        for h in range(self.per_chunk):
            cols = self.cols(c, h)
            part, lse = window_part(
                self.q_two[c, :, self.head(h)], self.k_in[:, cols], self.v_t[cols, :], self.bias_two[...]
            )
            self.o_snd2[c, self.head(h), :] = part.astype(BF16)
            self.l_snd2[c, self.lse_at(h), :] = self.spread(lse)
        for each in self.back_two(c):
            each.start()

    def incoming(self, got, h, c):
        first = h * self.lse_step
        return jnp.where(self.shard == 0, LOW, got[c, first : first + 1, :])

    def one(self, c):
        parts = []
        for h in range(self.per_chunk):
            cols = self.cols(c, h)
            parts.append(
                window_part(self.q_one[c, :, self.head(h)], self.k_in[:, cols], self.v_t[cols, :], None)
            )
        for each in self.back_two(c):
            each.wait_recv()
        for h in range(self.per_chunk):
            part, lse = merged(
                *parts[h], self.o_got2[c, self.head(h), :].astype(F32), self.incoming(self.l_got2, h, c)
            )
            self.o_snd1[c, self.head(h), :] = part.astype(BF16)
            self.l_snd1[c, self.lse_at(h), :] = self.spread(lse)
        for each in self.back_one(c):
            each.start()

    def final(self, c):
        for each in self.back_one(c):
            each.wait_recv()
        for h in range(self.per_chunk):
            first = h * self.lse_step
            part, _ = merged(
                self.o_own[c, self.head(h), :], self.l_own[c, first : first + 1, :],
                self.o_got1[c, self.head(h), :].astype(F32), self.incoming(self.l_got1, h, c),
            )
            self.store(c, h, part.T.astype(BF16))

    def store(self, c, h, value):
        self.out[:, self.cols(c, h)] = value

    def step(self, t):
        @pl.when(t < self.chunks)
        def _():
            self.pump(t)
            self.own(t)

        @pl.when((t >= 1) & (t <= self.chunks))
        def _():
            self.two(t - 1)

        @pl.when((t >= 2) & (t <= self.chunks + 1))
        def _():
            self.one(t - 2)

        @pl.when((t >= 3) & (t <= self.chunks + 2))
        def _():
            self.final(t - 3)

    def drain(self):
        def body(c, carry):
            self.hop_one(c).wait_send()
            self.hop_two(c).wait_send()
            for each in self.back_two(c) + self.back_one(c):
                each.wait_send()
            return carry

        lax.fori_loop(0, self.chunks, body, 0)

    @staticmethod
    def scratch(rows, tok, full, per_chunk):
        width = per_chunk * HEAD
        chunks = full // width
        queries = pltpu.VMEM((chunks, rows, width), BF16)
        outs = pltpu.VMEM((chunks, width, rows), BF16)
        lses = pltpu.VMEM((chunks, 8, rows), F32)
        return [
            queries, queries, queries, pltpu.VMEM((full, tok), BF16), pltpu.VMEM((chunks, width, rows), F32), lses,
            outs, lses, outs, lses, outs, lses, outs, lses,
            pltpu.VMEM((tok, rows), F32), pltpu.VMEM((tok, rows), F32),
            pltpu.SemaphoreType.DMA((6, chunks)), pltpu.SemaphoreType.DMA((6, chunks)),
        ]


SIDE = 4


class Spread:
    OFFSETS = (0, 1, SIDE - 1, 2)

    def __init__(self, got, send_sem, recv_sem):
        self.got, self.send_sem, self.recv_sem = got, send_sem, recv_sem
        shard = lax.axis_index(SEQ)
        self.row, self.col = shard // SIDE, lax.rem(shard, SIDE)

    @staticmethod
    def turn(at, by):
        return lax.rem(at + by + SIDE, SIDE)

    def neighbours(self):
        return [self.row * SIDE + self.turn(self.col, by) for by in (1, -1)] + [
            self.turn(self.row, by) * SIDE + self.col for by in (1, -1)
        ]

    def places(self, c):
        rows_first = (c >= 3) & (lax.rem(c, 2) == 1)
        return rows_first, jnp.where(rows_first, self.row, self.col), jnp.where(rows_first, self.col, self.row)

    def message(self, c, which, place, half, target):
        rows_first, _, _ = self.places(c)
        a, b = place
        ta, tb = target
        slot = jnp.where(rows_first, a * SIDE + b, b * SIDE + a)
        device = jnp.where(rows_first, ta * SIDE + tb, tb * SIDE + ta)
        ref = self.got.at[c, slot] if half is None else self.got.at[c, slot, half]
        return pltpu.make_async_remote_copy(
            src_ref=ref, dst_ref=ref, send_sem=self.send_sem.at[c, which], recv_sem=self.recv_sem.at[c, which],
            device_id={SEQ: device}, device_id_type=MESH,
        )

    def ring(self, c, base, near):
        here, up, down, far = near(0), near(1), near(-1), near(2)
        direct = (
            self.message(c, base, here, None, up), self.message(c, base + 1, here, None, down),
        )
        direct_in = (
            self.message(c, base, down, None, up), self.message(c, base + 1, up, None, down),
        )
        half = (
            self.message(c, base + 2, down, 0, up), self.message(c, base + 3, up, 1, down),
        )
        half_in = (
            self.message(c, base + 2, far, 0, up), self.message(c, base + 3, far, 1, down),
        )
        return direct, direct_in, half, half_in

    def first_ring(self, c):
        _, a, b = self.places(c)
        return self.ring(c, 0, lambda by: (self.turn(a, by), b))

    def second_ring(self, c, k):
        _, a, b = self.places(c)
        origin = self.turn(a, self.OFFSETS[k])
        direct, direct_in, half, half_in = self.ring(c, 4 + 4 * k, lambda by: (origin, self.turn(b, by)))
        return direct, direct_in, half, half_in

    def second_sends(self, c, k):
        _, a, b = self.places(c)
        origin = self.turn(a, self.OFFSETS[k])
        up, down = (a, self.turn(b, 1)), (a, self.turn(b, -1))
        base = 4 + 4 * k
        direct = (
            self.message(c, base, (origin, b), None, up), self.message(c, base + 1, (origin, b), None, down),
        )
        half = (
            self.message(c, base + 2, (origin, self.turn(b, -1)), 0, up),
            self.message(c, base + 3, (origin, self.turn(b, 1)), 1, down),
        )
        return direct, half

    def launch(self, c):
        for each in self.first_ring(c)[0]:
            each.start()

    def relay(self, c):
        _, direct_in, half, _ = self.first_ring(c)
        for each in direct_in:
            each.wait_recv()
        for each in half:
            each.start()
        for k in range(3):
            for each in self.second_sends(c, k)[0]:
                each.start()

    def relay_far(self, c):
        for each in self.first_ring(c)[3]:
            each.wait_recv()
        for each in self.second_sends(c, 3)[0]:
            each.start()

    def second_relay(self, c):
        for k in range(4):
            for each in self.second_ring(c, k)[1]:
                each.wait_recv()
            for each in self.second_sends(c, k)[1]:
                each.start()

    def settle(self, c):
        for k in range(4):
            for each in self.second_ring(c, k)[3]:
                each.wait_recv()

    def drain(self, c):
        direct, _, half, _ = self.first_ring(c)
        for each in direct + half:
            each.wait_send()
        for k in range(4):
            direct, half = self.second_sends(c, k)
            for each in direct + half:
                each.wait_send()


def front_kernel(
    kept_shard, kept_at, sel, q_in, k_in, v_in, weights, out, rows_out, projected, scale_out,
    got, held, staged, staged_sem, total, squares, spread_send, spread_recv, *scratch,
):
    kept = kept_shard.shape[0]
    flow = Flow(sel, q_in, k_in, v_in, out, scratch)
    spread = Spread(got, spread_send, spread_recv)
    chunks, width = flow.chunks, flow.width
    total_rows, local = projected.shape
    full = k_in.shape[1]
    block = 512

    def store(c, h, value):
        out[:, flow.cols(c, h)] = value
        for a in range(flow.rows // BLK):
            got[c, flow.shard, a, :, flow.head(h)] = value[a * BLK : (a + 1) * BLK, :]

    flow.store = store
    flow.begin(3, spread.neighbours())
    total[...] = jnp.zeros_like(total)
    squares[...] = jnp.zeros_like(squares)

    def staged_copy(c):
        which = lax.rem(c, 2)
        return pltpu.make_async_copy(staged.at[which], rows_out.at[c], staged_sem.at[which])

    def project_chunk(c):
        which = lax.rem(c, 2)

        @pl.when(c >= 2)
        def _():
            staged_copy(c - 2).wait()

        def hold(i, carry):
            held[i] = got[c, i]
            return carry

        lax.fori_loop(0, SIDE * SIDE, hold, 0)

        def pick(j, carry):
            at = pl.ds(pl.multiple_of(j * BLK, BLK), BLK)
            staged[which, at, :] = held[kept_shard[j], kept_at[j]]
            return carry

        lax.fori_loop(0, kept, pick, 0)
        staged_copy(c).start()
        weight = weights[pl.ds(pl.multiple_of(c * width, width), width), :]

        def multiply(r, carry):
            at = pl.ds(pl.multiple_of(r * block, block), block)
            rows = staged[which, at, :]
            total[at, :] += jnp.dot(rows, weight, preferred_element_type=F32)
            wide = rows.astype(F32)
            square = wide * wide
            squares[at, :] += sum(square[:, h * HEAD : (h + 1) * HEAD] for h in range(flow.per_chunk))
            return carry

        lax.fori_loop(0, total_rows // block, multiply, 0)

    def step(t, carry):
        flow.step(t)

        def stage(late, call):
            @pl.when((t >= late) & (t < chunks + late))
            def _():
                call(t - late)

        stage(3, spread.launch)
        stage(4, spread.relay)
        stage(5, spread.relay_far)
        stage(6, spread.second_relay)

        @pl.when(t >= 7)
        def _():
            spread.settle(t - 7)
            project_chunk(t - 7)

        return carry

    lax.fori_loop(0, chunks + 7, step, 0)

    def finish(r, carry):
        at = pl.ds(pl.multiple_of(r * block, block), block)
        square = squares[at, :]
        inv = lax.rsqrt(jnp.sum(square, axis=1, keepdims=True) * (1.0 / full) + 1e-06)
        projected[at, :] = (total[at, :] * inv).astype(BF16)
        scale_out[:, at] = lax.rsqrt(jnp.sum(square.T, axis=0, keepdims=True) * (1.0 / full) + 1e-06)
        return carry

    lax.fori_loop(0, total_rows // block, finish, 0)

    def drain(c, carry):
        spread.drain(c)
        return carry

    lax.fori_loop(0, chunks, drain, 0)
    for c in (chunks - 2, chunks - 1):
        staged_copy(c).wait()
    flow.drain()


def front(kept_shard, kept_at, sel, query, key, value, weights, per_chunk, ident):
    tok, full = key.shape
    local = weights.shape[1]
    rows = sel.shape[0] // 3 * BLK
    total_rows = kept_shard.shape[0] * BLK
    width = per_chunk * HEAD
    chunks = full // width
    vmem = pl.BlockSpec(memory_space=pltpu.VMEM)
    smem = pl.BlockSpec(memory_space=pltpu.SMEM)
    return pl.pallas_call(
        front_kernel,
        out_shape=(
            jax.ShapeDtypeStruct((rows, full), BF16),
            jax.ShapeDtypeStruct((chunks, total_rows, width), BF16),
            jax.ShapeDtypeStruct((total_rows, local), BF16),
            jax.ShapeDtypeStruct((1, total_rows), F32),
        ),
        in_specs=[smem, smem, smem, vmem, vmem, vmem, vmem],
        out_specs=[vmem, pl.BlockSpec(memory_space=pl.ANY), vmem, vmem],
        scratch_shapes=[
            pltpu.VMEM((chunks, SIDE * SIDE, rows // BLK, BLK, width), BF16),
            pltpu.VMEM((SIDE * SIDE, rows // BLK, BLK, width), BF16),
            pltpu.VMEM((2, total_rows, width), BF16),
            pltpu.SemaphoreType.DMA((2,)),
            pltpu.VMEM((total_rows, local), F32),
            pltpu.VMEM((total_rows, HEAD), F32),
            pltpu.SemaphoreType.DMA((chunks, 20)),
            pltpu.SemaphoreType.DMA((chunks, 20)),
            *Flow.scratch(rows, tok, full, per_chunk),
        ],
        compiler_params=pltpu.CompilerParams(
            collective_id=ident, has_side_effects=True, vmem_limit_bytes=VMEM_LIMIT
        ),
        name="front",
    )(kept_shard, kept_at, sel, query, key, value, weights)


QB = 256
KB = 512


def causal_kernel(
    dest, sel, qkv, scale, cot, gathered, q_in, k_in, v_in, out, d_all, grads, rest,
    rows_in, rows_sem, d_all_t, v_t, k_t, do_own, do_t, p_buf, dk_acc, dv_acc, dq_t, *scratch,
):
    kept = dest.shape[0]
    total_rows = qkv.shape[0]
    blocks = total_rows // QB
    rows_copy = pltpu.make_async_copy(gathered, rows_in, rows_sem)
    rows_copy.start()
    flow = Flow(sel, q_in, k_in, v_in, rest, scratch)
    flow.begin(3)

    for j in range(kept):
        do_own[j * BLK : (j + 1) * BLK, :] = cot[dest[j]]

    def prepare(c, carry):
        at = pl.ds(pl.multiple_of(c * QB, QB), QB)
        k_t[:, at] = qkv[at, HEAD : 2 * HEAD].T
        v_t[:, at] = qkv[at, 2 * HEAD : 3 * HEAD].T
        do_t[:, at] = do_own[at, :].T
        return carry

    lax.fori_loop(0, blocks, prepare, 0)
    dk_acc[...] = jnp.zeros_like(dk_acc)
    dv_acc[...] = jnp.zeros_like(dv_acc)

    def query_block(i):
        rows = pl.ds(pl.multiple_of(i * QB, QB), QB)
        chunks = (i * QB + QB + KB - 1) // KB
        q_i = qkv[rows, :HEAD]
        do_i = do_own[rows, :]

        def scores_of(c, masked):
            keys = pl.ds(pl.multiple_of(c * KB, KB), KB)
            scores = lax.dot_general(qkv[keys, HEAD : 2 * HEAD], q_i, NT, preferred_element_type=F32)
            if masked:
                key_at = lax.broadcasted_iota(jnp.int32, (KB, QB), 0)
                row_at = lax.broadcasted_iota(jnp.int32, (KB, QB), 1)
                scores = jnp.where(key_at - row_at <= i * QB - (chunks - 1) * KB, scores, LOW)
            p_buf[keys, :] = scores
            return jnp.max(scores, axis=0, keepdims=True)

        top = lax.fori_loop(
            0, chunks - 1, lambda c, m: jnp.maximum(m, scores_of(c, False)), scores_of(chunks - 1, True)
        )

        def weigh(c, carry):
            total, acc = carry
            keys = pl.ds(pl.multiple_of(c * KB, KB), KB)
            weight = jnp.exp2((p_buf[keys, :] - top) * SCALE2)
            p_buf[keys, :] = weight
            total = total + jnp.sum(weight, axis=0, keepdims=True)
            acc = acc + jnp.dot(v_t[:, keys], weight.astype(BF16), preferred_element_type=F32)
            return total, acc

        total, acc = lax.fori_loop(
            0, chunks, weigh, (jnp.zeros((1, QB), F32), jnp.zeros((HEAD, QB), F32))
        )
        inv = 1.0 / total
        o_t = acc * inv
        delta = jnp.sum(o_t * do_t[:, rows].astype(F32), axis=0, keepdims=True)
        out[rows, :] = o_t.T.astype(BF16)

        def back(c, acc):
            keys = pl.ds(pl.multiple_of(c * KB, KB), KB)
            soft = p_buf[keys, :] * inv
            dv_acc[keys, :] += jnp.dot(soft.astype(BF16), do_i, preferred_element_type=F32)
            d_probs = lax.dot_general(qkv[keys, 2 * HEAD :], do_i, NT, preferred_element_type=F32)
            d_scores = (soft * (d_probs - delta) * SCALE).astype(BF16)
            dk_acc[keys, :] += jnp.dot(d_scores, q_i, preferred_element_type=F32)
            return acc + jnp.dot(k_t[:, keys], d_scores, preferred_element_type=F32)

        dq_t[:, rows] = lax.fori_loop(0, chunks, back, jnp.zeros((HEAD, QB), F32))

    def finish(c, carry):
        at = pl.ds(pl.multiple_of(c * QB, QB), QB)
        d_q = dq_t[:, at]
        d_all_t[:HEAD, at] = (d_q * scale[:, at]).astype(BF16)
        d_all[at, :HEAD] = d_q.T.astype(BF16)
        for which, acc in ((1, dk_acc), (2, dv_acc)):
            value = acc[at, :]
            d_all[at, which * HEAD : (which + 1) * HEAD] = value.astype(BF16)
            d_all_t[which * HEAD : (which + 1) * HEAD, at] = (value.T * scale[:, at]).astype(BF16)
        return carry

    def weight_block(g, carry):
        at = pl.ds(pl.multiple_of(g * QB, QB), QB)
        value = jnp.dot(d_all_t[...], rows_in[g], preferred_element_type=F32)
        for which in range(3):
            grads[which, at, :] = value[which * HEAD : (which + 1) * HEAD, :].T.astype(BF16)
        return carry

    col_blocks = rows_in.shape[0]
    share = (col_blocks + 2) // 3

    def step(t, carry):
        flow.step(t)

        @pl.when(t < blocks)
        def _():
            query_block(blocks - 1 - t)

        @pl.when(t == blocks)
        def _():
            lax.fori_loop(0, blocks, finish, 0)
            rows_copy.wait()

        @pl.when(t >= blocks)
        def _():
            low = (t - blocks) * share
            lax.fori_loop(low, jnp.minimum(low + share, col_blocks), weight_block, 0)

        return carry

    lax.fori_loop(0, blocks + 3, step, 0)
    flow.drain()


def causal(dest, sel, qkv, scale, cot, gathered, query, key, value, per_chunk, ident):
    total_rows, local = qkv.shape
    tok, full = key.shape
    rows = sel.shape[0] // 3 * BLK
    vmem = pl.BlockSpec(memory_space=pltpu.VMEM)
    smem = pl.BlockSpec(memory_space=pltpu.SMEM)
    return pl.pallas_call(
        causal_kernel,
        out_shape=(
            jax.ShapeDtypeStruct((total_rows, HEAD), BF16),
            jax.ShapeDtypeStruct((total_rows, local), BF16),
            jax.ShapeDtypeStruct((3, full, HEAD), BF16),
            jax.ShapeDtypeStruct((rows, full), BF16),
        ),
        in_specs=[smem, smem, vmem, vmem, vmem, pl.BlockSpec(memory_space=pl.ANY), vmem, vmem, vmem],
        out_specs=[vmem, vmem, vmem, vmem],
        scratch_shapes=[
            pltpu.VMEM(gathered.shape, BF16),
            pltpu.SemaphoreType.DMA,
            pltpu.VMEM((local, total_rows), BF16),
            pltpu.VMEM((HEAD, total_rows), BF16),
            pltpu.VMEM((HEAD, total_rows), BF16),
            pltpu.VMEM((total_rows, HEAD), BF16),
            pltpu.VMEM((HEAD, total_rows), BF16),
            pltpu.VMEM((total_rows, QB), F32),
            pltpu.VMEM((total_rows, HEAD), F32),
            pltpu.VMEM((total_rows, HEAD), F32),
            pltpu.VMEM((HEAD, total_rows), F32),
            *Flow.scratch(rows, tok, full, per_chunk),
        ],
        compiler_params=pltpu.CompilerParams(
            collective_id=ident, has_side_effects=True, vmem_limit_bytes=VMEM_LIMIT
        ),
        cost_estimate=pl.CostEstimate(
            flops=20 * 10**9, bytes_accessed=32 * 1024 * 1024, transcendentals=0
        ),
        name="causal",
    )(dest, sel, qkv, scale, cot, gathered, query, key, value)


def scatter_kernel(
    slot_at, d_all, weights, out, terms, got1, snd2, got2, sums, last1, lasts2, last2,
    send1, recv1, send2, recv2, send3, recv3, send4, recv4,
):
    shard = lax.axis_index(SEQ)
    row, col = shard // SIDE, lax.rem(shard, SIDE)
    wide = out.shape[1] // 2
    part = wide // 2
    place = ((row, col), (col, row))
    halves = (slice(0, part), slice(part, wide))

    def turn(at, by):
        return lax.rem(at + by + SIDE, SIDE)

    def slot(h, a, b):
        return a * SIDE + b if h == 0 else b * SIDE + a

    barrier = pltpu.get_barrier_semaphore()
    for by in (1, -1):
        for h in range(2):
            a, b = place[h]
            pl.semaphore_signal(
                barrier, inc=1, device_id={SEQ: slot(h, turn(a, by), b)}, device_id_type=MESH
            )

    def group(h, a):
        slots = [jnp.where(h == 0, a * SIDE + s, s * SIDE + a) for s in range(SIDE)]
        rows = jnp.concatenate([d_all[slot_at[one]] for one in slots], axis=0)
        cols = pl.ds(pl.multiple_of(h * wide, wide), wide)
        value = lax.dot_general(rows, weights[cols, :], NT, preferred_element_type=F32).astype(BF16)
        for s in range(SIDE):
            terms[h, a, s] = value[s * BLK : (s + 1) * BLK, :]

    def first_send(h, d, s):
        a, b = place[h]
        return pltpu.make_async_remote_copy(
            src_ref=terms.at[h, turn(a, 2), s, :, halves[d]], dst_ref=got1.at[h, d, s],
            send_sem=send1.at[h, d, s], recv_sem=recv1.at[h, d, s],
            device_id={SEQ: slot(h, turn(a, 1 - 2 * d), b)}, device_id_type=MESH,
        )

    def second_send(h, d, s):
        a, b = place[h]
        return pltpu.make_async_remote_copy(
            src_ref=snd2.at[h, d, s], dst_ref=got2.at[h, d, s],
            send_sem=send2.at[h, d, s], recv_sem=recv2.at[h, d, s],
            device_id={SEQ: slot(h, turn(a, 1 - 2 * d), b)}, device_id_type=MESH,
        )

    def third_send(h, d):
        a, b = place[h]
        return pltpu.make_async_remote_copy(
            src_ref=sums.at[h, turn(b, 2), :, halves[d]], dst_ref=last1.at[h, d],
            send_sem=send3.at[h, d], recv_sem=recv3.at[h, d],
            device_id={SEQ: slot(h, a, turn(b, 1 - 2 * d))}, device_id_type=MESH,
        )

    def fourth_send(h, d):
        a, b = place[h]
        return pltpu.make_async_remote_copy(
            src_ref=lasts2.at[h, d], dst_ref=last2.at[h, d],
            send_sem=send4.at[h, d], recv_sem=recv4.at[h, d],
            device_id={SEQ: slot(h, a, turn(b, 1 - 2 * d))}, device_id_type=MESH,
        )

    def group_far(h, carry):
        group(h, turn(jnp.where(h == 0, row, col), 2))
        return carry

    def group_rest(g, carry):
        h, which = lax.rem(g, 2), g // 2
        by = jnp.where(which == 0, 1, jnp.where(which == 1, SIDE - 1, 0))
        group(h, turn(jnp.where(h == 0, row, col), by))
        return carry

    lax.fori_loop(0, 2, group_far, 0)
    pl.semaphore_wait(barrier, 4)
    for k in (2, 1, 3, 0):
        for h in range(2):
            s = turn(place[h][1], k)
            for d in range(2):
                first_send(h, d, s).start()
    lax.fori_loop(0, 6, group_rest, 0)
    for k in (2, 1, 3, 0):
        for h in range(2):
            a, b = place[h]
            s = turn(b, k)
            for d in range(2):
                first_send(h, d, s).wait_recv()
                near = turn(a, 1 - 2 * d)
                other = halves[1 - d]
                snd2[h, d, s, :, other] = terms[h, near, s, :, other]
                snd2[h, d, s, :, halves[d]] = (
                    terms[h, near, s, :, halves[d]].astype(F32) + got1[h, d, s].astype(F32)
                ).astype(BF16)
                second_send(h, d, s).start()
    for k in (2, 1, 3, 0):
        for h in range(2):
            a, b = place[h]
            s = turn(b, k)
            for d in range(2):
                second_send(h, d, s).wait_recv()
            total = (
                terms[h, a, s].astype(F32) + got2[h, 0, s].astype(F32) + got2[h, 1, s].astype(F32)
            )
            if k != 0:
                sums[h, s] = total.astype(BF16)
            if k == 2:
                for d in range(2):
                    third_send(h, d).start()
            elif k != 0:
                d = 0 if k == 1 else 1
                third_send(h, d).wait_recv()
                other = halves[1 - d]
                lasts2[h, d, :, other] = sums[h, s, :, other]
                lasts2[h, d, :, halves[d]] = (total[:, halves[d]] + last1[h, d].astype(F32)).astype(BF16)
                fourth_send(h, d).start()
            else:
                for d in range(2):
                    fourth_send(h, d).wait_recv()
                out[:, h * wide : (h + 1) * wide] = (
                    total + last2[h, 0].astype(F32) + last2[h, 1].astype(F32)
                ).astype(BF16)
    for h in range(2):
        for d in range(2):
            for s in range(SIDE):
                first_send(h, d, s).wait_send()
                second_send(h, d, s).wait_send()
            third_send(h, d).wait_send()
            fourth_send(h, d).wait_send()


def scatter_terms(slot_at, d_all, weights, ident):
    blocks, _, local = d_all.shape
    full = weights.shape[0]
    wide = full // 2
    part = wide // 2
    vmem = pl.BlockSpec(memory_space=pltpu.VMEM)
    four = pltpu.SemaphoreType.DMA((2, 2, SIDE))
    two = pltpu.SemaphoreType.DMA((2, 2))
    return pl.pallas_call(
        scatter_kernel,
        out_shape=jax.ShapeDtypeStruct((BLK, full), BF16),
        in_specs=[pl.BlockSpec(memory_space=pltpu.SMEM), vmem, vmem],
        out_specs=vmem,
        scratch_shapes=[
            pltpu.VMEM((2, SIDE, SIDE, BLK, wide), BF16),
            pltpu.VMEM((2, 2, SIDE, BLK, part), BF16),
            pltpu.VMEM((2, 2, SIDE, BLK, wide), BF16),
            pltpu.VMEM((2, 2, SIDE, BLK, wide), BF16),
            pltpu.VMEM((2, SIDE, BLK, wide), BF16),
            pltpu.VMEM((2, 2, BLK, part), BF16),
            pltpu.VMEM((2, 2, BLK, wide), BF16),
            pltpu.VMEM((2, 2, BLK, wide), BF16),
            four, four, four, four, two, two, two, two,
        ],
        compiler_params=pltpu.CompilerParams(
            collective_id=ident, has_side_effects=True, vmem_limit_bytes=VMEM_LIMIT
        ),
        cost_estimate=pl.CostEstimate(
            flops=2 * blocks * BLK * local * full, bytes_accessed=100 * 1024 * 1024, transcendentals=0
        ),
        name="scatter_terms",
    )(slot_at, d_all, weights)


def assemble_kernel(table, head, rest, sorted_out, out, causal_out):
    kept = sorted_out.shape[0] // BLK
    first = table[kept + 3 * pl.program_id(0)] == 1

    @pl.when(pl.program_id(0) == 0)
    def _():
        for j in range(kept):
            causal_out[pl.ds(pl.multiple_of(table[j] * BLK, BLK), BLK), :] = sorted_out[j * BLK : (j + 1) * BLK, :]

    @pl.when(first)
    def _():
        out[...] = head[...]

    @pl.when(jnp.logical_not(first))
    def _():
        out[...] = rest[...]


def assemble(table, head, rest, sorted_out):
    rows, full = head.shape
    kept = sorted_out.shape[0] // BLK
    whole = pl.BlockSpec(sorted_out.shape, lambda g, t: (0, 0))
    return pl.pallas_call(
        assemble_kernel,
        out_shape=(
            jax.ShapeDtypeStruct((2 * rows, full), BF16),
            jax.ShapeDtypeStruct(sorted_out.shape, BF16),
        ),
        grid_spec=pltpu.PrefetchScalarGridSpec(
            num_scalar_prefetch=1,
            grid=(2 * rows // BLK,),
            in_specs=[
                pl.BlockSpec((BLK, full), lambda g, t: (t[kept + 3 * g + 1], 0)),
                pl.BlockSpec((BLK, full), lambda g, t: (t[kept + 3 * g + 2], 0)),
                whole,
            ],
            out_specs=[pl.BlockSpec((BLK, full), lambda g, t: (g, 0)), whole],
        ),
        name="assemble",
    )(table, head, rest, sorted_out)


def shards(query_input, key_input, value_input, keep_blocks, dest_slots, proj_weights, cotangent):
    tok, full = query_input.shape[1:]
    per_shard = tok // BLK
    shard = lax.axis_index(SEQ)
    count = lax.axis_size(SEQ)
    half_blocks = per_shard // 2
    query = query_input.reshape(per_shard, BLK, full)
    key = key_input[0]
    value = value_input[0]
    keep = keep_blocks[0]
    dest = dest_slots[0]

    kept = jnp.any(
        keep[None, None, :] == jnp.arange(count * per_shard).reshape(count, per_shard)[:, :, None], axis=2
    )
    order_key = jnp.where(kept, 0, per_shard) + jnp.arange(per_shard)[None, :]
    rank = jnp.sum(order_key[:, None, :] < order_key[:, :, None], axis=2).astype(jnp.int32)
    order = jnp.sum(
        jnp.where(
            rank[:, None, :] == jnp.arange(per_shard)[None, :, None], jnp.arange(per_shard)[None, None, :], 0
        ),
        axis=2,
    ).astype(jnp.int32)
    wrapped = jnp.concatenate([order, order[:2]], axis=0)
    near = lax.dynamic_slice_in_dim(wrapped, shard, 3, 0)
    sel_first = near[:, :half_blocks].reshape(-1)
    sel_rest = near[:, half_blocks:].reshape(-1)
    own_rank = lax.dynamic_slice_in_dim(rank, shard, 1, 0)[0]
    in_first = (own_rank < half_blocks).astype(jnp.int32)
    at = own_rank % half_blocks
    table = jnp.stack([in_first, at * in_first, at * (1 - in_first)], axis=1).reshape(-1)
    keep_shard = keep // per_shard
    before = jnp.sum((keep_shard[None, :] == keep_shard[:, None]) & (keep[None, :] < keep[:, None]), axis=1)
    weights = jnp.concatenate([proj_weights[0], proj_weights[1], proj_weights[2]], axis=1)

    slot_at = jnp.sum(
        jnp.where(dest[None, :] == jnp.arange(dest.shape[0])[:, None], jnp.arange(dest.shape[0])[None, :], 0),
        axis=1,
    ).astype(jnp.int32)

    first, gathered, qkv, scale = front(
        keep_shard.astype(jnp.int32), before.astype(jnp.int32), sel_first, query, key, value, weights, 2, 0
    )
    sorted_out, d_all, local_grads, rest = causal(
        dest, sel_rest, qkv, scale, cotangent.reshape(dest.shape[0], BLK, -1), gathered, query, key, value, 2, 1
    )
    grads = lax.psum(local_grads, "dp").astype(F32)
    window_out, causal_out = assemble(jnp.concatenate([dest, table]), first, rest, sorted_out)
    row_grad = scatter_terms(slot_at, d_all.reshape(dest.shape[0], BLK, -1), weights, 2)
    return (window_out[None], causal_out[None], grads, row_grad[None])


def solution(mesh):
    return jax.shard_map(
        shards,
        mesh=mesh,
        in_specs=(
            P("dp", "seq", None),
            P("dp", "seq", None),
            P("dp", "seq", None),
            P("dp", None),
            P("dp", None),
            P(None, None, "seq"),
            P("dp", None, "seq"),
        ),
        out_specs=(
            P("dp", "seq", None),
            P("dp", None, "seq"),
            P(None, None, "seq"),
            P("dp", "seq", None),
        ),
        check_vma=False,
    )
```

```python
import functools

import jax
import jax.numpy as jnp
from jax import lax
from jax.experimental import pallas as pl
from jax.experimental.pallas import tpu as pltpu
from jax.sharding import PartitionSpec as P

HEAD = 128
BLK = 128
SEQ = "seq"
MESH = pl.DeviceIdType.MESH
SCALE = HEAD ** (-0.5)
LOG2E = 1.4426950408889634
SCALE2 = SCALE * LOG2E
LOW = -1e30
NT = (((1,), (1,)), ((), ()))
BF16 = jnp.bfloat16
F32 = jnp.float32
VMEM_LIMIT = 56 * 1024 * 1024


def window_part(query, key, value_t, bias):
    scores = lax.dot_general(key, query, NT, preferred_element_type=F32)
    if bias is not None:
        scores = scores + bias
    top = jnp.max(scores, axis=0, keepdims=True)
    weight = jnp.exp2((scores - top) * SCALE2)
    total = jnp.sum(weight, axis=0, keepdims=True)
    out = jnp.dot(value_t, weight.astype(BF16), preferred_element_type=F32)
    return out / total, top * SCALE2 + jnp.log2(total)


def merged(out_a, lse_a, out_b, lse_b):
    top = jnp.maximum(lse_a, lse_b)
    weight_a = jnp.exp2(lse_a - top)
    weight_b = jnp.exp2(lse_b - top)
    total = weight_a + weight_b
    return out_a * (weight_a / total) + out_b * (weight_b / total), top + jnp.log2(total)


class Flow:
    def __init__(self, sel, q_in, k_in, v_in, out, scratch):
        (
            self.q_own, self.q_one, self.q_two, self.v_t, self.o_own, self.l_own, self.o_snd2, self.l_snd2,
            self.o_got2, self.l_got2, self.o_snd1, self.l_snd1, self.o_got1, self.l_got1,
            self.bias_own, self.bias_two, self.send_sem, self.recv_sem,
        ) = scratch
        self.sel, self.q_in, self.k_in, self.v_in, self.out = sel, q_in, k_in, v_in, out
        self.chunks, self.rows, self.width = self.q_own.shape
        self.per_chunk = self.width // HEAD
        self.lse_step = 8 // self.per_chunk
        self.shard = lax.axis_index(SEQ)
        count = lax.axis_size(SEQ)
        self.right = lax.rem(self.shard + 1, count)
        self.left = lax.rem(self.shard + count - 1, count)

    def copy(self, which, c, src, dst, target):
        return pltpu.make_async_remote_copy(
            src_ref=src.at[c], dst_ref=dst.at[c],
            send_sem=self.send_sem.at[which, c], recv_sem=self.recv_sem.at[which, c],
            device_id={SEQ: target}, device_id_type=MESH,
        )

    def hop_one(self, c):
        return self.copy(0, c, self.q_own, self.q_one, self.left)

    def hop_two(self, c):
        return self.copy(1, c, self.q_one, self.q_two, self.left)

    def back_two(self, c):
        return (
            self.copy(2, c, self.o_snd2, self.o_got2, self.right),
            self.copy(3, c, self.l_snd2, self.l_got2, self.right),
        )

    def back_one(self, c):
        return (
            self.copy(4, c, self.o_snd1, self.o_got1, self.right),
            self.copy(5, c, self.l_snd1, self.l_got1, self.right),
        )

    def begin(self, ahead, others=()):
        barrier = pltpu.get_barrier_semaphore()
        greeted = (self.left, self.right, *others)
        for neighbour in greeted:
            pl.semaphore_signal(barrier, inc=1, device_id={SEQ: neighbour}, device_id_type=MESH)
        picks = self.rows // BLK
        for a in range(picks):
            block = self.q_in[self.sel[a]]
            for c in range(self.chunks):
                self.q_own[c, a * BLK : (a + 1) * BLK, :] = block[:, c * self.width : (c + 1) * self.width]
        pl.semaphore_wait(barrier, len(greeted))
        for c in range(ahead):
            self.hop_one(c).start()
        self.ahead = ahead
        lane = lax.broadcasted_iota(jnp.int32, (1, self.rows), 1)
        key_at = lax.broadcasted_iota(jnp.int32, self.bias_own.shape, 0)
        for base, ref in ((0, self.bias_own), (2 * picks, self.bias_two)):
            place = lane
            for a in range(picks):
                place = jnp.where(lane // BLK == a, (lane - a * BLK) + self.sel[base + a] * BLK, place)
            seen = (key_at <= place) if base == 0 else (key_at > place)
            ref[...] = jnp.where(seen, 0.0, LOW)

    def cols(self, c, h):
        return pl.ds(pl.multiple_of(c * self.width + h * HEAD, HEAD), HEAD)

    def lse_at(self, h):
        return slice(h * self.lse_step, (h + 1) * self.lse_step)

    def spread(self, row):
        return jnp.broadcast_to(row, (self.lse_step, self.rows))

    def head(self, h):
        return slice(h * HEAD, (h + 1) * HEAD)

    def pump(self, c):
        self.hop_one(c).wait_recv()
        self.hop_two(c).start()

        @pl.when(c + self.ahead < self.chunks)
        def _():
            self.hop_one(c + self.ahead).start()

    def own(self, c):
        for h in range(self.per_chunk):
            cols = self.cols(c, h)
            value_t = self.v_in[:, cols].T
            self.v_t[cols, :] = value_t
            part, lse = window_part(
                self.q_own[c, :, self.head(h)], self.k_in[:, cols], value_t, self.bias_own[...]
            )
            self.o_own[c, self.head(h), :] = part
            self.l_own[c, self.lse_at(h), :] = self.spread(lse)

    def two(self, c):
        self.hop_two(c).wait_recv()
        for h in range(self.per_chunk):
            cols = self.cols(c, h)
            part, lse = window_part(
                self.q_two[c, :, self.head(h)], self.k_in[:, cols], self.v_t[cols, :], self.bias_two[...]
            )
            self.o_snd2[c, self.head(h), :] = part.astype(BF16)
            self.l_snd2[c, self.lse_at(h), :] = self.spread(lse)
        for each in self.back_two(c):
            each.start()

    def incoming(self, got, h, c):
        first = h * self.lse_step
        return jnp.where(self.shard == 0, LOW, got[c, first : first + 1, :])

    def one(self, c):
        parts = []
        for h in range(self.per_chunk):
            cols = self.cols(c, h)
            parts.append(
                window_part(self.q_one[c, :, self.head(h)], self.k_in[:, cols], self.v_t[cols, :], None)
            )
        for each in self.back_two(c):
            each.wait_recv()
        for h in range(self.per_chunk):
            part, lse = merged(
                *parts[h], self.o_got2[c, self.head(h), :].astype(F32), self.incoming(self.l_got2, h, c)
            )
            self.o_snd1[c, self.head(h), :] = part.astype(BF16)
            self.l_snd1[c, self.lse_at(h), :] = self.spread(lse)
        for each in self.back_one(c):
            each.start()

    def final(self, c):
        for each in self.back_one(c):
            each.wait_recv()
        for h in range(self.per_chunk):
            first = h * self.lse_step
            part, _ = merged(
                self.o_own[c, self.head(h), :], self.l_own[c, first : first + 1, :],
                self.o_got1[c, self.head(h), :].astype(F32), self.incoming(self.l_got1, h, c),
            )
            self.store(c, h, part.T.astype(BF16))

    def store(self, c, h, value):
        self.out[:, self.cols(c, h)] = value

    def step(self, t):
        @pl.when(t < self.chunks)
        def _():
            self.pump(t)
            self.own(t)

        @pl.when((t >= 1) & (t <= self.chunks))
        def _():
            self.two(t - 1)

        @pl.when((t >= 2) & (t <= self.chunks + 1))
        def _():
            self.one(t - 2)

        @pl.when((t >= 3) & (t <= self.chunks + 2))
        def _():
            self.final(t - 3)

    def drain(self):
        def body(c, carry):
            self.hop_one(c).wait_send()
            self.hop_two(c).wait_send()
            for each in self.back_two(c) + self.back_one(c):
                each.wait_send()
            return carry

        lax.fori_loop(0, self.chunks, body, 0)

    @staticmethod
    def scratch(rows, tok, full, per_chunk):
        width = per_chunk * HEAD
        chunks = full // width
        queries = pltpu.VMEM((chunks, rows, width), BF16)
        outs = pltpu.VMEM((chunks, width, rows), BF16)
        lses = pltpu.VMEM((chunks, 8, rows), F32)
        return [
            queries, queries, queries, pltpu.VMEM((full, tok), BF16), pltpu.VMEM((chunks, width, rows), F32), lses,
            outs, lses, outs, lses, outs, lses, outs, lses,
            pltpu.VMEM((tok, rows), F32), pltpu.VMEM((tok, rows), F32),
            pltpu.SemaphoreType.DMA((6, chunks)), pltpu.SemaphoreType.DMA((6, chunks)),
        ]


SIDE = 4


class Spread:
    OFFSETS = (0, 1, SIDE - 1, 2)
    MESSAGES = 20

    def __init__(self, got, send_sem, recv_sem):
        self.got, self.send_sem, self.recv_sem = got, send_sem, recv_sem
        shard = lax.axis_index(SEQ)
        row, col = shard // SIDE, lax.rem(shard, SIDE)
        self.here = ((col, row), (row, col))

    @staticmethod
    def turn(at, by):
        return lax.rem(at + by + SIDE, SIDE)

    @staticmethod
    def slot(kind, place):
        a, b = place
        return b * SIDE + a if kind == 0 else a * SIDE + b

    def neighbours(self):
        a, b = self.here[0]
        return [self.slot(0, (self.turn(a, by), b)) for by in (1, -1)] + [
            self.slot(0, (a, self.turn(b, by))) for by in (1, -1)
        ]

    def message(self, c, kind, which, place, half, target):
        slot = self.slot(kind, place)
        ref = self.got.at[c, kind, slot] if half is None else self.got.at[c, kind, slot, half]
        at = kind * self.MESSAGES + which
        return pltpu.make_async_remote_copy(
            src_ref=ref, dst_ref=ref, send_sem=self.send_sem.at[c, at], recv_sem=self.recv_sem.at[c, at],
            device_id={SEQ: self.slot(kind, target)}, device_id_type=MESH,
        )

    def first(self, c, kind, what):
        a, b = self.here[kind]
        up, down = (self.turn(a, 1), b), (self.turn(a, -1), b)
        return self.four(c, kind, 0, (a, b), up, down, (self.turn(a, 2), b), up, down, what)

    def second(self, c, kind, k, what):
        a, b = self.here[kind]
        origin = self.turn(a, self.OFFSETS[k])
        return self.four(
            c, kind, 4 + 4 * k, (origin, b), (origin, self.turn(b, 1)), (origin, self.turn(b, -1)),
            (origin, self.turn(b, 2)), (a, self.turn(b, 1)), (a, self.turn(b, -1)), what,
        )

    def four(self, c, kind, base, here, up, down, far, to_up, to_down, what):
        pairs = {
            "send": ((base, here, None, to_up), (base + 1, here, None, to_down)),
            "came": ((base, down, None, to_up), (base + 1, up, None, to_down)),
            "pass": ((base + 2, down, 0, to_up), (base + 3, up, 1, to_down)),
            "last": ((base + 2, far, 0, to_up), (base + 3, far, 1, to_down)),
        }[what]
        return [self.message(c, kind, *pair) for pair in pairs]

    def launch(self, c):
        for kind in range(2):
            for each in self.first(c, kind, "send"):
                each.start()

    def relay(self, c):
        for kind in range(2):
            for each in self.first(c, kind, "came"):
                each.wait_recv()
            for each in self.first(c, kind, "pass"):
                each.start()
            for k in range(3):
                for each in self.second(c, kind, k, "send"):
                    each.start()

    def relay_far(self, c):
        for kind in range(2):
            for each in self.first(c, kind, "last"):
                each.wait_recv()
            for each in self.second(c, kind, 3, "send"):
                each.start()

    def second_relay(self, c):
        for k in range(4):
            for kind in range(2):
                for each in self.second(c, kind, k, "came"):
                    each.wait_recv()
                for each in self.second(c, kind, k, "pass"):
                    each.start()

    def settle(self, c):
        for k in range(4):
            for kind in range(2):
                for each in self.second(c, kind, k, "last"):
                    each.wait_recv()

    def drain(self, c):
        for kind in range(2):
            for what in ("send", "pass"):
                for each in self.first(c, kind, what):
                    each.wait_send()
                for k in range(4):
                    for each in self.second(c, kind, k, what):
                        each.wait_send()


def front_kernel(
    kept_shard, kept_at, sel, q_in, k_in, v_in, three, out, rows_out, projected, scale_out,
    weights, got, held, staged, staged_sem, total, squares, spread_send, spread_recv, *scratch,
):
    kept = kept_shard.shape[0]
    flow = Flow(sel, q_in, k_in, v_in, out, scratch)
    spread = Spread(got, spread_send, spread_recv)
    chunks, width = flow.chunks, flow.width
    total_rows, local = projected.shape
    full = k_in.shape[1]
    block = 512

    def store(c, h, value):
        out[:, flow.cols(c, h)] = value
        for a in range(flow.rows // BLK):
            got[c, h, flow.shard, a] = value[a * BLK : (a + 1) * BLK, :]

    flow.store = store
    flow.begin(3, spread.neighbours())
    for which in range(3):
        weights[:, which * HEAD : (which + 1) * HEAD] = three[which]
    total[...] = jnp.zeros_like(total)
    squares[...] = jnp.zeros_like(squares)

    def staged_copy(c):
        which = lax.rem(c, 2)
        return pltpu.make_async_copy(staged.at[which], rows_out.at[c], staged_sem.at[which])

    def project_chunk(c):
        which = lax.rem(c, 2)

        @pl.when(c >= 2)
        def _():
            staged_copy(c - 2).wait()

        def hold(i, carry):
            for h in range(flow.per_chunk):
                held[i, :, :, flow.head(h)] = got[c, h, i]
            return carry

        lax.fori_loop(0, SIDE * SIDE, hold, 0)

        def pick(j, carry):
            at = pl.ds(pl.multiple_of(j * BLK, BLK), BLK)
            staged[which, at, :] = held[kept_shard[j], kept_at[j]]
            return carry

        lax.fori_loop(0, kept, pick, 0)
        staged_copy(c).start()
        weight = weights[pl.ds(pl.multiple_of(c * width, width), width), :]

        def multiply(r, carry):
            at = pl.ds(pl.multiple_of(r * block, block), block)
            rows = staged[which, at, :]
            total[at, :] += jnp.dot(rows, weight, preferred_element_type=F32)
            wide = rows.astype(F32)
            square = wide * wide
            squares[at, :] += sum(square[:, h * HEAD : (h + 1) * HEAD] for h in range(flow.per_chunk))
            return carry

        lax.fori_loop(0, total_rows // block, multiply, 0)

    def step(t, carry):
        flow.step(t)

        def stage(late, call):
            @pl.when((t >= late) & (t < chunks + late))
            def _():
                call(t - late)

        stage(3, spread.launch)
        stage(4, spread.relay)
        stage(5, spread.relay_far)
        stage(6, spread.second_relay)

        @pl.when(t >= 7)
        def _():
            spread.settle(t - 7)
            project_chunk(t - 7)

        return carry

    lax.fori_loop(0, chunks + 7, step, 0)

    def finish(r, carry):
        at = pl.ds(pl.multiple_of(r * block, block), block)
        square = squares[at, :]
        inv = lax.rsqrt(jnp.sum(square, axis=1, keepdims=True) * (1.0 / full) + 1e-06)
        projected[at, :] = (total[at, :] * inv).astype(BF16)
        scale_out[:, at] = lax.rsqrt(jnp.sum(square.T, axis=0, keepdims=True) * (1.0 / full) + 1e-06)
        return carry

    lax.fori_loop(0, total_rows // block, finish, 0)

    def drain(c, carry):
        spread.drain(c)
        return carry

    lax.fori_loop(0, chunks, drain, 0)
    for c in (chunks - 2, chunks - 1):
        staged_copy(c).wait()
    flow.drain()


def front(kept_shard, kept_at, sel, query, key, value, weights, per_chunk, ident):
    tok, full = key.shape
    local = 3 * HEAD
    rows = sel.shape[0] // 3 * BLK
    total_rows = kept_shard.shape[0] * BLK
    width = per_chunk * HEAD
    chunks = full // width
    vmem = pl.BlockSpec(memory_space=pltpu.VMEM)
    smem = pl.BlockSpec(memory_space=pltpu.SMEM)
    return pl.pallas_call(
        front_kernel,
        out_shape=(
            jax.ShapeDtypeStruct((rows, full), BF16),
            jax.ShapeDtypeStruct((chunks, total_rows, width), BF16),
            jax.ShapeDtypeStruct((total_rows, local), BF16),
            jax.ShapeDtypeStruct((1, total_rows), F32),
        ),
        in_specs=[smem, smem, smem, vmem, vmem, vmem, vmem],
        out_specs=[vmem, pl.BlockSpec(memory_space=pl.ANY), vmem, vmem],
        scratch_shapes=[
            pltpu.VMEM((full, local), BF16),
            pltpu.VMEM((chunks, 2, SIDE * SIDE, rows // BLK, BLK, HEAD), BF16),
            pltpu.VMEM((SIDE * SIDE, rows // BLK, BLK, width), BF16),
            pltpu.VMEM((2, total_rows, width), BF16),
            pltpu.SemaphoreType.DMA((2,)),
            pltpu.VMEM((total_rows, local), F32),
            pltpu.VMEM((total_rows, HEAD), F32),
            pltpu.SemaphoreType.DMA((chunks, 2 * Spread.MESSAGES)),
            pltpu.SemaphoreType.DMA((chunks, 2 * Spread.MESSAGES)),
            *Flow.scratch(rows, tok, full, per_chunk),
        ],
        compiler_params=pltpu.CompilerParams(
            collective_id=ident, has_side_effects=True, vmem_limit_bytes=VMEM_LIMIT
        ),
        name="front",
    )(kept_shard, kept_at, sel, query, key, value, weights)


QB = 256
KB = 512


def causal_kernel(
    dest, sel, qkv, scale, cot, gathered, q_in, k_in, v_in, out, d_all, grads, rest,
    rows_in, rows_sem, d_all_t, v_t, k_t, do_own, do_t, p_buf, dk_acc, dv_acc, dq_t, *scratch,
):
    kept = dest.shape[0]
    total_rows = qkv.shape[0]
    blocks = total_rows // QB
    rows_copy = pltpu.make_async_copy(gathered, rows_in, rows_sem)
    rows_copy.start()
    flow = Flow(sel, q_in, k_in, v_in, rest, scratch)
    flow.begin(3)

    for j in range(kept):
        do_own[j * BLK : (j + 1) * BLK, :] = cot[dest[j]]

    def prepare(c, carry):
        at = pl.ds(pl.multiple_of(c * QB, QB), QB)
        k_t[:, at] = qkv[at, HEAD : 2 * HEAD].T
        v_t[:, at] = qkv[at, 2 * HEAD : 3 * HEAD].T
        do_t[:, at] = do_own[at, :].T
        return carry

    lax.fori_loop(0, blocks, prepare, 0)
    dk_acc[...] = jnp.zeros_like(dk_acc)
    dv_acc[...] = jnp.zeros_like(dv_acc)

    def query_block(i):
        rows = pl.ds(pl.multiple_of(i * QB, QB), QB)
        chunks = (i * QB + QB + KB - 1) // KB
        q_i = qkv[rows, :HEAD]
        do_i = do_own[rows, :]

        def scores_of(c, masked):
            keys = pl.ds(pl.multiple_of(c * KB, KB), KB)
            scores = lax.dot_general(qkv[keys, HEAD : 2 * HEAD], q_i, NT, preferred_element_type=F32)
            if masked:
                key_at = lax.broadcasted_iota(jnp.int32, (KB, QB), 0)
                row_at = lax.broadcasted_iota(jnp.int32, (KB, QB), 1)
                scores = jnp.where(key_at - row_at <= i * QB - (chunks - 1) * KB, scores, LOW)
            p_buf[keys, :] = scores
            return jnp.max(scores, axis=0, keepdims=True)

        top = lax.fori_loop(
            0, chunks - 1, lambda c, m: jnp.maximum(m, scores_of(c, False)), scores_of(chunks - 1, True)
        )

        def weigh(c, carry):
            total, acc = carry
            keys = pl.ds(pl.multiple_of(c * KB, KB), KB)
            weight = jnp.exp2((p_buf[keys, :] - top) * SCALE2)
            p_buf[keys, :] = weight
            total = total + jnp.sum(weight, axis=0, keepdims=True)
            acc = acc + jnp.dot(v_t[:, keys], weight.astype(BF16), preferred_element_type=F32)
            return total, acc

        total, acc = lax.fori_loop(
            0, chunks, weigh, (jnp.zeros((1, QB), F32), jnp.zeros((HEAD, QB), F32))
        )
        inv = 1.0 / total
        o_t = acc * inv
        delta = jnp.sum(o_t * do_t[:, rows].astype(F32), axis=0, keepdims=True)
        out[rows, :] = o_t.T.astype(BF16)

        def back(c, acc):
            keys = pl.ds(pl.multiple_of(c * KB, KB), KB)
            soft = p_buf[keys, :] * inv
            dv_acc[keys, :] += jnp.dot(soft.astype(BF16), do_i, preferred_element_type=F32)
            d_probs = lax.dot_general(qkv[keys, 2 * HEAD :], do_i, NT, preferred_element_type=F32)
            d_scores = (soft * (d_probs - delta) * SCALE).astype(BF16)
            dk_acc[keys, :] += jnp.dot(d_scores, q_i, preferred_element_type=F32)
            return acc + jnp.dot(k_t[:, keys], d_scores, preferred_element_type=F32)

        dq_t[:, rows] = lax.fori_loop(0, chunks, back, jnp.zeros((HEAD, QB), F32))

    def finish(c, carry):
        at = pl.ds(pl.multiple_of(c * QB, QB), QB)
        d_q = dq_t[:, at]
        d_all_t[:HEAD, at] = (d_q * scale[:, at]).astype(BF16)
        d_all[at, :HEAD] = d_q.T.astype(BF16)
        for which, acc in ((1, dk_acc), (2, dv_acc)):
            value = acc[at, :]
            d_all[at, which * HEAD : (which + 1) * HEAD] = value.astype(BF16)
            d_all_t[which * HEAD : (which + 1) * HEAD, at] = (value.T * scale[:, at]).astype(BF16)
        return carry

    def weight_block(g, carry):
        at = pl.ds(pl.multiple_of(g * QB, QB), QB)
        value = jnp.dot(d_all_t[...], rows_in[g], preferred_element_type=F32)
        for which in range(3):
            grads[which, at, :] = value[which * HEAD : (which + 1) * HEAD, :].T.astype(BF16)
        return carry

    col_blocks = rows_in.shape[0]
    share = (col_blocks + 2) // 3

    def step(t, carry):
        flow.step(t)

        @pl.when(t < blocks)
        def _():
            query_block(blocks - 1 - t)

        @pl.when(t == blocks)
        def _():
            lax.fori_loop(0, blocks, finish, 0)
            rows_copy.wait()

        @pl.when(t >= blocks)
        def _():
            low = (t - blocks) * share
            lax.fori_loop(low, jnp.minimum(low + share, col_blocks), weight_block, 0)

        return carry

    lax.fori_loop(0, blocks + 3, step, 0)
    flow.drain()


def causal(dest, sel, qkv, scale, cot, gathered, query, key, value, per_chunk, ident):
    total_rows, local = qkv.shape
    tok, full = key.shape
    rows = sel.shape[0] // 3 * BLK
    vmem = pl.BlockSpec(memory_space=pltpu.VMEM)
    smem = pl.BlockSpec(memory_space=pltpu.SMEM)
    return pl.pallas_call(
        causal_kernel,
        out_shape=(
            jax.ShapeDtypeStruct((total_rows, HEAD), BF16),
            jax.ShapeDtypeStruct((total_rows, local), BF16),
            jax.ShapeDtypeStruct((3, full, HEAD), BF16),
            jax.ShapeDtypeStruct((rows, full), BF16),
        ),
        in_specs=[smem, smem, vmem, vmem, vmem, pl.BlockSpec(memory_space=pl.ANY), vmem, vmem, vmem],
        out_specs=[vmem, vmem, vmem, vmem],
        scratch_shapes=[
            pltpu.VMEM(gathered.shape, BF16),
            pltpu.SemaphoreType.DMA,
            pltpu.VMEM((local, total_rows), BF16),
            pltpu.VMEM((HEAD, total_rows), BF16),
            pltpu.VMEM((HEAD, total_rows), BF16),
            pltpu.VMEM((total_rows, HEAD), BF16),
            pltpu.VMEM((HEAD, total_rows), BF16),
            pltpu.VMEM((total_rows, QB), F32),
            pltpu.VMEM((total_rows, HEAD), F32),
            pltpu.VMEM((total_rows, HEAD), F32),
            pltpu.VMEM((HEAD, total_rows), F32),
            *Flow.scratch(rows, tok, full, per_chunk),
        ],
        compiler_params=pltpu.CompilerParams(
            collective_id=ident, has_side_effects=True, vmem_limit_bytes=VMEM_LIMIT
        ),
        cost_estimate=pl.CostEstimate(
            flops=20 * 10**9, bytes_accessed=32 * 1024 * 1024, transcendentals=0
        ),
        name="causal",
    )(dest, sel, qkv, scale, cot, gathered, query, key, value)


class Reduce:
    def __init__(self, value, pair_got, own, snd, got1, got2, whole, send_sem, recv_sem):
        self.value, self.pair_got, self.own, self.snd = value, pair_got, own, snd
        self.got1, self.got2, self.whole = got1, got2, whole
        self.send_sem, self.recv_sem = send_sem, recv_sem
        at = lax.axis_index("dp")
        self.y, self.core = at // 2, lax.rem(at, 2)
        self.partner = self.y * 2 + 1 - self.core
        self.next = [self.turn(by) * 2 + self.core for by in (1, -1)]
        middle = value.shape[3] // 2
        self.halves = (slice(0, middle), slice(middle, 2 * middle))

    def turn(self, by):
        return lax.rem(self.y + by + SIDE, SIDE)

    def copy(self, which, src, dst, target):
        return pltpu.make_async_remote_copy(
            src_ref=src, dst_ref=dst, send_sem=self.send_sem.at[which], recv_sem=self.recv_sem.at[which],
            device_id={"dp": target}, device_id_type=MESH,
        )

    def pair(self):
        return self.copy(0, self.value.at[:, 1 - self.core], self.pair_got, self.partner)

    def ring1(self, d):
        return self.copy(1 + d, self.snd.at[d, 0, :, self.halves[0]], self.got1.at[d], self.next[d])

    def ring2(self, d):
        return self.copy(3 + d, self.snd.at[d, 1], self.got2.at[d], self.next[d])

    def quarter(self, by, half=None):
        ref = self.whole.at[:, self.core, self.turn(by)]
        return ref if half is None else self.whole.at[:, self.core, self.turn(by), self.halves[half]]

    def spread1(self, d, by):
        return self.copy(5 + d, self.quarter(by), self.quarter(by), self.next[d])

    def spread2(self, d, by):
        return self.copy(7 + d, self.quarter(by, d), self.quarter(by, d), self.next[d])

    def back(self, core):
        return self.copy(9, self.whole.at[:, core], self.whole.at[:, core], self.partner)

    def stage1(self):
        self.pair().wait_recv()

        def add(q, carry):
            self.own[q] = self.value[:, self.core, q].astype(F32) + self.pair_got[:, q].astype(F32)
            return carry

        lax.fori_loop(0, SIDE, add, 0)
        for d in range(2):
            self.snd[d, 0, :, self.halves[0]] = self.own[self.turn(2), :, self.halves[d]].astype(BF16)
            self.ring1(d).start()

    def stage2(self):
        for d in range(2):
            self.ring1(d).wait_recv()
            near = self.turn(1 - 2 * d)
            self.snd[d, 1, :, self.halves[1 - d]] = self.own[near, :, self.halves[1 - d]].astype(BF16)
            self.snd[d, 1, :, self.halves[d]] = (
                self.own[near, :, self.halves[d]] + self.got1[d].astype(F32)
            ).astype(BF16)
            self.ring2(d).start()

    def stage3(self):
        for d in range(2):
            self.ring2(d).wait_recv()
        total = self.own[self.y] + self.got2[0].astype(F32) + self.got2[1].astype(F32)
        self.whole[:, self.core, self.y] = total.astype(BF16)
        for d in range(2):
            self.spread1(d, 0).start()

    def stage4(self):
        for d in range(2):
            self.spread1(d, 2 * d - 1).wait_recv()
            self.spread2(d, 2 * d - 1).start()

    def stage5(self):
        for d in range(2):
            self.spread2(d, 2).wait_recv()
        self.back(self.core).start()

    def stage6(self, out):
        self.back(1 - self.core).wait_recv()
        out[...] = self.whole[...]
        self.pair().wait_send()
        for d in range(2):
            self.ring1(d).wait_send()
            self.ring2(d).wait_send()
            self.spread1(d, 0).wait_send()
            self.spread2(d, 2 * d - 1).wait_send()
        self.back(self.core).wait_send()

    @staticmethod
    def scratch(shape):
        three, _, quarters, rows, width = shape
        return [
            pltpu.VMEM((three, quarters, rows, width), BF16),
            pltpu.VMEM((quarters, three, rows, width), F32),
            pltpu.VMEM((2, 2, three, rows, width), BF16),
            pltpu.VMEM((2, three, rows // 2, width), BF16),
            pltpu.VMEM((2, three, rows, width), BF16),
            pltpu.VMEM(shape, BF16),
            pltpu.SemaphoreType.DMA((10,)),
            pltpu.SemaphoreType.DMA((10,)),
        ]


def scatter_kernel(
    slot_at, d_all, three, value, out, summed, weights, terms, got1, snd2, got2, sums, last1, lasts2, last2,
    send1, recv1, send2, recv2, send3, recv3, send4, recv4, *reduce_scratch,
):
    shard = lax.axis_index(SEQ)
    row, col = shard // SIDE, lax.rem(shard, SIDE)
    wide = out.shape[1] // 2
    part = wide // 2
    place = ((row, col), (col, row))
    halves = (slice(0, part), slice(part, wide))

    def turn(at, by):
        return lax.rem(at + by + SIDE, SIDE)

    def slot(h, a, b):
        return a * SIDE + b if h == 0 else b * SIDE + a

    barrier = pltpu.get_barrier_semaphore()
    for by in (1, -1):
        for h in range(2):
            a, b = place[h]
            pl.semaphore_signal(
                barrier, inc=1, device_id={SEQ: slot(h, turn(a, by), b)}, device_id_type=MESH
            )
    reduce = Reduce(value, *reduce_scratch)
    for target in (reduce.partner, *reduce.next):
        pl.semaphore_signal(barrier, inc=1, device_id={"dp": target}, device_id_type=MESH)
    for which in range(3):
        weights[:, which * HEAD : (which + 1) * HEAD] = three[which]

    def group(h, a):
        slots = [jnp.where(h == 0, a * SIDE + s, s * SIDE + a) for s in range(SIDE)]
        rows = jnp.concatenate([d_all[slot_at[one]] for one in slots], axis=0)
        cols = pl.ds(pl.multiple_of(h * wide, wide), wide)
        value = lax.dot_general(rows, weights[cols, :], NT, preferred_element_type=F32).astype(BF16)
        for s in range(SIDE):
            terms[h, a, s] = value[s * BLK : (s + 1) * BLK, :]

    def first_send(h, d, s):
        a, b = place[h]
        return pltpu.make_async_remote_copy(
            src_ref=terms.at[h, turn(a, 2), s, :, halves[d]], dst_ref=got1.at[h, d, s],
            send_sem=send1.at[h, d, s], recv_sem=recv1.at[h, d, s],
            device_id={SEQ: slot(h, turn(a, 1 - 2 * d), b)}, device_id_type=MESH,
        )

    def second_send(h, d, s):
        a, b = place[h]
        return pltpu.make_async_remote_copy(
            src_ref=snd2.at[h, d, s], dst_ref=got2.at[h, d, s],
            send_sem=send2.at[h, d, s], recv_sem=recv2.at[h, d, s],
            device_id={SEQ: slot(h, turn(a, 1 - 2 * d), b)}, device_id_type=MESH,
        )

    def third_send(h, d):
        a, b = place[h]
        return pltpu.make_async_remote_copy(
            src_ref=sums.at[h, turn(b, 2), :, halves[d]], dst_ref=last1.at[h, d],
            send_sem=send3.at[h, d], recv_sem=recv3.at[h, d],
            device_id={SEQ: slot(h, a, turn(b, 1 - 2 * d))}, device_id_type=MESH,
        )

    def fourth_send(h, d):
        a, b = place[h]
        return pltpu.make_async_remote_copy(
            src_ref=lasts2.at[h, d], dst_ref=last2.at[h, d],
            send_sem=send4.at[h, d], recv_sem=recv4.at[h, d],
            device_id={SEQ: slot(h, a, turn(b, 1 - 2 * d))}, device_id_type=MESH,
        )

    def group_far(h, carry):
        group(h, turn(jnp.where(h == 0, row, col), 2))
        return carry

    def group_rest(g, carry):
        h, which = lax.rem(g, 2), g // 2
        by = jnp.where(which == 0, 1, jnp.where(which == 1, SIDE - 1, 0))
        group(h, turn(jnp.where(h == 0, row, col), by))
        return carry

    lax.fori_loop(0, 2, group_far, 0)
    pl.semaphore_wait(barrier, 7)
    reduce.pair().start()
    for k in (2, 1, 3, 0):
        for h in range(2):
            s = turn(place[h][1], k)
            for d in range(2):
                first_send(h, d, s).start()
    lax.fori_loop(0, 6, group_rest, 0)
    reduce.stage1()
    for k in (2, 1, 3, 0):
        for h in range(2):
            a, b = place[h]
            s = turn(b, k)
            for d in range(2):
                first_send(h, d, s).wait_recv()
                near = turn(a, 1 - 2 * d)
                other = halves[1 - d]
                snd2[h, d, s, :, other] = terms[h, near, s, :, other]
                snd2[h, d, s, :, halves[d]] = (
                    terms[h, near, s, :, halves[d]].astype(F32) + got1[h, d, s].astype(F32)
                ).astype(BF16)
                second_send(h, d, s).start()
    reduce.stage2()
    for k in (2, 1, 3, 0):
        for h in range(2):
            a, b = place[h]
            s = turn(b, k)
            for d in range(2):
                second_send(h, d, s).wait_recv()
            total = (
                terms[h, a, s].astype(F32) + got2[h, 0, s].astype(F32) + got2[h, 1, s].astype(F32)
            )
            if k != 0:
                sums[h, s] = total.astype(BF16)
            if k == 2:
                for d in range(2):
                    third_send(h, d).start()
            elif k != 0:
                d = 0 if k == 1 else 1
                third_send(h, d).wait_recv()
                other = halves[1 - d]
                lasts2[h, d, :, other] = sums[h, s, :, other]
                lasts2[h, d, :, halves[d]] = (total[:, halves[d]] + last1[h, d].astype(F32)).astype(BF16)
                fourth_send(h, d).start()
            else:
                for d in range(2):
                    fourth_send(h, d).wait_recv()
                out[:, h * wide : (h + 1) * wide] = (
                    total + last2[h, 0].astype(F32) + last2[h, 1].astype(F32)
                ).astype(BF16)
        if k == 2:
            reduce.stage3()
        elif k == 1:
            reduce.stage4()
        elif k == 3:
            reduce.stage5()
    reduce.stage6(summed)
    for h in range(2):
        for d in range(2):
            for s in range(SIDE):
                first_send(h, d, s).wait_send()
                second_send(h, d, s).wait_send()
            third_send(h, d).wait_send()
            fourth_send(h, d).wait_send()


def scatter_terms(slot_at, d_all, three, value, ident):
    blocks, _, local = d_all.shape
    full = three.shape[1]
    wide = full // 2
    part = wide // 2
    vmem = pl.BlockSpec(memory_space=pltpu.VMEM)
    four = pltpu.SemaphoreType.DMA((2, 2, SIDE))
    two = pltpu.SemaphoreType.DMA((2, 2))
    return pl.pallas_call(
        scatter_kernel,
        out_shape=(jax.ShapeDtypeStruct((BLK, full), BF16), jax.ShapeDtypeStruct(value.shape, BF16)),
        in_specs=[pl.BlockSpec(memory_space=pltpu.SMEM), vmem, vmem, vmem],
        out_specs=[vmem, vmem],
        scratch_shapes=[
            pltpu.VMEM((full, local), BF16),
            pltpu.VMEM((2, SIDE, SIDE, BLK, wide), BF16),
            pltpu.VMEM((2, 2, SIDE, BLK, part), BF16),
            pltpu.VMEM((2, 2, SIDE, BLK, wide), BF16),
            pltpu.VMEM((2, 2, SIDE, BLK, wide), BF16),
            pltpu.VMEM((2, SIDE, BLK, wide), BF16),
            pltpu.VMEM((2, 2, BLK, part), BF16),
            pltpu.VMEM((2, 2, BLK, wide), BF16),
            pltpu.VMEM((2, 2, BLK, wide), BF16),
            four, four, four, four, two, two, two, two,
            *Reduce.scratch(value.shape),
        ],
        compiler_params=pltpu.CompilerParams(
            collective_id=ident, has_side_effects=True, vmem_limit_bytes=VMEM_LIMIT
        ),
        cost_estimate=pl.CostEstimate(
            flops=2 * blocks * BLK * local * full, bytes_accessed=100 * 1024 * 1024, transcendentals=0
        ),
        name="scatter_terms",
    )(slot_at, d_all, three, value)


def assemble_kernel(table, head, rest, sorted_out, out, causal_out):
    kept = sorted_out.shape[0] // BLK
    first = table[kept + 3 * pl.program_id(0)] == 1

    @pl.when(pl.program_id(0) == 0)
    def _():
        for j in range(kept):
            causal_out[pl.ds(pl.multiple_of(table[j] * BLK, BLK), BLK), :] = sorted_out[j * BLK : (j + 1) * BLK, :]

    @pl.when(first)
    def _():
        out[...] = head[...]

    @pl.when(jnp.logical_not(first))
    def _():
        out[...] = rest[...]


def assemble(table, head, rest, sorted_out):
    rows, full = head.shape
    kept = sorted_out.shape[0] // BLK
    whole = pl.BlockSpec(sorted_out.shape, lambda g, t: (0, 0))
    return pl.pallas_call(
        assemble_kernel,
        out_shape=(
            jax.ShapeDtypeStruct((2 * rows, full), BF16),
            jax.ShapeDtypeStruct(sorted_out.shape, BF16),
        ),
        grid_spec=pltpu.PrefetchScalarGridSpec(
            num_scalar_prefetch=1,
            grid=(2 * rows // BLK,),
            in_specs=[
                pl.BlockSpec((BLK, full), lambda g, t: (t[kept + 3 * g + 1], 0)),
                pl.BlockSpec((BLK, full), lambda g, t: (t[kept + 3 * g + 2], 0)),
                whole,
            ],
            out_specs=[pl.BlockSpec((BLK, full), lambda g, t: (g, 0)), whole],
        ),
        name="assemble",
    )(table, head, rest, sorted_out)


def shards(query_input, key_input, value_input, keep_blocks, dest_slots, proj_weights, cotangent):
    tok, full = query_input.shape[1:]
    per_shard = tok // BLK
    shard = lax.axis_index(SEQ)
    count = lax.axis_size(SEQ)
    half_blocks = per_shard // 2
    query = query_input.reshape(per_shard, BLK, full)
    key = key_input[0]
    value = value_input[0]
    keep = keep_blocks[0]
    dest = dest_slots[0]

    kept = jnp.any(
        keep[None, None, :] == jnp.arange(count * per_shard).reshape(count, per_shard)[:, :, None], axis=2
    )
    order_key = jnp.where(kept, 0, per_shard) + jnp.arange(per_shard)[None, :]
    rank = jnp.sum(order_key[:, None, :] < order_key[:, :, None], axis=2).astype(jnp.int32)
    order = jnp.sum(
        jnp.where(
            rank[:, None, :] == jnp.arange(per_shard)[None, :, None], jnp.arange(per_shard)[None, None, :], 0
        ),
        axis=2,
    ).astype(jnp.int32)
    wrapped = jnp.concatenate([order, order[:2]], axis=0)
    near = lax.dynamic_slice_in_dim(wrapped, shard, 3, 0)
    sel_first = near[:, :half_blocks].reshape(-1)
    sel_rest = near[:, half_blocks:].reshape(-1)
    own_rank = lax.dynamic_slice_in_dim(rank, shard, 1, 0)[0]
    in_first = (own_rank < half_blocks).astype(jnp.int32)
    at = own_rank % half_blocks
    table = jnp.stack([in_first, at * in_first, at * (1 - in_first)], axis=1).reshape(-1)
    keep_shard = keep // per_shard
    before = jnp.sum((keep_shard[None, :] == keep_shard[:, None]) & (keep[None, :] < keep[:, None]), axis=1)

    slot_at = jnp.sum(
        jnp.where(dest[None, :] == jnp.arange(dest.shape[0])[:, None], jnp.arange(dest.shape[0])[None, :], 0),
        axis=1,
    ).astype(jnp.int32)

    first, gathered, qkv, scale = front(
        keep_shard.astype(jnp.int32), before.astype(jnp.int32), sel_first, query, key, value, proj_weights, 2, 0
    )
    sorted_out, d_all, local_grads, rest = causal(
        dest, sel_rest, qkv, scale, cotangent.reshape(dest.shape[0], BLK, -1), gathered, query, key, value, 2, 1
    )
    window_out, causal_out = assemble(jnp.concatenate([dest, table]), first, rest, sorted_out)
    row_grad, grads = scatter_terms(
        slot_at, d_all.reshape(dest.shape[0], BLK, -1), proj_weights,
        local_grads.reshape(3, 2, SIDE, full // 2 // SIDE, HEAD), 2,
    )
    grads = grads.reshape(proj_weights.shape).astype(F32)
    return (window_out[None], causal_out[None], grads, row_grad[None])


def solution(mesh):
    return jax.shard_map(
        shards,
        mesh=mesh,
        in_specs=(
            P("dp", "seq", None),
            P("dp", "seq", None),
            P("dp", "seq", None),
            P("dp", None),
            P("dp", None),
            P(None, None, "seq"),
            P("dp", None, "seq"),
        ),
        out_specs=(
            P("dp", "seq", None),
            P("dp", None, "seq"),
            P(None, None, "seq"),
            P("dp", "seq", None),
        ),
        check_vma=False,
    )
```

```python
import functools

import jax
import jax.numpy as jnp
from jax import lax
from jax.experimental import pallas as pl
from jax.experimental.pallas import tpu as pltpu
from jax.sharding import PartitionSpec as P

HEAD = 128
BLK = 128
SEQ = "seq"
MESH = pl.DeviceIdType.MESH
SCALE = HEAD ** (-0.5)
LOG2E = 1.4426950408889634
SCALE2 = SCALE * LOG2E
LOW = -1e30
NT = (((1,), (1,)), ((), ()))
BF16 = jnp.bfloat16
F32 = jnp.float32
VMEM_LIMIT = 56 * 1024 * 1024


def window_part(query, key, value_t, bias):
    scores = lax.dot_general(key, query, NT, preferred_element_type=F32)
    if bias is not None:
        scores = scores + bias
    top = jnp.max(scores, axis=0, keepdims=True)
    weight = jnp.exp2((scores - top) * SCALE2)
    total = jnp.sum(weight, axis=0, keepdims=True)
    out = jnp.dot(value_t, weight.astype(BF16), preferred_element_type=F32)
    return out / total, top * SCALE2 + jnp.log2(total)


def merged(out_a, lse_a, out_b, lse_b):
    top = jnp.maximum(lse_a, lse_b)
    weight_a = jnp.exp2(lse_a - top)
    weight_b = jnp.exp2(lse_b - top)
    total = weight_a + weight_b
    return out_a * (weight_a / total) + out_b * (weight_b / total), top + jnp.log2(total)


class Flow:
    def __init__(self, sel, q_in, k_in, v_in, out, scratch):
        (
            self.q_own, self.q_one, self.q_two, self.v_t, self.o_own, self.l_own, self.o_snd2, self.l_snd2,
            self.o_got2, self.l_got2, self.o_snd1, self.l_snd1, self.o_got1, self.l_got1,
            self.bias_own, self.bias_two, self.send_sem, self.recv_sem,
        ) = scratch
        self.sel, self.q_in, self.k_in, self.v_in, self.out = sel, q_in, k_in, v_in, out
        self.chunks, self.rows, self.width = self.q_own.shape
        self.per_chunk = self.width // HEAD
        self.lse_step = 8 // self.per_chunk
        self.shard = lax.axis_index(SEQ)
        count = lax.axis_size(SEQ)
        self.right = lax.rem(self.shard + 1, count)
        self.left = lax.rem(self.shard + count - 1, count)

    def copy(self, which, c, src, dst, target):
        return pltpu.make_async_remote_copy(
            src_ref=src.at[c], dst_ref=dst.at[c],
            send_sem=self.send_sem.at[which, c], recv_sem=self.recv_sem.at[which, c],
            device_id={SEQ: target}, device_id_type=MESH,
        )

    def hop_one(self, c):
        return self.copy(0, c, self.q_own, self.q_one, self.left)

    def hop_two(self, c):
        return self.copy(1, c, self.q_one, self.q_two, self.left)

    def back_two(self, c):
        return (
            self.copy(2, c, self.o_snd2, self.o_got2, self.right),
            self.copy(3, c, self.l_snd2, self.l_got2, self.right),
        )

    def back_one(self, c):
        return (
            self.copy(4, c, self.o_snd1, self.o_got1, self.right),
            self.copy(5, c, self.l_snd1, self.l_got1, self.right),
        )

    def begin(self, ahead, others=()):
        barrier = pltpu.get_barrier_semaphore()
        greeted = (self.left, self.right, *others)
        for neighbour in greeted:
            pl.semaphore_signal(barrier, inc=1, device_id={SEQ: neighbour}, device_id_type=MESH)
        picks = self.rows // BLK
        for a in range(picks):
            block = self.q_in[self.sel[a]]
            for c in range(self.chunks):
                self.q_own[c, a * BLK : (a + 1) * BLK, :] = block[:, c * self.width : (c + 1) * self.width]
        pl.semaphore_wait(barrier, len(greeted))
        for c in range(ahead):
            self.hop_one(c).start()
        self.ahead = ahead
        lane = lax.broadcasted_iota(jnp.int32, (1, self.rows), 1)
        key_at = lax.broadcasted_iota(jnp.int32, self.bias_own.shape, 0)
        for base, ref in ((0, self.bias_own), (2 * picks, self.bias_two)):
            place = lane
            for a in range(picks):
                place = jnp.where(lane // BLK == a, (lane - a * BLK) + self.sel[base + a] * BLK, place)
            seen = (key_at <= place) if base == 0 else (key_at > place)
            ref[...] = jnp.where(seen, 0.0, LOW)

    def cols(self, c, h):
        return pl.ds(pl.multiple_of(c * self.width + h * HEAD, HEAD), HEAD)

    def lse_at(self, h):
        return slice(h * self.lse_step, (h + 1) * self.lse_step)

    def spread(self, row):
        return jnp.broadcast_to(row, (self.lse_step, self.rows))

    def head(self, h):
        return slice(h * HEAD, (h + 1) * HEAD)

    def pump(self, c):
        self.hop_one(c).wait_recv()
        self.hop_two(c).start()

        @pl.when(c + self.ahead < self.chunks)
        def _():
            self.hop_one(c + self.ahead).start()

    def own(self, c):
        for h in range(self.per_chunk):
            cols = self.cols(c, h)
            value_t = self.v_in[:, cols].T
            self.v_t[cols, :] = value_t
            part, lse = window_part(
                self.q_own[c, :, self.head(h)], self.k_in[:, cols], value_t, self.bias_own[...]
            )
            self.o_own[c, self.head(h), :] = part
            self.l_own[c, self.lse_at(h), :] = self.spread(lse)

    def two(self, c):
        self.hop_two(c).wait_recv()
        for h in range(self.per_chunk):
            cols = self.cols(c, h)
            part, lse = window_part(
                self.q_two[c, :, self.head(h)], self.k_in[:, cols], self.v_t[cols, :], self.bias_two[...]
            )
            self.o_snd2[c, self.head(h), :] = part.astype(BF16)
            self.l_snd2[c, self.lse_at(h), :] = self.spread(lse)
        for each in self.back_two(c):
            each.start()

    def incoming(self, got, h, c):
        first = h * self.lse_step
        return jnp.where(self.shard == 0, LOW, got[c, first : first + 1, :])

    def one(self, c):
        parts = []
        for h in range(self.per_chunk):
            cols = self.cols(c, h)
            parts.append(
                window_part(self.q_one[c, :, self.head(h)], self.k_in[:, cols], self.v_t[cols, :], None)
            )
        for each in self.back_two(c):
            each.wait_recv()
        for h in range(self.per_chunk):
            part, lse = merged(
                *parts[h], self.o_got2[c, self.head(h), :].astype(F32), self.incoming(self.l_got2, h, c)
            )
            self.o_snd1[c, self.head(h), :] = part.astype(BF16)
            self.l_snd1[c, self.lse_at(h), :] = self.spread(lse)
        for each in self.back_one(c):
            each.start()

    def final(self, c):
        for each in self.back_one(c):
            each.wait_recv()
        for h in range(self.per_chunk):
            first = h * self.lse_step
            part, _ = merged(
                self.o_own[c, self.head(h), :], self.l_own[c, first : first + 1, :],
                self.o_got1[c, self.head(h), :].astype(F32), self.incoming(self.l_got1, h, c),
            )
            self.store(c, h, part.T.astype(BF16))

    def store(self, c, h, value):
        self.out[:, self.cols(c, h)] = value

    def step(self, t):
        @pl.when(t < self.chunks)
        def _():
            self.pump(t)
            self.own(t)

        @pl.when((t >= 1) & (t <= self.chunks))
        def _():
            self.two(t - 1)

        @pl.when((t >= 2) & (t <= self.chunks + 1))
        def _():
            self.one(t - 2)

        @pl.when((t >= 3) & (t <= self.chunks + 2))
        def _():
            self.final(t - 3)

    def drain(self):
        def body(c, carry):
            self.hop_one(c).wait_send()
            self.hop_two(c).wait_send()
            for each in self.back_two(c) + self.back_one(c):
                each.wait_send()
            return carry

        lax.fori_loop(0, self.chunks, body, 0)

    @staticmethod
    def scratch(rows, tok, full, per_chunk):
        width = per_chunk * HEAD
        chunks = full // width
        queries = pltpu.VMEM((chunks, rows, width), BF16)
        outs = pltpu.VMEM((chunks, width, rows), BF16)
        lses = pltpu.VMEM((chunks, 8, rows), F32)
        return [
            queries, queries, queries, pltpu.VMEM((full, tok), BF16), pltpu.VMEM((chunks, width, rows), F32), lses,
            outs, lses, outs, lses, outs, lses, outs, lses,
            pltpu.VMEM((tok, rows), F32), pltpu.VMEM((tok, rows), F32),
            pltpu.SemaphoreType.DMA((6, chunks)), pltpu.SemaphoreType.DMA((6, chunks)),
        ]


SIDE = 4


class Spread:
    OFFSETS = (0, 1, SIDE - 1, 2)
    MESSAGES = 20

    def __init__(self, got, send_sem, recv_sem):
        self.got, self.send_sem, self.recv_sem = got, send_sem, recv_sem
        shard = lax.axis_index(SEQ)
        row, col = shard // SIDE, lax.rem(shard, SIDE)
        self.here = ((col, row), (row, col))

    @staticmethod
    def turn(at, by):
        return lax.rem(at + by + SIDE, SIDE)

    @staticmethod
    def slot(kind, place):
        a, b = place
        return b * SIDE + a if kind == 0 else a * SIDE + b

    def neighbours(self):
        a, b = self.here[0]
        return [self.slot(0, (self.turn(a, by), b)) for by in (1, -1)] + [
            self.slot(0, (a, self.turn(b, by))) for by in (1, -1)
        ]

    def message(self, c, kind, which, place, half, target):
        slot = self.slot(kind, place)
        ref = self.got.at[c, kind, slot] if half is None else self.got.at[c, kind, slot, half]
        at = kind * self.MESSAGES + which
        return pltpu.make_async_remote_copy(
            src_ref=ref, dst_ref=ref, send_sem=self.send_sem.at[c, at], recv_sem=self.recv_sem.at[c, at],
            device_id={SEQ: self.slot(kind, target)}, device_id_type=MESH,
        )

    def first(self, c, kind, what):
        a, b = self.here[kind]
        up, down = (self.turn(a, 1), b), (self.turn(a, -1), b)
        return self.four(c, kind, 0, (a, b), up, down, (self.turn(a, 2), b), up, down, what)

    def second(self, c, kind, k, what):
        a, b = self.here[kind]
        origin = self.turn(a, self.OFFSETS[k])
        return self.four(
            c, kind, 4 + 4 * k, (origin, b), (origin, self.turn(b, 1)), (origin, self.turn(b, -1)),
            (origin, self.turn(b, 2)), (a, self.turn(b, 1)), (a, self.turn(b, -1)), what,
        )

    def four(self, c, kind, base, here, up, down, far, to_up, to_down, what):
        pairs = {
            "send": ((base, here, None, to_up), (base + 1, here, None, to_down)),
            "came": ((base, down, None, to_up), (base + 1, up, None, to_down)),
            "pass": ((base + 2, down, 0, to_up), (base + 3, up, 1, to_down)),
            "last": ((base + 2, far, 0, to_up), (base + 3, far, 1, to_down)),
        }[what]
        return [self.message(c, kind, *pair) for pair in pairs]

    def launch(self, c):
        for kind in range(2):
            for each in self.first(c, kind, "send"):
                each.start()

    def relay(self, c):
        for kind in range(2):
            for each in self.first(c, kind, "came"):
                each.wait_recv()
            for each in self.first(c, kind, "pass"):
                each.start()
            for k in range(3):
                for each in self.second(c, kind, k, "send"):
                    each.start()

    def relay_far(self, c):
        for kind in range(2):
            for each in self.first(c, kind, "last"):
                each.wait_recv()
            for each in self.second(c, kind, 3, "send"):
                each.start()

    def second_relay(self, c):
        for k in range(4):
            for kind in range(2):
                for each in self.second(c, kind, k, "came"):
                    each.wait_recv()
                for each in self.second(c, kind, k, "pass"):
                    each.start()

    def settle(self, c):
        for k in range(4):
            for kind in range(2):
                for each in self.second(c, kind, k, "last"):
                    each.wait_recv()

    def drain(self, c):
        for kind in range(2):
            for what in ("send", "pass"):
                for each in self.first(c, kind, what):
                    each.wait_send()
                for k in range(4):
                    for each in self.second(c, kind, k, what):
                        each.wait_send()


def front_kernel(
    kept_shard, kept_at, sel, q_in, k_in, v_in, three, out, rows_out, projected, scale_out,
    weights, got, held, staged, staged_sem, total, squares, spread_send, spread_recv, *scratch,
):
    kept = kept_shard.shape[0]
    flow = Flow(sel, q_in, k_in, v_in, out, scratch)
    spread = Spread(got, spread_send, spread_recv)
    chunks, width = flow.chunks, flow.width
    total_rows, local = projected.shape
    full = k_in.shape[1]
    block = 512

    def store(c, h, value):
        out[:, flow.cols(c, h)] = value
        for a in range(flow.rows // BLK):
            got[c, h, flow.shard, a] = value[a * BLK : (a + 1) * BLK, :]

    flow.store = store
    flow.begin(3, spread.neighbours())
    for which in range(3):
        weights[:, which * HEAD : (which + 1) * HEAD] = three[which]
    total[...] = jnp.zeros_like(total)
    squares[...] = jnp.zeros_like(squares)

    def staged_copy(c):
        which = lax.rem(c, 2)
        return pltpu.make_async_copy(staged.at[which], rows_out.at[c], staged_sem.at[which])

    def project_chunk(c):
        which = lax.rem(c, 2)

        @pl.when(c >= 2)
        def _():
            staged_copy(c - 2).wait()

        def hold(i, carry):
            for h in range(flow.per_chunk):
                held[i, :, :, flow.head(h)] = got[c, h, i]
            return carry

        lax.fori_loop(0, SIDE * SIDE, hold, 0)

        def pick(j, carry):
            at = pl.ds(pl.multiple_of(j * BLK, BLK), BLK)
            staged[which, at, :] = held[kept_shard[j], kept_at[j]]
            return carry

        lax.fori_loop(0, kept, pick, 0)
        staged_copy(c).start()
        weight = weights[pl.ds(pl.multiple_of(c * width, width), width), :]

        def multiply(r, carry):
            at = pl.ds(pl.multiple_of(r * block, block), block)
            rows = staged[which, at, :]
            total[at, :] += jnp.dot(rows, weight, preferred_element_type=F32)
            wide = rows.astype(F32)
            square = wide * wide
            squares[at, :] += sum(square[:, h * HEAD : (h + 1) * HEAD] for h in range(flow.per_chunk))
            return carry

        lax.fori_loop(0, total_rows // block, multiply, 0)

    def step(t, carry):
        def stage(late, *calls):
            @pl.when((t >= late) & (t < chunks + late))
            def _():
                for call in calls:
                    call(t - late)

        stage(0, flow.pump)
        stage(4, spread.relay)
        stage(0, flow.own)
        stage(5, spread.relay_far)
        stage(1, flow.two)
        stage(2, flow.one)
        stage(6, spread.second_relay)
        stage(3, flow.final, spread.launch)
        stage(7, spread.settle, project_chunk)
        return carry

    lax.fori_loop(0, chunks + 7, step, 0)

    def finish(r, carry):
        at = pl.ds(pl.multiple_of(r * block, block), block)
        square = squares[at, :]
        inv = lax.rsqrt(jnp.sum(square, axis=1, keepdims=True) * (1.0 / full) + 1e-06)
        projected[at, :] = (total[at, :] * inv).astype(BF16)
        scale_out[:, at] = lax.rsqrt(jnp.sum(square.T, axis=0, keepdims=True) * (1.0 / full) + 1e-06)
        return carry

    lax.fori_loop(0, total_rows // block, finish, 0)

    def drain(c, carry):
        spread.drain(c)
        return carry

    lax.fori_loop(0, chunks, drain, 0)
    for c in (chunks - 2, chunks - 1):
        staged_copy(c).wait()
    flow.drain()


def front(kept_shard, kept_at, sel, query, key, value, weights, per_chunk, ident):
    tok, full = key.shape
    local = 3 * HEAD
    rows = sel.shape[0] // 3 * BLK
    total_rows = kept_shard.shape[0] * BLK
    width = per_chunk * HEAD
    chunks = full // width
    vmem = pl.BlockSpec(memory_space=pltpu.VMEM)
    smem = pl.BlockSpec(memory_space=pltpu.SMEM)
    return pl.pallas_call(
        front_kernel,
        out_shape=(
            jax.ShapeDtypeStruct((rows, full), BF16),
            jax.ShapeDtypeStruct((chunks, total_rows, width), BF16),
            jax.ShapeDtypeStruct((total_rows, local), BF16),
            jax.ShapeDtypeStruct((1, total_rows), F32),
        ),
        in_specs=[smem, smem, smem, vmem, vmem, vmem, vmem],
        out_specs=[vmem, pl.BlockSpec(memory_space=pl.ANY), vmem, vmem],
        scratch_shapes=[
            pltpu.VMEM((full, local), BF16),
            pltpu.VMEM((chunks, 2, SIDE * SIDE, rows // BLK, BLK, HEAD), BF16),
            pltpu.VMEM((SIDE * SIDE, rows // BLK, BLK, width), BF16),
            pltpu.VMEM((2, total_rows, width), BF16),
            pltpu.SemaphoreType.DMA((2,)),
            pltpu.VMEM((total_rows, local), F32),
            pltpu.VMEM((total_rows, HEAD), F32),
            pltpu.SemaphoreType.DMA((chunks, 2 * Spread.MESSAGES)),
            pltpu.SemaphoreType.DMA((chunks, 2 * Spread.MESSAGES)),
            *Flow.scratch(rows, tok, full, per_chunk),
        ],
        compiler_params=pltpu.CompilerParams(
            collective_id=ident, has_side_effects=True, vmem_limit_bytes=VMEM_LIMIT
        ),
        name="front",
    )(kept_shard, kept_at, sel, query, key, value, weights)


QB = 256
KB = 512


def causal_kernel(
    dest, sel, qkv, scale, cot, gathered, q_in, k_in, v_in, out, d_all, grads, rest,
    rows_in, rows_sem, d_all_t, v_t, k_t, do_own, do_t, p_buf, dk_acc, dv_acc, dq_t, *scratch,
):
    kept = dest.shape[0]
    total_rows = qkv.shape[0]
    blocks = total_rows // QB
    rows_copy = pltpu.make_async_copy(gathered, rows_in, rows_sem)
    rows_copy.start()
    flow = Flow(sel, q_in, k_in, v_in, rest, scratch)
    flow.begin(4)

    for j in range(kept):
        do_own[j * BLK : (j + 1) * BLK, :] = cot[dest[j]]

    def prepare(c, carry):
        at = pl.ds(pl.multiple_of(c * QB, QB), QB)
        k_t[:, at] = qkv[at, HEAD : 2 * HEAD].T
        v_t[:, at] = qkv[at, 2 * HEAD : 3 * HEAD].T
        do_t[:, at] = do_own[at, :].T
        return carry

    lax.fori_loop(0, blocks, prepare, 0)
    dk_acc[...] = jnp.zeros_like(dk_acc)
    dv_acc[...] = jnp.zeros_like(dv_acc)

    def query_block(i):
        rows = pl.ds(pl.multiple_of(i * QB, QB), QB)
        chunks = (i * QB + QB + KB - 1) // KB
        q_i = qkv[rows, :HEAD]
        do_i = do_own[rows, :]

        def scores_of(c, masked):
            keys = pl.ds(pl.multiple_of(c * KB, KB), KB)
            scores = lax.dot_general(qkv[keys, HEAD : 2 * HEAD], q_i, NT, preferred_element_type=F32)
            if masked:
                key_at = lax.broadcasted_iota(jnp.int32, (KB, QB), 0)
                row_at = lax.broadcasted_iota(jnp.int32, (KB, QB), 1)
                scores = jnp.where(key_at - row_at <= i * QB - (chunks - 1) * KB, scores, LOW)
            p_buf[keys, :] = scores
            return jnp.max(scores, axis=0, keepdims=True)

        top = lax.fori_loop(
            0, chunks - 1, lambda c, m: jnp.maximum(m, scores_of(c, False)), scores_of(chunks - 1, True)
        )

        def weigh(c, carry):
            total, acc = carry
            keys = pl.ds(pl.multiple_of(c * KB, KB), KB)
            weight = jnp.exp2((p_buf[keys, :] - top) * SCALE2)
            p_buf[keys, :] = weight
            total = total + jnp.sum(weight, axis=0, keepdims=True)
            acc = acc + jnp.dot(v_t[:, keys], weight.astype(BF16), preferred_element_type=F32)
            return total, acc

        total, acc = lax.fori_loop(
            0, chunks, weigh, (jnp.zeros((1, QB), F32), jnp.zeros((HEAD, QB), F32))
        )
        inv = 1.0 / total
        o_t = acc * inv
        delta = jnp.sum(o_t * do_t[:, rows].astype(F32), axis=0, keepdims=True)
        out[rows, :] = o_t.T.astype(BF16)

        def back(c, acc):
            keys = pl.ds(pl.multiple_of(c * KB, KB), KB)
            soft = p_buf[keys, :] * inv
            dv_acc[keys, :] += jnp.dot(soft.astype(BF16), do_i, preferred_element_type=F32)
            d_probs = lax.dot_general(qkv[keys, 2 * HEAD :], do_i, NT, preferred_element_type=F32)
            d_scores = (soft * (d_probs - delta) * SCALE).astype(BF16)
            dk_acc[keys, :] += jnp.dot(d_scores, q_i, preferred_element_type=F32)
            return acc + jnp.dot(k_t[:, keys], d_scores, preferred_element_type=F32)

        dq_t[:, rows] = lax.fori_loop(0, chunks, back, jnp.zeros((HEAD, QB), F32))

    def finish(c, carry):
        at = pl.ds(pl.multiple_of(c * QB, QB), QB)
        d_q = dq_t[:, at]
        d_all_t[:HEAD, at] = (d_q * scale[:, at]).astype(BF16)
        d_all[at, :HEAD] = d_q.T.astype(BF16)
        for which, acc in ((1, dk_acc), (2, dv_acc)):
            value = acc[at, :]
            d_all[at, which * HEAD : (which + 1) * HEAD] = value.astype(BF16)
            d_all_t[which * HEAD : (which + 1) * HEAD, at] = (value.T * scale[:, at]).astype(BF16)
        return carry

    def weight_block(g, carry):
        at = pl.ds(pl.multiple_of(g * QB, QB), QB)
        value = jnp.dot(d_all_t[...], rows_in[g], preferred_element_type=F32)
        for which in range(3):
            grads[which, at, :] = value[which * HEAD : (which + 1) * HEAD, :].T.astype(BF16)
        return carry

    col_blocks = rows_in.shape[0]
    share = (col_blocks + 2) // 3
    every = flow.chunks // blocks

    def step(t, carry):
        flow.step(t)

        @pl.when((t < flow.chunks) & (lax.rem(t, every) == 0))
        def _():
            query_block(blocks - 1 - t // every)

        @pl.when(t == flow.chunks)
        def _():
            lax.fori_loop(0, blocks, finish, 0)
            rows_copy.wait()

        @pl.when(t >= flow.chunks)
        def _():
            low = (t - flow.chunks) * share
            lax.fori_loop(low, jnp.minimum(low + share, col_blocks), weight_block, 0)

        return carry

    lax.fori_loop(0, flow.chunks + 3, step, 0)
    flow.drain()


def causal(dest, sel, qkv, scale, cot, gathered, query, key, value, per_chunk, ident):
    total_rows, local = qkv.shape
    tok, full = key.shape
    rows = sel.shape[0] // 3 * BLK
    vmem = pl.BlockSpec(memory_space=pltpu.VMEM)
    smem = pl.BlockSpec(memory_space=pltpu.SMEM)
    return pl.pallas_call(
        causal_kernel,
        out_shape=(
            jax.ShapeDtypeStruct((total_rows, HEAD), BF16),
            jax.ShapeDtypeStruct((total_rows, local), BF16),
            jax.ShapeDtypeStruct((3, full, HEAD), BF16),
            jax.ShapeDtypeStruct((rows, full), BF16),
        ),
        in_specs=[smem, smem, vmem, vmem, vmem, pl.BlockSpec(memory_space=pl.ANY), vmem, vmem, vmem],
        out_specs=[vmem, vmem, vmem, vmem],
        scratch_shapes=[
            pltpu.VMEM(gathered.shape, BF16),
            pltpu.SemaphoreType.DMA,
            pltpu.VMEM((local, total_rows), BF16),
            pltpu.VMEM((HEAD, total_rows), BF16),
            pltpu.VMEM((HEAD, total_rows), BF16),
            pltpu.VMEM((total_rows, HEAD), BF16),
            pltpu.VMEM((HEAD, total_rows), BF16),
            pltpu.VMEM((total_rows, QB), F32),
            pltpu.VMEM((total_rows, HEAD), F32),
            pltpu.VMEM((total_rows, HEAD), F32),
            pltpu.VMEM((HEAD, total_rows), F32),
            *Flow.scratch(rows, tok, full, per_chunk),
        ],
        compiler_params=pltpu.CompilerParams(
            collective_id=ident, has_side_effects=True, vmem_limit_bytes=VMEM_LIMIT
        ),
        cost_estimate=pl.CostEstimate(
            flops=20 * 10**9, bytes_accessed=32 * 1024 * 1024, transcendentals=0
        ),
        name="causal",
    )(dest, sel, qkv, scale, cot, gathered, query, key, value)


class Reduce:
    def __init__(self, value, pair_got, own, snd, got1, got2, whole, send_sem, recv_sem):
        self.value, self.pair_got, self.own, self.snd = value, pair_got, own, snd
        self.got1, self.got2, self.whole = got1, got2, whole
        self.send_sem, self.recv_sem = send_sem, recv_sem
        at = lax.axis_index("dp")
        self.y, self.core = at // 2, lax.rem(at, 2)
        self.partner = self.y * 2 + 1 - self.core
        self.next = [self.turn(by) * 2 + self.core for by in (1, -1)]
        middle = value.shape[3] // 2
        self.halves = (slice(0, middle), slice(middle, 2 * middle))

    def turn(self, by):
        return lax.rem(self.y + by + SIDE, SIDE)

    def copy(self, which, src, dst, target):
        return pltpu.make_async_remote_copy(
            src_ref=src, dst_ref=dst, send_sem=self.send_sem.at[which], recv_sem=self.recv_sem.at[which],
            device_id={"dp": target}, device_id_type=MESH,
        )

    def pair(self):
        return self.copy(0, self.value.at[:, 1 - self.core], self.pair_got, self.partner)

    def ring1(self, d):
        return self.copy(1 + d, self.snd.at[d, 0, :, self.halves[0]], self.got1.at[d], self.next[d])

    def ring2(self, d):
        return self.copy(3 + d, self.snd.at[d, 1], self.got2.at[d], self.next[d])

    def quarter(self, by, half=None):
        ref = self.whole.at[:, self.core, self.turn(by)]
        return ref if half is None else self.whole.at[:, self.core, self.turn(by), self.halves[half]]

    def spread1(self, d, by):
        return self.copy(5 + d, self.quarter(by), self.quarter(by), self.next[d])

    def spread2(self, d, by):
        return self.copy(7 + d, self.quarter(by, d), self.quarter(by, d), self.next[d])

    def back(self, core):
        return self.copy(9, self.whole.at[:, core], self.whole.at[:, core], self.partner)

    def stage1(self):
        self.pair().wait_recv()

        def add(q, carry):
            self.own[q] = self.value[:, self.core, q].astype(F32) + self.pair_got[:, q].astype(F32)
            return carry

        lax.fori_loop(0, SIDE, add, 0)
        for d in range(2):
            self.snd[d, 0, :, self.halves[0]] = self.own[self.turn(2), :, self.halves[d]].astype(BF16)
            self.ring1(d).start()

    def stage2(self):
        for d in range(2):
            self.ring1(d).wait_recv()
            near = self.turn(1 - 2 * d)
            self.snd[d, 1, :, self.halves[1 - d]] = self.own[near, :, self.halves[1 - d]].astype(BF16)
            self.snd[d, 1, :, self.halves[d]] = (
                self.own[near, :, self.halves[d]] + self.got1[d].astype(F32)
            ).astype(BF16)
            self.ring2(d).start()

    def stage3(self):
        for d in range(2):
            self.ring2(d).wait_recv()
        total = self.own[self.y] + self.got2[0].astype(F32) + self.got2[1].astype(F32)
        self.whole[:, self.core, self.y] = total.astype(BF16)
        for d in range(2):
            self.spread1(d, 0).start()

    def stage4(self):
        for d in range(2):
            self.spread1(d, 2 * d - 1).wait_recv()
            self.spread2(d, 2 * d - 1).start()

    def stage5(self):
        for d in range(2):
            self.spread2(d, 2).wait_recv()
        self.back(self.core).start()

    def stage6(self, out):
        self.back(1 - self.core).wait_recv()
        out[...] = self.whole[...]
        self.pair().wait_send()
        for d in range(2):
            self.ring1(d).wait_send()
            self.ring2(d).wait_send()
            self.spread1(d, 0).wait_send()
            self.spread2(d, 2 * d - 1).wait_send()
        self.back(self.core).wait_send()

    @staticmethod
    def scratch(shape):
        three, _, quarters, rows, width = shape
        return [
            pltpu.VMEM((three, quarters, rows, width), BF16),
            pltpu.VMEM((quarters, three, rows, width), F32),
            pltpu.VMEM((2, 2, three, rows, width), BF16),
            pltpu.VMEM((2, three, rows // 2, width), BF16),
            pltpu.VMEM((2, three, rows, width), BF16),
            pltpu.VMEM(shape, BF16),
            pltpu.SemaphoreType.DMA((10,)),
            pltpu.SemaphoreType.DMA((10,)),
        ]


def scatter_kernel(
    slot_at, d_all, three, value, out, summed, weights, terms, got1, snd2, got2, sums, last1, lasts2, last2,
    send1, recv1, send2, recv2, send3, recv3, send4, recv4, *reduce_scratch,
):
    shard = lax.axis_index(SEQ)
    row, col = shard // SIDE, lax.rem(shard, SIDE)
    wide = out.shape[1] // 2
    part = wide // 2
    place = ((row, col), (col, row))
    halves = (slice(0, part), slice(part, wide))

    def turn(at, by):
        return lax.rem(at + by + SIDE, SIDE)

    def slot(h, a, b):
        return a * SIDE + b if h == 0 else b * SIDE + a

    barrier = pltpu.get_barrier_semaphore()
    for by in (1, -1):
        for h in range(2):
            a, b = place[h]
            pl.semaphore_signal(
                barrier, inc=1, device_id={SEQ: slot(h, turn(a, by), b)}, device_id_type=MESH
            )
    reduce = Reduce(value, *reduce_scratch)
    for target in (reduce.partner, *reduce.next):
        pl.semaphore_signal(barrier, inc=1, device_id={"dp": target}, device_id_type=MESH)
    for which in range(3):
        weights[:, which * HEAD : (which + 1) * HEAD] = three[which]

    def group(h, a):
        slots = [jnp.where(h == 0, a * SIDE + s, s * SIDE + a) for s in range(SIDE)]
        rows = jnp.concatenate([d_all[slot_at[one]] for one in slots], axis=0)
        cols = pl.ds(pl.multiple_of(h * wide, wide), wide)
        value = lax.dot_general(rows, weights[cols, :], NT, preferred_element_type=F32).astype(BF16)
        for s in range(SIDE):
            terms[h, a, s] = value[s * BLK : (s + 1) * BLK, :]

    def first_send(h, d, s):
        a, b = place[h]
        return pltpu.make_async_remote_copy(
            src_ref=terms.at[h, turn(a, 2), s, :, halves[d]], dst_ref=got1.at[h, d, s],
            send_sem=send1.at[h, d, s], recv_sem=recv1.at[h, d, s],
            device_id={SEQ: slot(h, turn(a, 1 - 2 * d), b)}, device_id_type=MESH,
        )

    def second_send(h, d, s):
        a, b = place[h]
        return pltpu.make_async_remote_copy(
            src_ref=snd2.at[h, d, s], dst_ref=got2.at[h, d, s],
            send_sem=send2.at[h, d, s], recv_sem=recv2.at[h, d, s],
            device_id={SEQ: slot(h, turn(a, 1 - 2 * d), b)}, device_id_type=MESH,
        )

    def third_send(h, d):
        a, b = place[h]
        return pltpu.make_async_remote_copy(
            src_ref=sums.at[h, turn(b, 2), :, halves[d]], dst_ref=last1.at[h, d],
            send_sem=send3.at[h, d], recv_sem=recv3.at[h, d],
            device_id={SEQ: slot(h, a, turn(b, 1 - 2 * d))}, device_id_type=MESH,
        )

    def fourth_send(h, d):
        a, b = place[h]
        return pltpu.make_async_remote_copy(
            src_ref=lasts2.at[h, d], dst_ref=last2.at[h, d],
            send_sem=send4.at[h, d], recv_sem=recv4.at[h, d],
            device_id={SEQ: slot(h, a, turn(b, 1 - 2 * d))}, device_id_type=MESH,
        )

    def group_far(h, carry):
        group(h, turn(jnp.where(h == 0, row, col), 2))
        return carry

    def group_rest(g, carry):
        h, which = lax.rem(g, 2), g // 2
        by = jnp.where(which == 0, 1, jnp.where(which == 1, SIDE - 1, 0))
        group(h, turn(jnp.where(h == 0, row, col), by))
        return carry

    lax.fori_loop(0, 2, group_far, 0)
    pl.semaphore_wait(barrier, 7)
    reduce.pair().start()
    for k in (2, 1, 3, 0):
        for h in range(2):
            s = turn(place[h][1], k)
            for d in range(2):
                first_send(h, d, s).start()
    lax.fori_loop(0, 2, group_rest, 0)
    reduce.stage1()
    lax.fori_loop(2, 6, group_rest, 0)
    reduce.stage2()
    for k in (2, 1, 3, 0):
        for h in range(2):
            a, b = place[h]
            s = turn(b, k)
            for d in range(2):
                first_send(h, d, s).wait_recv()
                near = turn(a, 1 - 2 * d)
                other = halves[1 - d]
                snd2[h, d, s, :, other] = terms[h, near, s, :, other]
                snd2[h, d, s, :, halves[d]] = (
                    terms[h, near, s, :, halves[d]].astype(F32) + got1[h, d, s].astype(F32)
                ).astype(BF16)
                second_send(h, d, s).start()
    reduce.stage3()
    for k in (2, 1, 3, 0):
        for h in range(2):
            a, b = place[h]
            s = turn(b, k)
            for d in range(2):
                second_send(h, d, s).wait_recv()
            total = (
                terms[h, a, s].astype(F32) + got2[h, 0, s].astype(F32) + got2[h, 1, s].astype(F32)
            )
            if k != 0:
                sums[h, s] = total.astype(BF16)
            if k == 2:
                for d in range(2):
                    third_send(h, d).start()
            elif k != 0:
                d = 0 if k == 1 else 1
                third_send(h, d).wait_recv()
                other = halves[1 - d]
                lasts2[h, d, :, other] = sums[h, s, :, other]
                lasts2[h, d, :, halves[d]] = (total[:, halves[d]] + last1[h, d].astype(F32)).astype(BF16)
                fourth_send(h, d).start()
            else:
                for d in range(2):
                    fourth_send(h, d).wait_recv()
                out[:, h * wide : (h + 1) * wide] = (
                    total + last2[h, 0].astype(F32) + last2[h, 1].astype(F32)
                ).astype(BF16)
        if k == 2:
            reduce.stage4()
        elif k == 1:
            reduce.stage5()
        elif k == 3:
            reduce.stage6(summed)
    for h in range(2):
        for d in range(2):
            for s in range(SIDE):
                first_send(h, d, s).wait_send()
                second_send(h, d, s).wait_send()
            third_send(h, d).wait_send()
            fourth_send(h, d).wait_send()


def scatter_terms(slot_at, d_all, three, value, ident):
    blocks, _, local = d_all.shape
    full = three.shape[1]
    wide = full // 2
    part = wide // 2
    vmem = pl.BlockSpec(memory_space=pltpu.VMEM)
    four = pltpu.SemaphoreType.DMA((2, 2, SIDE))
    two = pltpu.SemaphoreType.DMA((2, 2))
    return pl.pallas_call(
        scatter_kernel,
        out_shape=(jax.ShapeDtypeStruct((BLK, full), BF16), jax.ShapeDtypeStruct(value.shape, BF16)),
        in_specs=[pl.BlockSpec(memory_space=pltpu.SMEM), vmem, vmem, vmem],
        out_specs=[vmem, vmem],
        scratch_shapes=[
            pltpu.VMEM((full, local), BF16),
            pltpu.VMEM((2, SIDE, SIDE, BLK, wide), BF16),
            pltpu.VMEM((2, 2, SIDE, BLK, part), BF16),
            pltpu.VMEM((2, 2, SIDE, BLK, wide), BF16),
            pltpu.VMEM((2, 2, SIDE, BLK, wide), BF16),
            pltpu.VMEM((2, SIDE, BLK, wide), BF16),
            pltpu.VMEM((2, 2, BLK, part), BF16),
            pltpu.VMEM((2, 2, BLK, wide), BF16),
            pltpu.VMEM((2, 2, BLK, wide), BF16),
            four, four, four, four, two, two, two, two,
            *Reduce.scratch(value.shape),
        ],
        compiler_params=pltpu.CompilerParams(
            collective_id=ident, has_side_effects=True, vmem_limit_bytes=VMEM_LIMIT
        ),
        cost_estimate=pl.CostEstimate(
            flops=2 * blocks * BLK * local * full, bytes_accessed=100 * 1024 * 1024, transcendentals=0
        ),
        name="scatter_terms",
    )(slot_at, d_all, three, value)


def assemble_kernel(table, head, rest, sorted_out, out, causal_out):
    kept = sorted_out.shape[0] // BLK
    first = table[kept + 3 * pl.program_id(0)] == 1

    @pl.when(pl.program_id(0) == 0)
    def _():
        for j in range(kept):
            causal_out[pl.ds(pl.multiple_of(table[j] * BLK, BLK), BLK), :] = sorted_out[j * BLK : (j + 1) * BLK, :]

    @pl.when(first)
    def _():
        out[...] = head[...]

    @pl.when(jnp.logical_not(first))
    def _():
        out[...] = rest[...]


def assemble(table, head, rest, sorted_out):
    rows, full = head.shape
    kept = sorted_out.shape[0] // BLK
    whole = pl.BlockSpec(sorted_out.shape, lambda g, t: (0, 0))
    return pl.pallas_call(
        assemble_kernel,
        out_shape=(
            jax.ShapeDtypeStruct((2 * rows, full), BF16),
            jax.ShapeDtypeStruct(sorted_out.shape, BF16),
        ),
        grid_spec=pltpu.PrefetchScalarGridSpec(
            num_scalar_prefetch=1,
            grid=(2 * rows // BLK,),
            in_specs=[
                pl.BlockSpec((BLK, full), lambda g, t: (t[kept + 3 * g + 1], 0)),
                pl.BlockSpec((BLK, full), lambda g, t: (t[kept + 3 * g + 2], 0)),
                whole,
            ],
            out_specs=[pl.BlockSpec((BLK, full), lambda g, t: (g, 0)), whole],
        ),
        name="assemble",
    )(table, head, rest, sorted_out)


def shards(query_input, key_input, value_input, keep_blocks, dest_slots, proj_weights, cotangent):
    tok, full = query_input.shape[1:]
    per_shard = tok // BLK
    shard = lax.axis_index(SEQ)
    count = lax.axis_size(SEQ)
    half_blocks = per_shard // 2
    query = query_input.reshape(per_shard, BLK, full)
    key = key_input[0]
    value = value_input[0]
    keep = keep_blocks[0]
    dest = dest_slots[0]

    kept = jnp.any(
        keep[None, None, :] == jnp.arange(count * per_shard).reshape(count, per_shard)[:, :, None], axis=2
    )
    order_key = jnp.where(kept, 0, per_shard) + jnp.arange(per_shard)[None, :]
    rank = jnp.sum(order_key[:, None, :] < order_key[:, :, None], axis=2).astype(jnp.int32)
    order = jnp.sum(
        jnp.where(
            rank[:, None, :] == jnp.arange(per_shard)[None, :, None], jnp.arange(per_shard)[None, None, :], 0
        ),
        axis=2,
    ).astype(jnp.int32)
    wrapped = jnp.concatenate([order, order[:2]], axis=0)
    near = lax.dynamic_slice_in_dim(wrapped, shard, 3, 0)
    sel_first = near[:, :half_blocks].reshape(-1)
    sel_rest = near[:, half_blocks:].reshape(-1)
    own_rank = lax.dynamic_slice_in_dim(rank, shard, 1, 0)[0]
    in_first = (own_rank < half_blocks).astype(jnp.int32)
    at = own_rank % half_blocks
    table = jnp.stack([in_first, at * in_first, at * (1 - in_first)], axis=1).reshape(-1)
    keep_shard = keep // per_shard
    before = jnp.sum((keep_shard[None, :] == keep_shard[:, None]) & (keep[None, :] < keep[:, None]), axis=1)

    slot_at = jnp.sum(
        jnp.where(dest[None, :] == jnp.arange(dest.shape[0])[:, None], jnp.arange(dest.shape[0])[None, :], 0),
        axis=1,
    ).astype(jnp.int32)

    first, gathered, qkv, scale = front(
        keep_shard.astype(jnp.int32), before.astype(jnp.int32), sel_first, query, key, value, proj_weights, 2, 0
    )
    sorted_out, d_all, local_grads, rest = causal(
        dest, sel_rest, qkv, scale, cotangent.reshape(dest.shape[0], BLK, -1), gathered, query, key, value, 1, 1
    )
    window_out, causal_out = assemble(jnp.concatenate([dest, table]), first, rest, sorted_out)
    row_grad, grads = scatter_terms(
        slot_at, d_all.reshape(dest.shape[0], BLK, -1), proj_weights,
        local_grads.reshape(3, 2, SIDE, full // 2 // SIDE, HEAD), 2,
    )
    grads = grads.reshape(proj_weights.shape).astype(F32)
    return (window_out[None], causal_out[None], grads, row_grad[None])


def solution(mesh):
    return jax.shard_map(
        shards,
        mesh=mesh,
        in_specs=(
            P("dp", "seq", None),
            P("dp", "seq", None),
            P("dp", "seq", None),
            P("dp", None),
            P("dp", None),
            P(None, None, "seq"),
            P("dp", None, "seq"),
        ),
        out_specs=(
            P("dp", "seq", None),
            P("dp", None, "seq"),
            P(None, None, "seq"),
            P("dp", "seq", None),
        ),
        check_vma=False,
    )
```

```python
import functools

import jax
import jax.numpy as jnp
from jax import lax
from jax.experimental import pallas as pl
from jax.experimental.pallas import tpu as pltpu
from jax.sharding import PartitionSpec as P

HEAD = 128
BLK = 128
SEQ = "seq"
MESH = pl.DeviceIdType.MESH
SCALE = HEAD ** (-0.5)
LOG2E = 1.4426950408889634
SCALE2 = SCALE * LOG2E
LOW = -1e30
NT = (((1,), (1,)), ((), ()))
BF16 = jnp.bfloat16
F32 = jnp.float32
VMEM_LIMIT = 56 * 1024 * 1024


def window_part(query, key, value_t, bias):
    scores = lax.dot_general(key, query, NT, preferred_element_type=F32)
    if bias is not None:
        scores = scores + bias
    top = jnp.max(scores, axis=0, keepdims=True)
    weight = jnp.exp2((scores - top) * SCALE2)
    total = jnp.sum(weight, axis=0, keepdims=True)
    out = jnp.dot(value_t, weight.astype(BF16), preferred_element_type=F32)
    return out / total, top * SCALE2 + jnp.log2(total)


def merged(out_a, lse_a, out_b, lse_b):
    top = jnp.maximum(lse_a, lse_b)
    weight_a = jnp.exp2(lse_a - top)
    weight_b = jnp.exp2(lse_b - top)
    total = weight_a + weight_b
    return out_a * (weight_a / total) + out_b * (weight_b / total), top + jnp.log2(total)


def block_ranks(keep, shard, per_shard):
    kept = [
        functools.reduce(
            lambda found, j: jnp.where(keep[0, j] == shard * per_shard + b, 1, found), range(keep.shape[1]), 0
        )
        for b in range(per_shard)
    ]
    total = sum(kept)
    return [
        jnp.where(kept[b] == 1, sum(kept[:b], 0), total + b - sum(kept[:b], 0)) for b in range(per_shard)
    ]


def picked(ranks, places):
    return [functools.reduce(lambda got, b: jnp.where(ranks[b] == at, b, got), range(len(ranks)), 0) for at in places]


def near_ranks(keep, per_shard):
    shard, count = lax.axis_index(SEQ), lax.axis_size(SEQ)
    return [block_ranks(keep, lax.rem(shard + by, count), per_shard) for by in range(3)]


class Flow:
    def __init__(self, sel, q_in, k_in, v_in, out, scratch):
        (
            self.q_own, self.q_one, self.q_two, self.v_t, self.o_own, self.l_own, self.o_snd2, self.l_snd2,
            self.o_got2, self.l_got2, self.o_snd1, self.l_snd1, self.o_got1, self.l_got1,
            self.bias_own, self.bias_two, self.send_sem, self.recv_sem,
        ) = scratch
        self.sel, self.q_in, self.k_in, self.v_in, self.out = sel, q_in, k_in, v_in, out
        self.chunks, self.rows, self.width = self.q_own.shape
        self.per_chunk = self.width // HEAD
        self.lse_step = 8 // self.per_chunk
        self.shard = lax.axis_index(SEQ)
        count = lax.axis_size(SEQ)
        self.right = lax.rem(self.shard + 1, count)
        self.left = lax.rem(self.shard + count - 1, count)

    def copy(self, which, c, src, dst, target):
        return pltpu.make_async_remote_copy(
            src_ref=src.at[c], dst_ref=dst.at[c],
            send_sem=self.send_sem.at[which, c], recv_sem=self.recv_sem.at[which, c],
            device_id={SEQ: target}, device_id_type=MESH,
        )

    def hop_one(self, c):
        return self.copy(0, c, self.q_own, self.q_one, self.left)

    def hop_two(self, c):
        return self.copy(1, c, self.q_one, self.q_two, self.left)

    def back_two(self, c):
        return (
            self.copy(2, c, self.o_snd2, self.o_got2, self.right),
            self.copy(3, c, self.l_snd2, self.l_got2, self.right),
        )

    def back_one(self, c):
        return (
            self.copy(4, c, self.o_snd1, self.o_got1, self.right),
            self.copy(5, c, self.l_snd1, self.l_got1, self.right),
        )

    def begin(self, ahead, others=()):
        barrier = pltpu.get_barrier_semaphore()
        greeted = (self.left, self.right, *others)
        for neighbour in greeted:
            pl.semaphore_signal(barrier, inc=1, device_id={SEQ: neighbour}, device_id_type=MESH)
        picks = self.rows // BLK
        for a in range(picks):
            block = self.q_in[self.sel[a]]
            for c in range(self.chunks):
                self.q_own[c, a * BLK : (a + 1) * BLK, :] = block[:, c * self.width : (c + 1) * self.width]
        pl.semaphore_wait(barrier, len(greeted))
        for c in range(ahead):
            self.hop_one(c).start()
        self.ahead = ahead
        lane = lax.broadcasted_iota(jnp.int32, (1, self.rows), 1)
        key_at = lax.broadcasted_iota(jnp.int32, self.bias_own.shape, 0)
        for base, ref in ((0, self.bias_own), (2 * picks, self.bias_two)):
            place = lane
            for a in range(picks):
                place = jnp.where(lane // BLK == a, (lane - a * BLK) + self.sel[base + a] * BLK, place)
            seen = (key_at <= place) if base == 0 else (key_at > place)
            ref[...] = jnp.where(seen, 0.0, LOW)

    def cols(self, c, h):
        return pl.ds(pl.multiple_of(c * self.width + h * HEAD, HEAD), HEAD)

    def lse_at(self, h):
        return slice(h * self.lse_step, (h + 1) * self.lse_step)

    def spread(self, row):
        return jnp.broadcast_to(row, (self.lse_step, self.rows))

    def head(self, h):
        return slice(h * HEAD, (h + 1) * HEAD)

    def pump(self, c):
        self.hop_one(c).wait_recv()
        self.hop_two(c).start()

        @pl.when(c + self.ahead < self.chunks)
        def _():
            self.hop_one(c + self.ahead).start()

    def own(self, c):
        for h in range(self.per_chunk):
            cols = self.cols(c, h)
            value_t = self.v_in[:, cols].T
            self.v_t[cols, :] = value_t
            part, lse = window_part(
                self.q_own[c, :, self.head(h)], self.k_in[:, cols], value_t, self.bias_own[...]
            )
            self.o_own[c, self.head(h), :] = part
            self.l_own[c, self.lse_at(h), :] = self.spread(lse)

    def two(self, c):
        self.hop_two(c).wait_recv()
        for h in range(self.per_chunk):
            cols = self.cols(c, h)
            part, lse = window_part(
                self.q_two[c, :, self.head(h)], self.k_in[:, cols], self.v_t[cols, :], self.bias_two[...]
            )
            self.o_snd2[c, self.head(h), :] = part.astype(BF16)
            self.l_snd2[c, self.lse_at(h), :] = self.spread(lse)
        for each in self.back_two(c):
            each.start()

    def incoming(self, got, h, c):
        first = h * self.lse_step
        return jnp.where(self.shard == 0, LOW, got[c, first : first + 1, :])

    def one(self, c):
        parts = []
        for h in range(self.per_chunk):
            cols = self.cols(c, h)
            parts.append(
                window_part(self.q_one[c, :, self.head(h)], self.k_in[:, cols], self.v_t[cols, :], None)
            )
        for each in self.back_two(c):
            each.wait_recv()
        for h in range(self.per_chunk):
            part, lse = merged(
                *parts[h], self.o_got2[c, self.head(h), :].astype(F32), self.incoming(self.l_got2, h, c)
            )
            self.o_snd1[c, self.head(h), :] = part.astype(BF16)
            self.l_snd1[c, self.lse_at(h), :] = self.spread(lse)
        for each in self.back_one(c):
            each.start()

    def final(self, c):
        for each in self.back_one(c):
            each.wait_recv()
        for h in range(self.per_chunk):
            first = h * self.lse_step
            part, _ = merged(
                self.o_own[c, self.head(h), :], self.l_own[c, first : first + 1, :],
                self.o_got1[c, self.head(h), :].astype(F32), self.incoming(self.l_got1, h, c),
            )
            self.store(c, h, part.T.astype(BF16))

    def store(self, c, h, value):
        self.out[:, self.cols(c, h)] = value

    def step(self, t, lag):
        def stage(late, *calls):
            @pl.when((t >= late) & (t < self.chunks + late))
            def _():
                for call in calls:
                    call(t - late)

        stage(0, self.pump, self.own)
        stage(lag, self.two)
        stage(2 * lag, self.one)
        stage(3 * lag, self.final)

    def drain(self):
        def body(c, carry):
            self.hop_one(c).wait_send()
            self.hop_two(c).wait_send()
            for each in self.back_two(c) + self.back_one(c):
                each.wait_send()
            return carry

        lax.fori_loop(0, self.chunks, body, 0)

    @staticmethod
    def scratch(rows, tok, full, per_chunk):
        width = per_chunk * HEAD
        chunks = full // width
        queries = pltpu.VMEM((chunks, rows, width), BF16)
        outs = pltpu.VMEM((chunks, width, rows), BF16)
        lses = pltpu.VMEM((chunks, 8, rows), F32)
        return [
            queries, queries, queries, pltpu.VMEM((full, tok), BF16), pltpu.VMEM((chunks, width, rows), F32), lses,
            outs, lses, outs, lses, outs, lses, outs, lses,
            pltpu.VMEM((tok, rows), F32), pltpu.VMEM((tok, rows), F32),
            pltpu.SemaphoreType.DMA((6, chunks)), pltpu.SemaphoreType.DMA((6, chunks)),
        ]


SIDE = 4


class Spread:
    OFFSETS = (0, 1, SIDE - 1, 2)
    MESSAGES = 20

    def __init__(self, got, send_sem, recv_sem):
        self.got, self.send_sem, self.recv_sem = got, send_sem, recv_sem
        shard = lax.axis_index(SEQ)
        row, col = shard // SIDE, lax.rem(shard, SIDE)
        self.here = ((col, row), (row, col))

    @staticmethod
    def turn(at, by):
        return lax.rem(at + by + SIDE, SIDE)

    @staticmethod
    def slot(kind, place):
        a, b = place
        return b * SIDE + a if kind == 0 else a * SIDE + b

    def neighbours(self):
        a, b = self.here[0]
        return [self.slot(0, (self.turn(a, by), b)) for by in (1, -1)] + [
            self.slot(0, (a, self.turn(b, by))) for by in (1, -1)
        ]

    def message(self, c, kind, which, place, half, target):
        slot = self.slot(kind, place)
        ref = self.got.at[c, kind, slot] if half is None else self.got.at[c, kind, slot, half]
        at = kind * self.MESSAGES + which
        return pltpu.make_async_remote_copy(
            src_ref=ref, dst_ref=ref, send_sem=self.send_sem.at[c, at], recv_sem=self.recv_sem.at[c, at],
            device_id={SEQ: self.slot(kind, target)}, device_id_type=MESH,
        )

    def first(self, c, kind, what):
        a, b = self.here[kind]
        up, down = (self.turn(a, 1), b), (self.turn(a, -1), b)
        return self.four(c, kind, 0, (a, b), up, down, (self.turn(a, 2), b), up, down, what)

    def second(self, c, kind, k, what):
        a, b = self.here[kind]
        origin = self.turn(a, self.OFFSETS[k])
        return self.four(
            c, kind, 4 + 4 * k, (origin, b), (origin, self.turn(b, 1)), (origin, self.turn(b, -1)),
            (origin, self.turn(b, 2)), (a, self.turn(b, 1)), (a, self.turn(b, -1)), what,
        )

    def four(self, c, kind, base, here, up, down, far, to_up, to_down, what):
        pairs = {
            "send": ((base, here, None, to_up), (base + 1, here, None, to_down)),
            "came": ((base, down, None, to_up), (base + 1, up, None, to_down)),
            "pass": ((base + 2, down, 0, to_up), (base + 3, up, 1, to_down)),
            "last": ((base + 2, far, 0, to_up), (base + 3, far, 1, to_down)),
        }[what]
        return [self.message(c, kind, *pair) for pair in pairs]

    def launch(self, c):
        for kind in range(2):
            for each in self.first(c, kind, "send"):
                each.start()

    def relay(self, c):
        for kind in range(2):
            for each in self.first(c, kind, "came"):
                each.wait_recv()
            for each in self.first(c, kind, "pass"):
                each.start()
            for k in range(3):
                for each in self.second(c, kind, k, "send"):
                    each.start()

    def relay_far(self, c):
        for kind in range(2):
            for each in self.first(c, kind, "last"):
                each.wait_recv()
            for each in self.second(c, kind, 3, "send"):
                each.start()

    def second_relay(self, c):
        for k in range(4):
            for kind in range(2):
                for each in self.second(c, kind, k, "came"):
                    each.wait_recv()
                for each in self.second(c, kind, k, "pass"):
                    each.start()

    def settle(self, c):
        for k in range(4):
            for kind in range(2):
                for each in self.second(c, kind, k, "last"):
                    each.wait_recv()

    def drain(self, c):
        for kind in range(2):
            for what in ("send", "pass"):
                for each in self.first(c, kind, what):
                    each.wait_send()
                for k in range(4):
                    for each in self.second(c, kind, k, what):
                        each.wait_send()


def front_kernel(
    keep, q_in, k_in, v_in, three, out, rows_out, projected, scale_out, table,
    weights, got, held, staged, staged_sem, total, squares, spread_send, spread_recv, *scratch,
):
    kept = keep.shape[1]
    per_shard = q_in.shape[0]
    ranks = near_ranks(keep, per_shard)
    half = per_shard // 2
    sel = [at for each in ranks for at in picked(each, range(half))]
    for b in range(per_shard):
        late = jnp.where(ranks[0][b] >= half, 1, 0)
        table[3 * b] = late
        table[3 * b + 1] = ranks[0][b] * (1 - late)
        table[3 * b + 2] = (ranks[0][b] - half) * late
    owner = [keep[0, j] // per_shard for j in range(kept)]
    nth = [0] + [jnp.where(owner[j] == owner[j - 1], 1, 0) for j in range(1, kept)]
    flow = Flow(sel, q_in, k_in, v_in, out, scratch)
    spread = Spread(got, spread_send, spread_recv)
    chunks, width = flow.chunks, flow.width
    total_rows, local = projected.shape
    full = k_in.shape[1]
    block = 512
    per_kind = flow.per_chunk // 2

    def store(c, h, value):
        out[:, flow.cols(c, h)] = value
        for a in range(flow.rows // BLK):
            got[c, h // per_kind, flow.shard, a, :, flow.head(h % per_kind)] = value[a * BLK : (a + 1) * BLK, :]

    flow.store = store
    flow.begin(3, spread.neighbours())
    for which in range(3):
        weights[:, which * HEAD : (which + 1) * HEAD] = three[which]
    total[...] = jnp.zeros_like(total)
    squares[...] = jnp.zeros_like(squares)

    def staged_copy(c):
        which = lax.rem(c, 2)
        return pltpu.make_async_copy(staged.at[which], rows_out.at[c], staged_sem.at[which])

    def project_chunk(c):
        which = lax.rem(c, 2)

        @pl.when(c >= 2)
        def _():
            staged_copy(c - 2).wait()

        def hold(i, carry):
            for kind in range(2):
                held[i, :, :, kind * width // 2 : (kind + 1) * width // 2] = got[c, kind, i]
            return carry

        lax.fori_loop(0, SIDE * SIDE, hold, 0)

        for j in range(kept):
            staged[which, j * BLK : (j + 1) * BLK, :] = held[owner[j], nth[j]]
        staged_copy(c).start()
        weight = weights[pl.ds(pl.multiple_of(c * width, width), width), :]

        def multiply(r, carry):
            at = pl.ds(pl.multiple_of(r * block, block), block)
            rows = staged[which, at, :]
            total[at, :] += jnp.dot(rows, weight, preferred_element_type=F32)
            wide = rows.astype(F32)
            square = wide * wide
            squares[at, :] += sum(square[:, h * HEAD : (h + 1) * HEAD] for h in range(flow.per_chunk))
            return carry

        lax.fori_loop(0, total_rows // block, multiply, 0)

    def step(t, carry):
        flow.step(t, 1)

        def stage(late, call):
            @pl.when((t >= late) & (t < chunks + late))
            def _():
                call(t - late)

        stage(3, spread.launch)
        stage(4, spread.relay)
        stage(5, spread.relay_far)
        stage(6, spread.second_relay)

        @pl.when(t >= 7)
        def _():
            spread.settle(t - 7)
            project_chunk(t - 7)

        return carry

    lax.fori_loop(0, chunks + 7, step, 0)

    def finish(r, carry):
        at = pl.ds(pl.multiple_of(r * block, block), block)
        square = squares[at, :]
        inv = lax.rsqrt(jnp.sum(square, axis=1, keepdims=True) * (1.0 / full) + 1e-06)
        projected[at, :] = (total[at, :] * inv).astype(BF16)
        scale_out[:, at] = lax.rsqrt(jnp.sum(square.T, axis=0, keepdims=True) * (1.0 / full) + 1e-06)
        return carry

    lax.fori_loop(0, total_rows // block, finish, 0)

    def drain(c, carry):
        spread.drain(c)
        return carry

    lax.fori_loop(0, chunks, drain, 0)
    for c in (chunks - 2, chunks - 1):
        staged_copy(c).wait()
    flow.drain()


def front(keep, query, key, value, weights, per_chunk, ident):
    tok, full = key.shape
    local = 3 * HEAD
    rows = query.shape[0] // 2 * BLK
    total_rows = keep.shape[1] * BLK
    width = per_chunk * HEAD
    chunks = full // width
    vmem = pl.BlockSpec(memory_space=pltpu.VMEM)
    smem = pl.BlockSpec(memory_space=pltpu.SMEM)
    return pl.pallas_call(
        front_kernel,
        out_shape=(
            jax.ShapeDtypeStruct((rows, full), BF16),
            jax.ShapeDtypeStruct((chunks, total_rows, width), BF16),
            jax.ShapeDtypeStruct((total_rows, local), BF16),
            jax.ShapeDtypeStruct((1, total_rows), F32),
            jax.ShapeDtypeStruct((3 * query.shape[0],), jnp.int32),
        ),
        in_specs=[smem, vmem, vmem, vmem, vmem],
        out_specs=[vmem, pl.BlockSpec(memory_space=pl.ANY), vmem, vmem, smem],
        scratch_shapes=[
            pltpu.VMEM((full, local), BF16),
            pltpu.VMEM((chunks, 2, SIDE * SIDE, rows // BLK, BLK, width // 2), BF16),
            pltpu.VMEM((SIDE * SIDE, rows // BLK, BLK, width), BF16),
            pltpu.VMEM((2, total_rows, width), BF16),
            pltpu.SemaphoreType.DMA((2,)),
            pltpu.VMEM((total_rows, local), F32),
            pltpu.VMEM((total_rows, HEAD), F32),
            pltpu.SemaphoreType.DMA((chunks, 2 * Spread.MESSAGES)),
            pltpu.SemaphoreType.DMA((chunks, 2 * Spread.MESSAGES)),
            *Flow.scratch(rows, tok, full, per_chunk),
        ],
        compiler_params=pltpu.CompilerParams(
            collective_id=ident, has_side_effects=True, vmem_limit_bytes=VMEM_LIMIT
        ),
        name="front",
    )(keep, query, key, value, weights)


QB = 256
KB = 512


def causal_kernel(
    dest, keep, qkv, scale, cot, gathered, q_in, k_in, v_in, out, d_all, grads, rest,
    rows_in, rows_sem, d_all_t, v_t, k_t, do_own, do_t, p_buf, dk_acc, dv_acc, dq_t, *scratch,
):
    kept = dest.shape[1]
    total_rows = qkv.shape[0]
    per_shard = q_in.shape[0]
    sel = [at for each in near_ranks(keep, per_shard) for at in picked(each, range(per_shard // 2, per_shard))]
    blocks = total_rows // QB
    rows_copy = pltpu.make_async_copy(gathered, rows_in, rows_sem)
    rows_copy.start()
    flow = Flow(sel, q_in, k_in, v_in, rest, scratch)
    flow.begin(3)

    for j in range(kept):
        do_own[j * BLK : (j + 1) * BLK, :] = cot[dest[0, j]]

    def prepare(c, carry):
        at = pl.ds(pl.multiple_of(c * QB, QB), QB)
        k_t[:, at] = qkv[at, HEAD : 2 * HEAD].T
        v_t[:, at] = qkv[at, 2 * HEAD : 3 * HEAD].T
        do_t[:, at] = do_own[at, :].T
        return carry

    lax.fori_loop(0, blocks, prepare, 0)
    dk_acc[...] = jnp.zeros_like(dk_acc)
    dv_acc[...] = jnp.zeros_like(dv_acc)

    def query_block(i):
        rows = pl.ds(pl.multiple_of(i * QB, QB), QB)
        chunks = (i * QB + QB + KB - 1) // KB
        q_i = qkv[rows, :HEAD]
        do_i = do_own[rows, :]

        def scores_of(c, masked):
            keys = pl.ds(pl.multiple_of(c * KB, KB), KB)
            scores = lax.dot_general(qkv[keys, HEAD : 2 * HEAD], q_i, NT, preferred_element_type=F32)
            if masked:
                key_at = lax.broadcasted_iota(jnp.int32, (KB, QB), 0)
                row_at = lax.broadcasted_iota(jnp.int32, (KB, QB), 1)
                scores = jnp.where(key_at - row_at <= i * QB - (chunks - 1) * KB, scores, LOW)
            p_buf[keys, :] = scores
            return jnp.max(scores, axis=0, keepdims=True)

        top = lax.fori_loop(
            0, chunks - 1, lambda c, m: jnp.maximum(m, scores_of(c, False)), scores_of(chunks - 1, True)
        )

        def weigh(c, carry):
            total, acc = carry
            keys = pl.ds(pl.multiple_of(c * KB, KB), KB)
            weight = jnp.exp2((p_buf[keys, :] - top) * SCALE2)
            p_buf[keys, :] = weight
            total = total + jnp.sum(weight, axis=0, keepdims=True)
            acc = acc + jnp.dot(v_t[:, keys], weight.astype(BF16), preferred_element_type=F32)
            return total, acc

        total, acc = lax.fori_loop(
            0, chunks, weigh, (jnp.zeros((1, QB), F32), jnp.zeros((HEAD, QB), F32))
        )
        inv = 1.0 / total
        o_t = acc * inv
        delta = jnp.sum(o_t * do_t[:, rows].astype(F32), axis=0, keepdims=True)
        out[rows, :] = o_t.T.astype(BF16)

        def back(c, acc):
            keys = pl.ds(pl.multiple_of(c * KB, KB), KB)
            soft = p_buf[keys, :] * inv
            dv_acc[keys, :] += jnp.dot(soft.astype(BF16), do_i, preferred_element_type=F32)
            d_probs = lax.dot_general(qkv[keys, 2 * HEAD :], do_i, NT, preferred_element_type=F32)
            d_scores = (soft * (d_probs - delta) * SCALE).astype(BF16)
            dk_acc[keys, :] += jnp.dot(d_scores, q_i, preferred_element_type=F32)
            return acc + jnp.dot(k_t[:, keys], d_scores, preferred_element_type=F32)

        dq_t[:, rows] = lax.fori_loop(0, chunks, back, jnp.zeros((HEAD, QB), F32))

    def finish(c, carry):
        at = pl.ds(pl.multiple_of(c * QB, QB), QB)
        d_q = dq_t[:, at]
        d_all_t[:HEAD, at] = (d_q * scale[:, at]).astype(BF16)
        d_all[at, :HEAD] = d_q.T.astype(BF16)
        for which, acc in ((1, dk_acc), (2, dv_acc)):
            value = acc[at, :]
            d_all[at, which * HEAD : (which + 1) * HEAD] = value.astype(BF16)
            d_all_t[which * HEAD : (which + 1) * HEAD, at] = (value.T * scale[:, at]).astype(BF16)
        return carry

    def weight_block(g, carry):
        wide = rows_in.shape[2]
        at = pl.ds(pl.multiple_of(g * wide, wide), wide)
        value = jnp.dot(d_all_t[...], rows_in[g], preferred_element_type=F32)
        for which in range(3):
            grads[which, at, :] = value[which * HEAD : (which + 1) * HEAD, :].T.astype(BF16)
        return carry

    col_blocks = rows_in.shape[0]
    lag = 2
    share = (col_blocks + 3 * lag - 2) // (3 * lag - 1)

    def step(t, carry):
        flow.step(t, lag)

        @pl.when(t < blocks)
        def _():
            query_block(blocks - 1 - t)

        @pl.when(t == blocks)
        def _():
            lax.fori_loop(0, blocks, finish, 0)
            rows_copy.wait()

        @pl.when(t >= blocks)
        def _():
            low = (t - blocks) * share
            lax.fori_loop(low, jnp.minimum(low + share, col_blocks), weight_block, 0)

        return carry

    lax.fori_loop(0, blocks + 3 * lag, step, 0)
    flow.drain()


def causal(dest, keep, qkv, scale, cot, gathered, query, key, value, per_chunk, ident):
    total_rows, local = qkv.shape
    tok, full = key.shape
    rows = query.shape[0] // 2 * BLK
    vmem = pl.BlockSpec(memory_space=pltpu.VMEM)
    smem = pl.BlockSpec(memory_space=pltpu.SMEM)
    return pl.pallas_call(
        causal_kernel,
        out_shape=(
            jax.ShapeDtypeStruct((total_rows, HEAD), BF16),
            jax.ShapeDtypeStruct((total_rows, local), BF16),
            jax.ShapeDtypeStruct((3, full, HEAD), BF16),
            jax.ShapeDtypeStruct((rows, full), BF16),
        ),
        in_specs=[smem, smem, vmem, vmem, vmem, pl.BlockSpec(memory_space=pl.ANY), vmem, vmem, vmem],
        out_specs=[vmem, vmem, vmem, vmem],
        scratch_shapes=[
            pltpu.VMEM(gathered.shape, BF16),
            pltpu.SemaphoreType.DMA,
            pltpu.VMEM((local, total_rows), BF16),
            pltpu.VMEM((HEAD, total_rows), BF16),
            pltpu.VMEM((HEAD, total_rows), BF16),
            pltpu.VMEM((total_rows, HEAD), BF16),
            pltpu.VMEM((HEAD, total_rows), BF16),
            pltpu.VMEM((total_rows, QB), F32),
            pltpu.VMEM((total_rows, HEAD), F32),
            pltpu.VMEM((total_rows, HEAD), F32),
            pltpu.VMEM((HEAD, total_rows), F32),
            *Flow.scratch(rows, tok, full, per_chunk),
        ],
        compiler_params=pltpu.CompilerParams(
            collective_id=ident, has_side_effects=True, vmem_limit_bytes=VMEM_LIMIT
        ),
        cost_estimate=pl.CostEstimate(
            flops=20 * 10**9, bytes_accessed=32 * 1024 * 1024, transcendentals=0
        ),
        name="causal",
    )(dest, keep, qkv, scale, cot, gathered, query, key, value)


class Reduce:
    def __init__(self, value, pair_got, own, snd, got1, got2, whole, send_sem, recv_sem):
        self.value, self.pair_got, self.own, self.snd = value, pair_got, own, snd
        self.got1, self.got2, self.whole = got1, got2, whole
        self.send_sem, self.recv_sem = send_sem, recv_sem
        at = lax.axis_index("dp")
        self.y, self.core = at // 2, lax.rem(at, 2)
        self.partner = self.y * 2 + 1 - self.core
        self.next = [self.turn(by) * 2 + self.core for by in (1, -1)]
        middle = value.shape[3] // 2
        self.halves = (slice(0, middle), slice(middle, 2 * middle))

    def turn(self, by):
        return lax.rem(self.y + by + SIDE, SIDE)

    def copy(self, which, src, dst, target):
        return pltpu.make_async_remote_copy(
            src_ref=src, dst_ref=dst, send_sem=self.send_sem.at[which], recv_sem=self.recv_sem.at[which],
            device_id={"dp": target}, device_id_type=MESH,
        )

    def pair(self):
        return self.copy(0, self.value.at[:, 1 - self.core], self.pair_got, self.partner)

    def ring1(self, d):
        return self.copy(1 + d, self.snd.at[d, 0, :, self.halves[0]], self.got1.at[d], self.next[d])

    def ring2(self, d):
        return self.copy(3 + d, self.snd.at[d, 1], self.got2.at[d], self.next[d])

    def quarter(self, by, half=None):
        ref = self.whole.at[:, self.core, self.turn(by)]
        return ref if half is None else self.whole.at[:, self.core, self.turn(by), self.halves[half]]

    def spread1(self, d, by):
        return self.copy(5 + d, self.quarter(by), self.quarter(by), self.next[d])

    def spread2(self, d, by):
        return self.copy(7 + d, self.quarter(by, d), self.quarter(by, d), self.next[d])

    def back(self, core):
        return self.copy(9, self.whole.at[:, core], self.whole.at[:, core], self.partner)

    def stage1(self):
        self.pair().wait_recv()

        def add(q, carry):
            self.own[q] = self.value[:, self.core, q].astype(F32) + self.pair_got[:, q].astype(F32)
            return carry

        lax.fori_loop(0, SIDE, add, 0)
        for d in range(2):
            self.snd[d, 0, :, self.halves[0]] = self.own[self.turn(2), :, self.halves[d]].astype(BF16)
            self.ring1(d).start()

    def stage2(self):
        for d in range(2):
            self.ring1(d).wait_recv()
            near = self.turn(1 - 2 * d)
            self.snd[d, 1, :, self.halves[1 - d]] = self.own[near, :, self.halves[1 - d]].astype(BF16)
            self.snd[d, 1, :, self.halves[d]] = (
                self.own[near, :, self.halves[d]] + self.got1[d].astype(F32)
            ).astype(BF16)
            self.ring2(d).start()

    def stage3(self):
        for d in range(2):
            self.ring2(d).wait_recv()
        total = self.own[self.y] + self.got2[0].astype(F32) + self.got2[1].astype(F32)
        self.whole[:, self.core, self.y] = total.astype(BF16)
        for d in range(2):
            self.spread1(d, 0).start()

    def stage4(self):
        for d in range(2):
            self.spread1(d, 2 * d - 1).wait_recv()
            self.spread2(d, 2 * d - 1).start()

    def stage5(self):
        for d in range(2):
            self.spread2(d, 2).wait_recv()
        self.back(self.core).start()

    def stage6(self, out):
        self.back(1 - self.core).wait_recv()
        out[...] = self.whole[...]
        self.pair().wait_send()
        for d in range(2):
            self.ring1(d).wait_send()
            self.ring2(d).wait_send()
            self.spread1(d, 0).wait_send()
            self.spread2(d, 2 * d - 1).wait_send()
        self.back(self.core).wait_send()

    @staticmethod
    def scratch(shape):
        three, _, quarters, rows, width = shape
        return [
            pltpu.VMEM((three, quarters, rows, width), BF16),
            pltpu.VMEM((quarters, three, rows, width), F32),
            pltpu.VMEM((2, 2, three, rows, width), BF16),
            pltpu.VMEM((2, three, rows // 2, width), BF16),
            pltpu.VMEM((2, three, rows, width), BF16),
            pltpu.VMEM(shape, BF16),
            pltpu.SemaphoreType.DMA((10,)),
            pltpu.SemaphoreType.DMA((10,)),
        ]


def scatter_kernel(
    dest, d_all, three, value, out, summed, slot_at, weights, terms, got1, snd2, got2, sums, last1, lasts2, last2,
    send1, recv1, send2, recv2, send3, recv3, send4, recv4, *reduce_scratch,
):
    shard = lax.axis_index(SEQ)
    row, col = shard // SIDE, lax.rem(shard, SIDE)
    wide = out.shape[1] // 2
    part = wide // 2
    place = ((row, col), (col, row))
    halves = (slice(0, part), slice(part, wide))

    def turn(at, by):
        return lax.rem(at + by + SIDE, SIDE)

    def slot(h, a, b):
        return a * SIDE + b if h == 0 else b * SIDE + a

    barrier = pltpu.get_barrier_semaphore()
    for by in (1, -1):
        for h in range(2):
            a, b = place[h]
            pl.semaphore_signal(
                barrier, inc=1, device_id={SEQ: slot(h, turn(a, by), b)}, device_id_type=MESH
            )
    kept = dest.shape[1]
    for at in range(kept):
        slot_at[at] = functools.reduce(lambda got, j: jnp.where(dest[0, j] == at, j, got), range(kept), 0)
    reduce = Reduce(value, *reduce_scratch)
    for target in (reduce.partner, *reduce.next):
        pl.semaphore_signal(barrier, inc=1, device_id={"dp": target}, device_id_type=MESH)
    for which in range(3):
        weights[:, which * HEAD : (which + 1) * HEAD] = three[which]

    def group(h, a):
        slots = [jnp.where(h == 0, a * SIDE + s, s * SIDE + a) for s in range(SIDE)]
        rows = jnp.concatenate([d_all[slot_at[one]] for one in slots], axis=0)
        cols = pl.ds(pl.multiple_of(h * wide, wide), wide)
        value = lax.dot_general(rows, weights[cols, :], NT, preferred_element_type=F32).astype(BF16)
        for s in range(SIDE):
            terms[h, a, s] = value[s * BLK : (s + 1) * BLK, :]

    def first_send(h, d, s):
        a, b = place[h]
        return pltpu.make_async_remote_copy(
            src_ref=terms.at[h, turn(a, 2), s, :, halves[d]], dst_ref=got1.at[h, d, s],
            send_sem=send1.at[h, d, s], recv_sem=recv1.at[h, d, s],
            device_id={SEQ: slot(h, turn(a, 1 - 2 * d), b)}, device_id_type=MESH,
        )

    def second_send(h, d, s):
        a, b = place[h]
        return pltpu.make_async_remote_copy(
            src_ref=snd2.at[h, d, s], dst_ref=got2.at[h, d, s],
            send_sem=send2.at[h, d, s], recv_sem=recv2.at[h, d, s],
            device_id={SEQ: slot(h, turn(a, 1 - 2 * d), b)}, device_id_type=MESH,
        )

    def third_send(h, d):
        a, b = place[h]
        return pltpu.make_async_remote_copy(
            src_ref=sums.at[h, turn(b, 2), :, halves[d]], dst_ref=last1.at[h, d],
            send_sem=send3.at[h, d], recv_sem=recv3.at[h, d],
            device_id={SEQ: slot(h, a, turn(b, 1 - 2 * d))}, device_id_type=MESH,
        )

    def fourth_send(h, d):
        a, b = place[h]
        return pltpu.make_async_remote_copy(
            src_ref=lasts2.at[h, d], dst_ref=last2.at[h, d],
            send_sem=send4.at[h, d], recv_sem=recv4.at[h, d],
            device_id={SEQ: slot(h, a, turn(b, 1 - 2 * d))}, device_id_type=MESH,
        )

    def group_far(h, carry):
        group(h, turn(jnp.where(h == 0, row, col), 2))
        return carry

    def group_rest(g, carry):
        h, which = lax.rem(g, 2), g // 2
        by = jnp.where(which == 0, 1, jnp.where(which == 1, SIDE - 1, 0))
        group(h, turn(jnp.where(h == 0, row, col), by))
        return carry

    lax.fori_loop(0, 2, group_far, 0)
    pl.semaphore_wait(barrier, 7)
    reduce.pair().start()
    for k in (2, 1, 3, 0):
        for h in range(2):
            s = turn(place[h][1], k)
            for d in range(2):
                first_send(h, d, s).start()
    lax.fori_loop(0, 2, group_rest, 0)
    reduce.stage1()
    lax.fori_loop(2, 6, group_rest, 0)
    reduce.stage2()
    for k in (2, 1, 3, 0):
        for h in range(2):
            a, b = place[h]
            s = turn(b, k)
            for d in range(2):
                first_send(h, d, s).wait_recv()
                near = turn(a, 1 - 2 * d)
                other = halves[1 - d]
                snd2[h, d, s, :, other] = terms[h, near, s, :, other]
                snd2[h, d, s, :, halves[d]] = (
                    terms[h, near, s, :, halves[d]].astype(F32) + got1[h, d, s].astype(F32)
                ).astype(BF16)
                second_send(h, d, s).start()
    reduce.stage3()
    for k in (2, 1, 3, 0):
        for h in range(2):
            a, b = place[h]
            s = turn(b, k)
            for d in range(2):
                second_send(h, d, s).wait_recv()
            total = (
                terms[h, a, s].astype(F32) + got2[h, 0, s].astype(F32) + got2[h, 1, s].astype(F32)
            )
            if k != 0:
                sums[h, s] = total.astype(BF16)
            if k == 2:
                for d in range(2):
                    third_send(h, d).start()
            elif k != 0:
                d = 0 if k == 1 else 1
                third_send(h, d).wait_recv()
                other = halves[1 - d]
                lasts2[h, d, :, other] = sums[h, s, :, other]
                lasts2[h, d, :, halves[d]] = (total[:, halves[d]] + last1[h, d].astype(F32)).astype(BF16)
                fourth_send(h, d).start()
            else:
                for d in range(2):
                    fourth_send(h, d).wait_recv()
                out[:, h * wide : (h + 1) * wide] = (
                    total + last2[h, 0].astype(F32) + last2[h, 1].astype(F32)
                ).astype(BF16)
        if k == 2:
            reduce.stage4()
        elif k == 1:
            reduce.stage5()
        elif k == 3:
            reduce.stage6(summed)
    for h in range(2):
        for d in range(2):
            for s in range(SIDE):
                first_send(h, d, s).wait_send()
                second_send(h, d, s).wait_send()
            third_send(h, d).wait_send()
            fourth_send(h, d).wait_send()


def scatter_terms(dest, d_all, three, value, ident):
    blocks, _, local = d_all.shape
    full = three.shape[1]
    wide = full // 2
    part = wide // 2
    vmem = pl.BlockSpec(memory_space=pltpu.VMEM)
    four = pltpu.SemaphoreType.DMA((2, 2, SIDE))
    two = pltpu.SemaphoreType.DMA((2, 2))
    return pl.pallas_call(
        scatter_kernel,
        out_shape=(jax.ShapeDtypeStruct((BLK, full), BF16), jax.ShapeDtypeStruct(value.shape, BF16)),
        in_specs=[pl.BlockSpec(memory_space=pltpu.SMEM), vmem, vmem, vmem],
        out_specs=[vmem, vmem],
        scratch_shapes=[
            pltpu.SMEM((blocks,), jnp.int32),
            pltpu.VMEM((full, local), BF16),
            pltpu.VMEM((2, SIDE, SIDE, BLK, wide), BF16),
            pltpu.VMEM((2, 2, SIDE, BLK, part), BF16),
            pltpu.VMEM((2, 2, SIDE, BLK, wide), BF16),
            pltpu.VMEM((2, 2, SIDE, BLK, wide), BF16),
            pltpu.VMEM((2, SIDE, BLK, wide), BF16),
            pltpu.VMEM((2, 2, BLK, part), BF16),
            pltpu.VMEM((2, 2, BLK, wide), BF16),
            pltpu.VMEM((2, 2, BLK, wide), BF16),
            four, four, four, four, two, two, two, two,
            *Reduce.scratch(value.shape),
        ],
        compiler_params=pltpu.CompilerParams(
            collective_id=ident, has_side_effects=True, vmem_limit_bytes=VMEM_LIMIT
        ),
        cost_estimate=pl.CostEstimate(
            flops=2 * blocks * BLK * local * full, bytes_accessed=100 * 1024 * 1024, transcendentals=0
        ),
        name="scatter_terms",
    )(dest, d_all, three, value)


def assemble_kernel(dest, table, head, rest, sorted_out, summed, out, causal_out, grads):
    kept = sorted_out.shape[0] // BLK
    late = table[3 * pl.program_id(0)] == 1
    grads[...] = summed[...].astype(F32)

    @pl.when(pl.program_id(0) == 0)
    def _():
        for j in range(kept):
            causal_out[pl.ds(pl.multiple_of(dest[j] * BLK, BLK), BLK), :] = sorted_out[j * BLK : (j + 1) * BLK, :]

    @pl.when(late)
    def _():
        out[...] = rest[...]

    @pl.when(jnp.logical_not(late))
    def _():
        out[...] = head[...]


def assemble(dest, table, head, rest, sorted_out, summed):
    rows, full = head.shape
    steps = 2 * rows // BLK
    whole = pl.BlockSpec(sorted_out.shape, lambda g, d, t: (0, 0))
    part = pl.BlockSpec((3, full // steps, HEAD), lambda g, d, t: (0, g, 0))
    return pl.pallas_call(
        assemble_kernel,
        out_shape=(
            jax.ShapeDtypeStruct((2 * rows, full), BF16),
            jax.ShapeDtypeStruct(sorted_out.shape, BF16),
            jax.ShapeDtypeStruct(summed.shape, F32),
        ),
        grid_spec=pltpu.PrefetchScalarGridSpec(
            num_scalar_prefetch=2,
            grid=(steps,),
            in_specs=[
                pl.BlockSpec((BLK, full), lambda g, d, t: (t[3 * g + 1], 0)),
                pl.BlockSpec((BLK, full), lambda g, d, t: (t[3 * g + 2], 0)),
                whole,
                part,
            ],
            out_specs=[pl.BlockSpec((BLK, full), lambda g, d, t: (g, 0)), whole, part],
        ),
        compiler_params=pltpu.CompilerParams(vmem_limit_bytes=VMEM_LIMIT),
        name="assemble",
    )(dest, table, head, rest, sorted_out, summed)


def shards(query_input, key_input, value_input, keep_blocks, dest_slots, proj_weights, cotangent):
    tok, full = query_input.shape[1:]
    per_shard = tok // BLK
    kept = keep_blocks.shape[1]
    query = query_input.reshape(per_shard, BLK, full)
    key = key_input[0]
    value = value_input[0]
    first, gathered, qkv, scale, table = front(keep_blocks, query, key, value, proj_weights, 4, 0)
    sorted_out, d_all, local_grads, rest = causal(
        dest_slots, keep_blocks, qkv, scale, cotangent.reshape(kept, BLK, -1), gathered, query, key, value, 2, 1
    )
    row_grad, summed = scatter_terms(
        dest_slots, d_all.reshape(kept, BLK, -1), proj_weights,
        local_grads.reshape(3, 2, SIDE, full // 2 // SIDE, HEAD), 2,
    )
    window_out, causal_out, grads = assemble(
        dest_slots[0], table, first, rest, sorted_out, summed.reshape(proj_weights.shape)
    )
    return (window_out[None], causal_out[None], grads, row_grad[None])


def solution(mesh):
    return jax.shard_map(
        shards,
        mesh=mesh,
        in_specs=(
            P("dp", "seq", None),
            P("dp", "seq", None),
            P("dp", "seq", None),
            P("dp", None),
            P("dp", None),
            P(None, None, "seq"),
            P("dp", None, "seq"),
        ),
        out_specs=(
            P("dp", "seq", None),
            P("dp", None, "seq"),
            P(None, None, "seq"),
            P("dp", "seq", None),
        ),
        check_vma=False,
    )
```

```python
import functools

import jax
import jax.numpy as jnp
from jax import lax
from jax.experimental import pallas as pl
from jax.experimental.pallas import tpu as pltpu
from jax.sharding import PartitionSpec as P

HEAD = 128
BLK = 128
SEQ = "seq"
MESH = pl.DeviceIdType.MESH
SCALE = HEAD ** (-0.5)
LOG2E = 1.4426950408889634
SCALE2 = SCALE * LOG2E
LOW = -1e30
NT = (((1,), (1,)), ((), ()))
BF16 = jnp.bfloat16
F32 = jnp.float32
VMEM_LIMIT = 56 * 1024 * 1024


def window_parts(heads):
    def scores_of(query, key, value_t, bias):
        scores = lax.dot_general(key, query, NT, preferred_element_type=F32)
        if bias is not None:
            scores = scores + bias
        return scores, jnp.max(scores, axis=0, keepdims=True), value_t

    def rest_of(scores, top, value_t):
        weight = jnp.exp2((scores - top) * SCALE2)
        total = jnp.sum(weight, axis=0, keepdims=True)
        out = jnp.dot(value_t, weight.astype(BF16), preferred_element_type=F32)
        return out * (1.0 / total), top * SCALE2 + jnp.log2(total)

    done = []
    ahead = scores_of(*heads[0])
    for h in range(len(heads)):
        current = ahead
        if h + 1 < len(heads):
            ahead = scores_of(*heads[h + 1])
        done.append(rest_of(*current))
    return done


def merged(out_a, lse_a, out_b, lse_b):
    top = jnp.maximum(lse_a, lse_b)
    weight_a = jnp.exp2(lse_a - top)
    weight_b = jnp.exp2(lse_b - top)
    total = weight_a + weight_b
    return out_a * (weight_a / total) + out_b * (weight_b / total), top + jnp.log2(total)


def block_ranks(keep, shard, per_shard):
    kept = [
        functools.reduce(
            lambda found, j: jnp.where(keep[0, j] == shard * per_shard + b, 1, found), range(keep.shape[1]), 0
        )
        for b in range(per_shard)
    ]
    total = sum(kept)
    return [
        jnp.where(kept[b] == 1, sum(kept[:b], 0), total + b - sum(kept[:b], 0)) for b in range(per_shard)
    ]


def picked(ranks, places):
    return [functools.reduce(lambda got, b: jnp.where(ranks[b] == at, b, got), range(len(ranks)), 0) for at in places]


def near_ranks(keep, per_shard):
    shard, count = lax.axis_index(SEQ), lax.axis_size(SEQ)
    return [block_ranks(keep, lax.rem(shard + by, count), per_shard) for by in range(3)]


class Flow:
    def __init__(self, sel, q_in, k_in, v_in, out, scratch):
        (
            self.q_own, self.q_one, self.q_two, self.v_t, self.o_own, self.l_own, self.o_snd2, self.l_snd2,
            self.o_got2, self.l_got2, self.o_snd1, self.l_snd1, self.o_got1, self.l_got1,
            self.bias_own, self.bias_two, self.send_sem, self.recv_sem,
        ) = scratch
        self.sel, self.q_in, self.k_in, self.v_in, self.out = sel, q_in, k_in, v_in, out
        self.chunks, self.rows, self.width = self.q_own.shape
        self.per_chunk = self.width // HEAD
        self.lse_step = 8 // self.per_chunk
        self.shard = lax.axis_index(SEQ)
        count = lax.axis_size(SEQ)
        self.right = lax.rem(self.shard + 1, count)
        self.left = lax.rem(self.shard + count - 1, count)

    def copy(self, which, c, src, dst, target):
        return pltpu.make_async_remote_copy(
            src_ref=src.at[c], dst_ref=dst.at[c],
            send_sem=self.send_sem.at[which, c], recv_sem=self.recv_sem.at[which, c],
            device_id={SEQ: target}, device_id_type=MESH,
        )

    def hop_one(self, c):
        return self.copy(0, c, self.q_own, self.q_one, self.left)

    def hop_two(self, c):
        return self.copy(1, c, self.q_one, self.q_two, self.left)

    def back_two(self, c):
        return (
            self.copy(2, c, self.o_snd2, self.o_got2, self.right),
            self.copy(3, c, self.l_snd2, self.l_got2, self.right),
        )

    def back_one(self, c):
        return (
            self.copy(4, c, self.o_snd1, self.o_got1, self.right),
            self.copy(5, c, self.l_snd1, self.l_got1, self.right),
        )

    def begin(self, ahead, others=()):
        barrier = pltpu.get_barrier_semaphore()
        greeted = (self.left, self.right, *others)
        for neighbour in greeted:
            pl.semaphore_signal(barrier, inc=1, device_id={SEQ: neighbour}, device_id_type=MESH)
        picks = self.rows // BLK
        for a in range(picks):
            block = self.q_in[self.sel[a]]
            for c in range(self.chunks):
                self.q_own[c, a * BLK : (a + 1) * BLK, :] = block[:, c * self.width : (c + 1) * self.width]
        pl.semaphore_wait(barrier, len(greeted))
        for c in range(ahead):
            self.hop_one(c).start()
        self.ahead = ahead
        lane = lax.broadcasted_iota(jnp.int32, (1, self.rows), 1)
        key_at = lax.broadcasted_iota(jnp.int32, self.bias_own.shape, 0)
        for base, ref in ((0, self.bias_own), (2 * picks, self.bias_two)):
            place = lane
            for a in range(picks):
                place = jnp.where(lane // BLK == a, (lane - a * BLK) + self.sel[base + a] * BLK, place)
            seen = (key_at <= place) if base == 0 else (key_at > place)
            ref[...] = jnp.where(seen, 0.0, LOW)

    def cols(self, c, h):
        return pl.ds(pl.multiple_of(c * self.width + h * HEAD, HEAD), HEAD)

    def lse_at(self, h):
        return slice(h * self.lse_step, (h + 1) * self.lse_step)

    def spread(self, row):
        return jnp.broadcast_to(row, (self.lse_step, self.rows))

    def head(self, h):
        return slice(h * HEAD, (h + 1) * HEAD)

    def pump(self, c):
        self.hop_one(c).wait_recv()
        self.hop_two(c).start()

        @pl.when(c + self.ahead < self.chunks)
        def _():
            self.hop_one(c + self.ahead).start()

    def own(self, c):
        heads = []
        for h in range(self.per_chunk):
            cols = self.cols(c, h)
            value_t = self.v_in[:, cols].T
            self.v_t[cols, :] = value_t
            heads.append((self.q_own[c, :, self.head(h)], self.k_in[:, cols], value_t, self.bias_own[...]))
        for h, (part, lse) in enumerate(window_parts(heads)):
            self.o_own[c, self.head(h), :] = part
            self.l_own[c, self.lse_at(h), :] = self.spread(lse)

    def two(self, c):
        self.hop_two(c).wait_recv()
        heads = [
            (self.q_two[c, :, self.head(h)], self.k_in[:, self.cols(c, h)], self.v_t[self.cols(c, h), :], self.bias_two[...])
            for h in range(self.per_chunk)
        ]
        for h, (part, lse) in enumerate(window_parts(heads)):
            self.o_snd2[c, self.head(h), :] = part.astype(BF16)
            self.l_snd2[c, self.lse_at(h), :] = self.spread(lse)
        for each in self.back_two(c):
            each.start()

    def incoming(self, got, h, c):
        first = h * self.lse_step
        return jnp.where(self.shard == 0, LOW, got[c, first : first + 1, :])

    def one(self, c):
        parts = window_parts([
            (self.q_one[c, :, self.head(h)], self.k_in[:, self.cols(c, h)], self.v_t[self.cols(c, h), :], None)
            for h in range(self.per_chunk)
        ])
        for each in self.back_two(c):
            each.wait_recv()
        for h in range(self.per_chunk):
            part, lse = merged(
                *parts[h], self.o_got2[c, self.head(h), :].astype(F32), self.incoming(self.l_got2, h, c)
            )
            self.o_snd1[c, self.head(h), :] = part.astype(BF16)
            self.l_snd1[c, self.lse_at(h), :] = self.spread(lse)
        for each in self.back_one(c):
            each.start()

    def final(self, c):
        for each in self.back_one(c):
            each.wait_recv()
        for h in range(self.per_chunk):
            first = h * self.lse_step
            part, _ = merged(
                self.o_own[c, self.head(h), :], self.l_own[c, first : first + 1, :],
                self.o_got1[c, self.head(h), :].astype(F32), self.incoming(self.l_got1, h, c),
            )
            self.store(c, h, part.T.astype(BF16))

    def store(self, c, h, value):
        self.out[:, self.cols(c, h)] = value

    def step(self, t, lag):
        def stage(late, *calls):
            @pl.when((t >= late) & (t < self.chunks + late))
            def _():
                for call in calls:
                    call(t - late)

        stage(0, self.pump, self.own)
        stage(lag, self.two)
        stage(2 * lag, self.one)
        stage(3 * lag, self.final)

    def drain(self):
        def body(c, carry):
            self.hop_one(c).wait_send()
            self.hop_two(c).wait_send()
            for each in self.back_two(c) + self.back_one(c):
                each.wait_send()
            return carry

        lax.fori_loop(0, self.chunks, body, 0)

    @staticmethod
    def scratch(rows, tok, full, per_chunk):
        width = per_chunk * HEAD
        chunks = full // width
        queries = pltpu.VMEM((chunks, rows, width), BF16)
        outs = pltpu.VMEM((chunks, width, rows), BF16)
        lses = pltpu.VMEM((chunks, 8, rows), F32)
        return [
            queries, queries, queries, pltpu.VMEM((full, tok), BF16), pltpu.VMEM((chunks, width, rows), F32), lses,
            outs, lses, outs, lses, outs, lses, outs, lses,
            pltpu.VMEM((tok, rows), F32), pltpu.VMEM((tok, rows), F32),
            pltpu.SemaphoreType.DMA((6, chunks)), pltpu.SemaphoreType.DMA((6, chunks)),
        ]


SIDE = 4


class Spread:
    OFFSETS = (0, 1, SIDE - 1, 2)
    MESSAGES = 20

    def __init__(self, got, send_sem, recv_sem):
        self.got, self.send_sem, self.recv_sem = got, send_sem, recv_sem
        shard = lax.axis_index(SEQ)
        row, col = shard // SIDE, lax.rem(shard, SIDE)
        self.here = ((col, row), (row, col))

    @staticmethod
    def turn(at, by):
        return lax.rem(at + by + SIDE, SIDE)

    @staticmethod
    def slot(kind, place):
        a, b = place
        return b * SIDE + a if kind == 0 else a * SIDE + b

    def neighbours(self):
        a, b = self.here[0]
        return [self.slot(0, (self.turn(a, by), b)) for by in (1, -1)] + [
            self.slot(0, (a, self.turn(b, by))) for by in (1, -1)
        ]

    def message(self, c, kind, which, place, half, target):
        slot = self.slot(kind, place)
        ref = self.got.at[c, kind, slot] if half is None else self.got.at[c, kind, slot, half]
        at = kind * self.MESSAGES + which
        return pltpu.make_async_remote_copy(
            src_ref=ref, dst_ref=ref, send_sem=self.send_sem.at[c, at], recv_sem=self.recv_sem.at[c, at],
            device_id={SEQ: self.slot(kind, target)}, device_id_type=MESH,
        )

    def first(self, c, kind, what):
        a, b = self.here[kind]
        up, down = (self.turn(a, 1), b), (self.turn(a, -1), b)
        return self.four(c, kind, 0, (a, b), up, down, (self.turn(a, 2), b), up, down, what)

    def second(self, c, kind, k, what):
        a, b = self.here[kind]
        origin = self.turn(a, self.OFFSETS[k])
        return self.four(
            c, kind, 4 + 4 * k, (origin, b), (origin, self.turn(b, 1)), (origin, self.turn(b, -1)),
            (origin, self.turn(b, 2)), (a, self.turn(b, 1)), (a, self.turn(b, -1)), what,
        )

    def four(self, c, kind, base, here, up, down, far, to_up, to_down, what):
        pairs = {
            "send": ((base, here, None, to_up), (base + 1, here, None, to_down)),
            "came": ((base, down, None, to_up), (base + 1, up, None, to_down)),
            "pass": ((base + 2, down, 0, to_up), (base + 3, up, 1, to_down)),
            "last": ((base + 2, far, 0, to_up), (base + 3, far, 1, to_down)),
        }[what]
        return [self.message(c, kind, *pair) for pair in pairs]

    def launch(self, c):
        for kind in range(2):
            for each in self.first(c, kind, "send"):
                each.start()

    def relay(self, c):
        for kind in range(2):
            for each in self.first(c, kind, "came"):
                each.wait_recv()
            for each in self.first(c, kind, "pass"):
                each.start()
            for k in range(3):
                for each in self.second(c, kind, k, "send"):
                    each.start()

    def relay_far(self, c):
        for kind in range(2):
            for each in self.first(c, kind, "last"):
                each.wait_recv()
            for each in self.second(c, kind, 3, "send"):
                each.start()

    def second_relay(self, c):
        for k in range(4):
            for kind in range(2):
                for each in self.second(c, kind, k, "came"):
                    each.wait_recv()
                for each in self.second(c, kind, k, "pass"):
                    each.start()

    def settle(self, c):
        for k in range(4):
            for kind in range(2):
                for each in self.second(c, kind, k, "last"):
                    each.wait_recv()

    def drain(self, c):
        for kind in range(2):
            for what in ("send", "pass"):
                for each in self.first(c, kind, what):
                    each.wait_send()
                for k in range(4):
                    for each in self.second(c, kind, k, what):
                        each.wait_send()


def front_kernel(
    keep, q_in, k_in, v_in, three, out, rows_out, projected, scale_out, table,
    weights, got, held, staged, staged_sem, total, squares, spread_send, spread_recv, *scratch,
):
    kept = keep.shape[1]
    per_shard = q_in.shape[0]
    ranks = near_ranks(keep, per_shard)
    half = per_shard // 2
    sel = [at for each in ranks for at in picked(each, range(half))]
    for b in range(per_shard):
        late = jnp.where(ranks[0][b] >= half, 1, 0)
        table[3 * b] = late
        table[3 * b + 1] = ranks[0][b] * (1 - late)
        table[3 * b + 2] = (ranks[0][b] - half) * late
    owner = [keep[0, j] // per_shard for j in range(kept)]
    nth = [0] + [jnp.where(owner[j] == owner[j - 1], 1, 0) for j in range(1, kept)]
    flow = Flow(sel, q_in, k_in, v_in, out, scratch)
    spread = Spread(got, spread_send, spread_recv)
    chunks, width = flow.chunks, flow.width
    total_rows, local = projected.shape
    full = k_in.shape[1]
    block = 512
    per_kind = flow.per_chunk // 2

    def store(c, h, value):
        out[:, flow.cols(c, h)] = value
        for a in range(flow.rows // BLK):
            got[c, h // per_kind, flow.shard, a, :, flow.head(h % per_kind)] = value[a * BLK : (a + 1) * BLK, :]

    flow.store = store
    flow.begin(3, spread.neighbours())
    for which in range(3):
        weights[:, which * HEAD : (which + 1) * HEAD] = three[which]
    total[...] = jnp.zeros_like(total)
    squares[...] = jnp.zeros_like(squares)

    def staged_copy(c):
        which = lax.rem(c, 2)
        return pltpu.make_async_copy(staged.at[which], rows_out.at[c], staged_sem.at[which])

    def project_chunk(c):
        which = lax.rem(c, 2)

        @pl.when(c >= 2)
        def _():
            staged_copy(c - 2).wait()

        def hold(i, carry):
            for kind in range(2):
                held[i, :, :, kind * width // 2 : (kind + 1) * width // 2] = got[c, kind, i]
            return carry

        lax.fori_loop(0, SIDE * SIDE, hold, 0)

        for j in range(kept):
            staged[which, j * BLK : (j + 1) * BLK, :] = held[owner[j], nth[j]]
        staged_copy(c).start()
        weight = weights[pl.ds(pl.multiple_of(c * width, width), width), :]

        def multiply(r, carry):
            at = pl.ds(pl.multiple_of(r * block, block), block)
            rows = staged[which, at, :]
            total[at, :] += jnp.dot(rows, weight, preferred_element_type=F32)
            wide = rows.astype(F32)
            square = wide * wide
            squares[at, :] += sum(square[:, h * HEAD : (h + 1) * HEAD] for h in range(flow.per_chunk))
            return carry

        lax.fori_loop(0, total_rows // block, multiply, 0)

    def step(t, carry):
        flow.step(t, 1)

        def stage(late, call):
            @pl.when((t >= late) & (t < chunks + late))
            def _():
                call(t - late)

        stage(3, spread.launch)
        stage(4, spread.relay)
        stage(5, spread.relay_far)
        stage(6, spread.second_relay)

        @pl.when(t >= 7)
        def _():
            spread.settle(t - 7)
            project_chunk(t - 7)

        return carry

    lax.fori_loop(0, chunks + 7, step, 0)

    def finish(r, carry):
        at = pl.ds(pl.multiple_of(r * block, block), block)
        square = squares[at, :]
        inv = lax.rsqrt(jnp.sum(square, axis=1, keepdims=True) * (1.0 / full) + 1e-06)
        projected[at, :] = (total[at, :] * inv).astype(BF16)
        scale_out[:, at] = lax.rsqrt(jnp.sum(square.T, axis=0, keepdims=True) * (1.0 / full) + 1e-06)
        return carry

    lax.fori_loop(0, total_rows // block, finish, 0)

    def drain(c, carry):
        spread.drain(c)
        return carry

    lax.fori_loop(0, chunks, drain, 0)
    for c in (chunks - 2, chunks - 1):
        staged_copy(c).wait()
    flow.drain()


def front(keep, query, key, value, weights, per_chunk, ident):
    tok, full = key.shape
    local = 3 * HEAD
    rows = query.shape[0] // 2 * BLK
    total_rows = keep.shape[1] * BLK
    width = per_chunk * HEAD
    chunks = full // width
    vmem = pl.BlockSpec(memory_space=pltpu.VMEM)
    smem = pl.BlockSpec(memory_space=pltpu.SMEM)
    return pl.pallas_call(
        front_kernel,
        out_shape=(
            jax.ShapeDtypeStruct((rows, full), BF16),
            jax.ShapeDtypeStruct((chunks, total_rows, width), BF16),
            jax.ShapeDtypeStruct((total_rows, local), BF16),
            jax.ShapeDtypeStruct((1, total_rows), F32),
            jax.ShapeDtypeStruct((3 * query.shape[0],), jnp.int32),
        ),
        in_specs=[smem, vmem, vmem, vmem, vmem],
        out_specs=[vmem, pl.BlockSpec(memory_space=pl.ANY), vmem, vmem, smem],
        scratch_shapes=[
            pltpu.VMEM((full, local), BF16),
            pltpu.VMEM((chunks, 2, SIDE * SIDE, rows // BLK, BLK, width // 2), BF16),
            pltpu.VMEM((SIDE * SIDE, rows // BLK, BLK, width), BF16),
            pltpu.VMEM((2, total_rows, width), BF16),
            pltpu.SemaphoreType.DMA((2,)),
            pltpu.VMEM((total_rows, local), F32),
            pltpu.VMEM((total_rows, HEAD), F32),
            pltpu.SemaphoreType.DMA((chunks, 2 * Spread.MESSAGES)),
            pltpu.SemaphoreType.DMA((chunks, 2 * Spread.MESSAGES)),
            *Flow.scratch(rows, tok, full, per_chunk),
        ],
        compiler_params=pltpu.CompilerParams(
            collective_id=ident, has_side_effects=True, vmem_limit_bytes=VMEM_LIMIT
        ),
        name="front",
    )(keep, query, key, value, weights)


QB = 256
KB = 512


def causal_kernel(
    dest, keep, qkv, scale, cot, gathered, q_in, k_in, v_in, out, d_all, grads, rest,
    rows_in, rows_sem, d_all_t, v_t, k_t, do_own, do_t, p_buf, dk_acc, dv_acc, dq_t, *scratch,
):
    kept = dest.shape[1]
    total_rows = qkv.shape[0]
    per_shard = q_in.shape[0]
    sel = [at for each in near_ranks(keep, per_shard) for at in picked(each, range(per_shard // 2, per_shard))]
    blocks = total_rows // QB
    rows_copy = pltpu.make_async_copy(gathered, rows_in, rows_sem)
    rows_copy.start()
    flow = Flow(sel, q_in, k_in, v_in, rest, scratch)
    flow.begin(2)

    for j in range(kept):
        do_own[j * BLK : (j + 1) * BLK, :] = cot[dest[0, j]]

    def prepare(c, carry):
        at = pl.ds(pl.multiple_of(c * QB, QB), QB)
        k_t[:, at] = qkv[at, HEAD : 2 * HEAD].T
        v_t[:, at] = qkv[at, 2 * HEAD : 3 * HEAD].T
        do_t[:, at] = do_own[at, :].T
        return carry

    lax.fori_loop(0, blocks, prepare, 0)
    dk_acc[...] = jnp.zeros_like(dk_acc)
    dv_acc[...] = jnp.zeros_like(dv_acc)

    def query_block(i):
        rows = pl.ds(pl.multiple_of(i * QB, QB), QB)
        chunks = (i * QB + QB + KB - 1) // KB
        q_i = qkv[rows, :HEAD]
        do_i = do_own[rows, :]

        def scores_of(c, masked):
            keys = pl.ds(pl.multiple_of(c * KB, KB), KB)
            scores = lax.dot_general(qkv[keys, HEAD : 2 * HEAD], q_i, NT, preferred_element_type=F32)
            if masked:
                key_at = lax.broadcasted_iota(jnp.int32, (KB, QB), 0)
                row_at = lax.broadcasted_iota(jnp.int32, (KB, QB), 1)
                scores = jnp.where(key_at - row_at <= i * QB - (chunks - 1) * KB, scores, LOW)
            p_buf[keys, :] = scores
            return jnp.max(scores, axis=0, keepdims=True)

        top = lax.fori_loop(
            0, chunks - 1, lambda c, m: jnp.maximum(m, scores_of(c, False)), scores_of(chunks - 1, True)
        )

        def weigh(c, carry):
            total, acc = carry
            keys = pl.ds(pl.multiple_of(c * KB, KB), KB)
            weight = jnp.exp2((p_buf[keys, :] - top) * SCALE2)
            p_buf[keys, :] = weight
            total = total + jnp.sum(weight, axis=0, keepdims=True)
            acc = acc + jnp.dot(v_t[:, keys], weight.astype(BF16), preferred_element_type=F32)
            return total, acc

        total, acc = lax.fori_loop(
            0, chunks, weigh, (jnp.zeros((1, QB), F32), jnp.zeros((HEAD, QB), F32))
        )
        inv = 1.0 / total
        o_t = acc * inv
        delta = jnp.sum(o_t * do_t[:, rows].astype(F32), axis=0, keepdims=True)
        out[rows, :] = o_t.T.astype(BF16)

        def back(c, acc):
            keys = pl.ds(pl.multiple_of(c * KB, KB), KB)
            soft = p_buf[keys, :] * inv
            dv_acc[keys, :] += jnp.dot(soft.astype(BF16), do_i, preferred_element_type=F32)
            d_probs = lax.dot_general(qkv[keys, 2 * HEAD :], do_i, NT, preferred_element_type=F32)
            d_scores = (soft * (d_probs - delta) * SCALE).astype(BF16)
            dk_acc[keys, :] += jnp.dot(d_scores, q_i, preferred_element_type=F32)
            return acc + jnp.dot(k_t[:, keys], d_scores, preferred_element_type=F32)

        dq_t[:, rows] = lax.fori_loop(0, chunks, back, jnp.zeros((HEAD, QB), F32))

    def finish(c, carry):
        at = pl.ds(pl.multiple_of(c * QB, QB), QB)
        d_q = dq_t[:, at]
        d_all_t[:HEAD, at] = (d_q * scale[:, at]).astype(BF16)
        d_all[at, :HEAD] = d_q.T.astype(BF16)
        for which, acc in ((1, dk_acc), (2, dv_acc)):
            value = acc[at, :]
            d_all[at, which * HEAD : (which + 1) * HEAD] = value.astype(BF16)
            d_all_t[which * HEAD : (which + 1) * HEAD, at] = (value.T * scale[:, at]).astype(BF16)
        return carry

    def weight_block(g, carry):
        wide = rows_in.shape[2]
        at = pl.ds(pl.multiple_of(g * wide, wide), wide)
        value = jnp.dot(d_all_t[...], rows_in[g], preferred_element_type=F32)
        for which in range(3):
            grads[which, at, :] = value[which * HEAD : (which + 1) * HEAD, :].T.astype(BF16)
        return carry

    col_blocks = rows_in.shape[0]
    lag = 1
    per_step = blocks // flow.chunks
    share = (col_blocks + 3 * lag - 2) // (3 * lag - 1)

    def step(t, carry):
        flow.step(t, lag)

        @pl.when(t < flow.chunks)
        def _():
            def one_block(r, carry):
                query_block(blocks - 1 - t * per_step - r)
                return carry

            lax.fori_loop(0, per_step, one_block, 0)

        @pl.when(t == flow.chunks)
        def _():
            lax.fori_loop(0, blocks, finish, 0)
            rows_copy.wait()

        @pl.when(t >= flow.chunks)
        def _():
            low = (t - flow.chunks) * share
            lax.fori_loop(low, jnp.minimum(low + share, col_blocks), weight_block, 0)

        return carry

    lax.fori_loop(0, flow.chunks + 3 * lag, step, 0)
    flow.drain()


def causal(dest, keep, qkv, scale, cot, gathered, query, key, value, per_chunk, ident):
    total_rows, local = qkv.shape
    tok, full = key.shape
    rows = query.shape[0] // 2 * BLK
    vmem = pl.BlockSpec(memory_space=pltpu.VMEM)
    smem = pl.BlockSpec(memory_space=pltpu.SMEM)
    return pl.pallas_call(
        causal_kernel,
        out_shape=(
            jax.ShapeDtypeStruct((total_rows, HEAD), BF16),
            jax.ShapeDtypeStruct((total_rows, local), BF16),
            jax.ShapeDtypeStruct((3, full, HEAD), BF16),
            jax.ShapeDtypeStruct((rows, full), BF16),
        ),
        in_specs=[smem, smem, vmem, vmem, vmem, pl.BlockSpec(memory_space=pl.ANY), vmem, vmem, vmem],
        out_specs=[vmem, vmem, vmem, vmem],
        scratch_shapes=[
            pltpu.VMEM(gathered.shape, BF16),
            pltpu.SemaphoreType.DMA,
            pltpu.VMEM((local, total_rows), BF16),
            pltpu.VMEM((HEAD, total_rows), BF16),
            pltpu.VMEM((HEAD, total_rows), BF16),
            pltpu.VMEM((total_rows, HEAD), BF16),
            pltpu.VMEM((HEAD, total_rows), BF16),
            pltpu.VMEM((total_rows, QB), F32),
            pltpu.VMEM((total_rows, HEAD), F32),
            pltpu.VMEM((total_rows, HEAD), F32),
            pltpu.VMEM((HEAD, total_rows), F32),
            *Flow.scratch(rows, tok, full, per_chunk),
        ],
        compiler_params=pltpu.CompilerParams(
            collective_id=ident, has_side_effects=True, vmem_limit_bytes=VMEM_LIMIT
        ),
        cost_estimate=pl.CostEstimate(
            flops=20 * 10**9, bytes_accessed=32 * 1024 * 1024, transcendentals=0
        ),
        name="causal",
    )(dest, keep, qkv, scale, cot, gathered, query, key, value)


class Reduce:
    def __init__(self, value, pair_got, own, snd, got1, got2, whole, send_sem, recv_sem):
        self.value, self.pair_got, self.own, self.snd = value, pair_got, own, snd
        self.got1, self.got2, self.whole = got1, got2, whole
        self.send_sem, self.recv_sem = send_sem, recv_sem
        at = lax.axis_index("dp")
        self.y, self.core = at // 2, lax.rem(at, 2)
        self.partner = self.y * 2 + 1 - self.core
        self.next = [self.turn(by) * 2 + self.core for by in (1, -1)]
        middle = value.shape[3] // 2
        self.halves = (slice(0, middle), slice(middle, 2 * middle))

    def turn(self, by):
        return lax.rem(self.y + by + SIDE, SIDE)

    def copy(self, which, src, dst, target):
        return pltpu.make_async_remote_copy(
            src_ref=src, dst_ref=dst, send_sem=self.send_sem.at[which], recv_sem=self.recv_sem.at[which],
            device_id={"dp": target}, device_id_type=MESH,
        )

    def pair(self):
        return self.copy(0, self.value.at[:, 1 - self.core], self.pair_got, self.partner)

    def ring1(self, d):
        return self.copy(1 + d, self.snd.at[d, 0, :, self.halves[0]], self.got1.at[d], self.next[d])

    def ring2(self, d):
        return self.copy(3 + d, self.snd.at[d, 1], self.got2.at[d], self.next[d])

    def quarter(self, by, half=None):
        ref = self.whole.at[:, self.core, self.turn(by)]
        return ref if half is None else self.whole.at[:, self.core, self.turn(by), self.halves[half]]

    def spread1(self, d, by):
        return self.copy(5 + d, self.quarter(by), self.quarter(by), self.next[d])

    def spread2(self, d, by):
        return self.copy(7 + d, self.quarter(by, d), self.quarter(by, d), self.next[d])

    def back(self, core):
        return self.copy(9, self.whole.at[:, core], self.whole.at[:, core], self.partner)

    def stage1(self):
        self.pair().wait_recv()

        def add(q, carry):
            self.own[q] = self.value[:, self.core, q].astype(F32) + self.pair_got[:, q].astype(F32)
            return carry

        lax.fori_loop(0, SIDE, add, 0)
        for d in range(2):
            self.snd[d, 0, :, self.halves[0]] = self.own[self.turn(2), :, self.halves[d]].astype(BF16)
            self.ring1(d).start()

    def stage2(self):
        for d in range(2):
            self.ring1(d).wait_recv()
            near = self.turn(1 - 2 * d)
            self.snd[d, 1, :, self.halves[1 - d]] = self.own[near, :, self.halves[1 - d]].astype(BF16)
            self.snd[d, 1, :, self.halves[d]] = (
                self.own[near, :, self.halves[d]] + self.got1[d].astype(F32)
            ).astype(BF16)
            self.ring2(d).start()

    def stage3(self):
        for d in range(2):
            self.ring2(d).wait_recv()
        total = self.own[self.y] + self.got2[0].astype(F32) + self.got2[1].astype(F32)
        self.whole[:, self.core, self.y] = total.astype(BF16)
        for d in range(2):
            self.spread1(d, 0).start()

    def stage4(self):
        for d in range(2):
            self.spread1(d, 2 * d - 1).wait_recv()
            self.spread2(d, 2 * d - 1).start()

    def stage5(self):
        for d in range(2):
            self.spread2(d, 2).wait_recv()
        self.back(self.core).start()

    def stage6(self, out):
        self.back(1 - self.core).wait_recv()
        out[...] = self.whole[...]
        self.pair().wait_send()
        for d in range(2):
            self.ring1(d).wait_send()
            self.ring2(d).wait_send()
            self.spread1(d, 0).wait_send()
            self.spread2(d, 2 * d - 1).wait_send()
        self.back(self.core).wait_send()

    @staticmethod
    def scratch(shape):
        three, _, quarters, rows, width = shape
        return [
            pltpu.VMEM((three, quarters, rows, width), BF16),
            pltpu.VMEM((quarters, three, rows, width), F32),
            pltpu.VMEM((2, 2, three, rows, width), BF16),
            pltpu.VMEM((2, three, rows // 2, width), BF16),
            pltpu.VMEM((2, three, rows, width), BF16),
            pltpu.VMEM(shape, BF16),
            pltpu.SemaphoreType.DMA((10,)),
            pltpu.SemaphoreType.DMA((10,)),
        ]


def scatter_kernel(
    dest, d_all, three, value, out, summed, slot_at, weights, terms, got1, snd2, got2, sums, last1, lasts2, last2,
    send1, recv1, send2, recv2, send3, recv3, send4, recv4, *reduce_scratch,
):
    shard = lax.axis_index(SEQ)
    row, col = shard // SIDE, lax.rem(shard, SIDE)
    wide = out.shape[1] // 2
    part = wide // 2
    place = ((row, col), (col, row))
    halves = (slice(0, part), slice(part, wide))

    def turn(at, by):
        return lax.rem(at + by + SIDE, SIDE)

    def slot(h, a, b):
        return a * SIDE + b if h == 0 else b * SIDE + a

    barrier = pltpu.get_barrier_semaphore()
    for by in (1, -1):
        for h in range(2):
            a, b = place[h]
            pl.semaphore_signal(
                barrier, inc=1, device_id={SEQ: slot(h, turn(a, by), b)}, device_id_type=MESH
            )
    kept = dest.shape[1]
    for at in range(kept):
        slot_at[at] = functools.reduce(lambda got, j: jnp.where(dest[0, j] == at, j, got), range(kept), 0)
    reduce = Reduce(value, *reduce_scratch)
    for target in (reduce.partner, *reduce.next):
        pl.semaphore_signal(barrier, inc=1, device_id={"dp": target}, device_id_type=MESH)
    for which in range(3):
        weights[:, which * HEAD : (which + 1) * HEAD] = three[which]

    def group(h, a):
        slots = [jnp.where(h == 0, a * SIDE + s, s * SIDE + a) for s in range(SIDE)]
        rows = jnp.concatenate([d_all[slot_at[one]] for one in slots], axis=0)
        cols = pl.ds(pl.multiple_of(h * wide, wide), wide)
        value = lax.dot_general(rows, weights[cols, :], NT, preferred_element_type=F32).astype(BF16)
        for s in range(SIDE):
            terms[h, a, s] = value[s * BLK : (s + 1) * BLK, :]

    def first_send(h, d, s):
        a, b = place[h]
        return pltpu.make_async_remote_copy(
            src_ref=terms.at[h, turn(a, 2), s, :, halves[d]], dst_ref=got1.at[h, d, s],
            send_sem=send1.at[h, d, s], recv_sem=recv1.at[h, d, s],
            device_id={SEQ: slot(h, turn(a, 1 - 2 * d), b)}, device_id_type=MESH,
        )

    def second_send(h, d, s):
        a, b = place[h]
        return pltpu.make_async_remote_copy(
            src_ref=snd2.at[h, d, s], dst_ref=got2.at[h, d, s],
            send_sem=send2.at[h, d, s], recv_sem=recv2.at[h, d, s],
            device_id={SEQ: slot(h, turn(a, 1 - 2 * d), b)}, device_id_type=MESH,
        )

    def third_send(h, d):
        a, b = place[h]
        return pltpu.make_async_remote_copy(
            src_ref=sums.at[h, turn(b, 2), :, halves[d]], dst_ref=last1.at[h, d],
            send_sem=send3.at[h, d], recv_sem=recv3.at[h, d],
            device_id={SEQ: slot(h, a, turn(b, 1 - 2 * d))}, device_id_type=MESH,
        )

    def fourth_send(h, d):
        a, b = place[h]
        return pltpu.make_async_remote_copy(
            src_ref=lasts2.at[h, d], dst_ref=last2.at[h, d],
            send_sem=send4.at[h, d], recv_sem=recv4.at[h, d],
            device_id={SEQ: slot(h, a, turn(b, 1 - 2 * d))}, device_id_type=MESH,
        )

    def group_far(h, carry):
        group(h, turn(jnp.where(h == 0, row, col), 2))
        return carry

    def group_rest(g, carry):
        h, which = lax.rem(g, 2), g // 2
        by = jnp.where(which == 0, 1, jnp.where(which == 1, SIDE - 1, 0))
        group(h, turn(jnp.where(h == 0, row, col), by))
        return carry

    lax.fori_loop(0, 2, group_far, 0)
    pl.semaphore_wait(barrier, 7)
    reduce.pair().start()
    for k in (2, 1, 3, 0):
        for h in range(2):
            s = turn(place[h][1], k)
            for d in range(2):
                first_send(h, d, s).start()
    lax.fori_loop(0, 2, group_rest, 0)
    reduce.stage1()
    lax.fori_loop(2, 6, group_rest, 0)
    reduce.stage2()
    for k in (2, 1, 3, 0):
        for h in range(2):
            a, b = place[h]
            s = turn(b, k)
            for d in range(2):
                first_send(h, d, s).wait_recv()
                near = turn(a, 1 - 2 * d)
                other = halves[1 - d]
                snd2[h, d, s, :, other] = terms[h, near, s, :, other]
                snd2[h, d, s, :, halves[d]] = (
                    terms[h, near, s, :, halves[d]].astype(F32) + got1[h, d, s].astype(F32)
                ).astype(BF16)
                second_send(h, d, s).start()
    reduce.stage3()
    for k in (2, 1, 3, 0):
        for h in range(2):
            a, b = place[h]
            s = turn(b, k)
            for d in range(2):
                second_send(h, d, s).wait_recv()
            total = (
                terms[h, a, s].astype(F32) + got2[h, 0, s].astype(F32) + got2[h, 1, s].astype(F32)
            )
            if k != 0:
                sums[h, s] = total.astype(BF16)
            if k == 2:
                for d in range(2):
                    third_send(h, d).start()
            elif k != 0:
                d = 0 if k == 1 else 1
                third_send(h, d).wait_recv()
                other = halves[1 - d]
                lasts2[h, d, :, other] = sums[h, s, :, other]
                lasts2[h, d, :, halves[d]] = (total[:, halves[d]] + last1[h, d].astype(F32)).astype(BF16)
                fourth_send(h, d).start()
            else:
                for d in range(2):
                    fourth_send(h, d).wait_recv()
                out[:, h * wide : (h + 1) * wide] = (
                    total + last2[h, 0].astype(F32) + last2[h, 1].astype(F32)
                ).astype(BF16)
        if k == 2:
            reduce.stage4()
        elif k == 1:
            reduce.stage5()
        elif k == 3:
            reduce.stage6(summed)
    for h in range(2):
        for d in range(2):
            for s in range(SIDE):
                first_send(h, d, s).wait_send()
                second_send(h, d, s).wait_send()
            third_send(h, d).wait_send()
            fourth_send(h, d).wait_send()


def scatter_terms(dest, d_all, three, value, ident):
    blocks, _, local = d_all.shape
    full = three.shape[1]
    wide = full // 2
    part = wide // 2
    vmem = pl.BlockSpec(memory_space=pltpu.VMEM)
    four = pltpu.SemaphoreType.DMA((2, 2, SIDE))
    two = pltpu.SemaphoreType.DMA((2, 2))
    return pl.pallas_call(
        scatter_kernel,
        out_shape=(jax.ShapeDtypeStruct((BLK, full), BF16), jax.ShapeDtypeStruct(value.shape, BF16)),
        in_specs=[pl.BlockSpec(memory_space=pltpu.SMEM), vmem, vmem, vmem],
        out_specs=[vmem, vmem],
        scratch_shapes=[
            pltpu.SMEM((blocks,), jnp.int32),
            pltpu.VMEM((full, local), BF16),
            pltpu.VMEM((2, SIDE, SIDE, BLK, wide), BF16),
            pltpu.VMEM((2, 2, SIDE, BLK, part), BF16),
            pltpu.VMEM((2, 2, SIDE, BLK, wide), BF16),
            pltpu.VMEM((2, 2, SIDE, BLK, wide), BF16),
            pltpu.VMEM((2, SIDE, BLK, wide), BF16),
            pltpu.VMEM((2, 2, BLK, part), BF16),
            pltpu.VMEM((2, 2, BLK, wide), BF16),
            pltpu.VMEM((2, 2, BLK, wide), BF16),
            four, four, four, four, two, two, two, two,
            *Reduce.scratch(value.shape),
        ],
        compiler_params=pltpu.CompilerParams(
            collective_id=ident, has_side_effects=True, vmem_limit_bytes=VMEM_LIMIT
        ),
        cost_estimate=pl.CostEstimate(
            flops=2 * blocks * BLK * local * full, bytes_accessed=100 * 1024 * 1024, transcendentals=0
        ),
        name="scatter_terms",
    )(dest, d_all, three, value)


def assemble_kernel(dest, table, head, rest, sorted_out, summed, out, causal_out, grads):
    kept = sorted_out.shape[0] // BLK
    late = table[3 * pl.program_id(0)] == 1
    grads[...] = summed[...].astype(F32)

    @pl.when(pl.program_id(0) == 0)
    def _():
        for j in range(kept):
            causal_out[pl.ds(pl.multiple_of(dest[j] * BLK, BLK), BLK), :] = sorted_out[j * BLK : (j + 1) * BLK, :]

    @pl.when(late)
    def _():
        out[...] = rest[...]

    @pl.when(jnp.logical_not(late))
    def _():
        out[...] = head[...]


def assemble(dest, table, head, rest, sorted_out, summed):
    rows, full = head.shape
    steps = 2 * rows // BLK
    whole = pl.BlockSpec(sorted_out.shape, lambda g, d, t: (0, 0))
    part = pl.BlockSpec((3, full // steps, HEAD), lambda g, d, t: (0, g, 0))
    return pl.pallas_call(
        assemble_kernel,
        out_shape=(
            jax.ShapeDtypeStruct((2 * rows, full), BF16),
            jax.ShapeDtypeStruct(sorted_out.shape, BF16),
            jax.ShapeDtypeStruct(summed.shape, F32),
        ),
        grid_spec=pltpu.PrefetchScalarGridSpec(
            num_scalar_prefetch=2,
            grid=(steps,),
            in_specs=[
                pl.BlockSpec((BLK, full), lambda g, d, t: (t[3 * g + 1], 0)),
                pl.BlockSpec((BLK, full), lambda g, d, t: (t[3 * g + 2], 0)),
                whole,
                part,
            ],
            out_specs=[pl.BlockSpec((BLK, full), lambda g, d, t: (g, 0)), whole, part],
        ),
        compiler_params=pltpu.CompilerParams(vmem_limit_bytes=VMEM_LIMIT),
        name="assemble",
    )(dest, table, head, rest, sorted_out, summed)


def shards(query_input, key_input, value_input, keep_blocks, dest_slots, proj_weights, cotangent):
    tok, full = query_input.shape[1:]
    per_shard = tok // BLK
    kept = keep_blocks.shape[1]
    query = query_input.reshape(per_shard, BLK, full)
    key = key_input[0]
    value = value_input[0]
    first, gathered, qkv, scale, table = front(keep_blocks, query, key, value, proj_weights, 2, 0)
    sorted_out, d_all, local_grads, rest = causal(
        dest_slots, keep_blocks, qkv, scale, cotangent.reshape(kept, BLK, -1), gathered, query, key, value, 4, 1
    )
    row_grad, summed = scatter_terms(
        dest_slots, d_all.reshape(kept, BLK, -1), proj_weights,
        local_grads.reshape(3, 2, SIDE, full // 2 // SIDE, HEAD), 2,
    )
    window_out, causal_out, grads = assemble(
        dest_slots[0], table, first, rest, sorted_out, summed.reshape(proj_weights.shape)
    )
    return (window_out[None], causal_out[None], grads, row_grad[None])


def solution(mesh):
    return jax.shard_map(
        shards,
        mesh=mesh,
        in_specs=(
            P("dp", "seq", None),
            P("dp", "seq", None),
            P("dp", "seq", None),
            P("dp", None),
            P("dp", None),
            P(None, None, "seq"),
            P("dp", None, "seq"),
        ),
        out_specs=(
            P("dp", "seq", None),
            P("dp", None, "seq"),
            P(None, None, "seq"),
            P("dp", "seq", None),
        ),
        check_vma=False,
    )
```

```python
import functools

import jax
import jax.numpy as jnp
from jax import lax
from jax.experimental import pallas as pl
from jax.experimental.pallas import tpu as pltpu
from jax.sharding import PartitionSpec as P

HEAD = 128
BLK = 128
SEQ = "seq"
MESH = pl.DeviceIdType.MESH
SCALE = HEAD ** (-0.5)
LOG2E = 1.4426950408889634
SCALE2 = SCALE * LOG2E
LOW = -1e30
NT = (((1,), (1,)), ((), ()))
BF16 = jnp.bfloat16
F32 = jnp.float32
VMEM_LIMIT = 56 * 1024 * 1024


def window_parts(heads):
    def scores_of(query, key, value_t, bias):
        scores = lax.dot_general(key, query, NT, preferred_element_type=F32)
        if bias is not None:
            scores = scores + bias
        return scores, jnp.max(scores, axis=0, keepdims=True), value_t

    def rest_of(scores, top, value_t):
        weight = jnp.exp2((scores - top) * SCALE2)
        total = jnp.sum(weight, axis=0, keepdims=True)
        out = jnp.dot(value_t, weight.astype(BF16), preferred_element_type=F32)
        return out * (1.0 / total), top * SCALE2 + jnp.log2(total)

    done = []
    ahead = scores_of(*heads[0])
    for h in range(len(heads)):
        current = ahead
        if h + 1 < len(heads):
            ahead = scores_of(*heads[h + 1])
        done.append(rest_of(*current))
    return done


def merged(out_a, lse_a, out_b, lse_b):
    top = jnp.maximum(lse_a, lse_b)
    weight_a = jnp.exp2(lse_a - top)
    weight_b = jnp.exp2(lse_b - top)
    total = weight_a + weight_b
    return out_a * (weight_a / total) + out_b * (weight_b / total), top + jnp.log2(total)


def block_ranks(keep, shard, per_shard):
    kept = [
        functools.reduce(
            lambda found, j: jnp.where(keep[0, j] == shard * per_shard + b, 1, found), range(keep.shape[1]), 0
        )
        for b in range(per_shard)
    ]
    total = sum(kept)
    return [
        jnp.where(kept[b] == 1, sum(kept[:b], 0), total + b - sum(kept[:b], 0)) for b in range(per_shard)
    ]


def picked(ranks, places):
    return [functools.reduce(lambda got, b: jnp.where(ranks[b] == at, b, got), range(len(ranks)), 0) for at in places]


def near_ranks(keep, per_shard):
    shard, count = lax.axis_index(SEQ), lax.axis_size(SEQ)
    return [block_ranks(keep, lax.rem(shard + by, count), per_shard) for by in range(3)]


class Flow:
    def __init__(self, sel, q_in, k_in, v_in, out, scratch):
        (
            self.q_own, self.q_one, self.q_two, self.v_t, self.o_own, self.l_own, self.o_snd2, self.l_snd2,
            self.o_got2, self.l_got2, self.o_snd1, self.l_snd1, self.o_got1, self.l_got1,
            self.bias_own, self.bias_two, self.send_sem, self.recv_sem,
        ) = scratch
        self.sel, self.q_in, self.k_in, self.v_in, self.out = sel, q_in, k_in, v_in, out
        self.chunks, self.rows, self.width = self.q_own.shape
        self.per_chunk = self.width // HEAD
        self.lse_step = 8 // self.per_chunk
        self.shard = lax.axis_index(SEQ)
        count = lax.axis_size(SEQ)
        self.right = lax.rem(self.shard + 1, count)
        self.left = lax.rem(self.shard + count - 1, count)

    def copy(self, which, c, src, dst, target):
        return pltpu.make_async_remote_copy(
            src_ref=src.at[c], dst_ref=dst.at[c],
            send_sem=self.send_sem.at[which, c], recv_sem=self.recv_sem.at[which, c],
            device_id={SEQ: target}, device_id_type=MESH,
        )

    def hop_one(self, c):
        return self.copy(0, c, self.q_own, self.q_one, self.left)

    def hop_two(self, c):
        return self.copy(1, c, self.q_one, self.q_two, self.left)

    def back_two(self, c):
        return (
            self.copy(2, c, self.o_snd2, self.o_got2, self.right),
            self.copy(3, c, self.l_snd2, self.l_got2, self.right),
        )

    def back_one(self, c):
        return (
            self.copy(4, c, self.o_snd1, self.o_got1, self.right),
            self.copy(5, c, self.l_snd1, self.l_got1, self.right),
        )

    def begin(self, ahead, others=()):
        barrier = pltpu.get_barrier_semaphore()
        greeted = (self.left, self.right, *others)
        for neighbour in greeted:
            pl.semaphore_signal(barrier, inc=1, device_id={SEQ: neighbour}, device_id_type=MESH)
        picks = self.rows // BLK
        for a in range(picks):
            block = self.q_in[self.sel[a]]
            for c in range(self.chunks):
                self.q_own[c, a * BLK : (a + 1) * BLK, :] = block[:, c * self.width : (c + 1) * self.width]
        pl.semaphore_wait(barrier, len(greeted))
        for c in range(ahead):
            self.hop_one(c).start()
        self.ahead = ahead
        lane = lax.broadcasted_iota(jnp.int32, (1, self.rows), 1)
        key_at = lax.broadcasted_iota(jnp.int32, self.bias_own.shape, 0)
        for base, ref in ((0, self.bias_own), (2 * picks, self.bias_two)):
            place = lane
            for a in range(picks):
                place = jnp.where(lane // BLK == a, (lane - a * BLK) + self.sel[base + a] * BLK, place)
            seen = (key_at <= place) if base == 0 else (key_at > place)
            ref[...] = jnp.where(seen, 0.0, LOW)

    def cols(self, c, h):
        return pl.ds(pl.multiple_of(c * self.width + h * HEAD, HEAD), HEAD)

    def lse_at(self, h):
        return slice(h * self.lse_step, (h + 1) * self.lse_step)

    def spread(self, row):
        return jnp.broadcast_to(row, (self.lse_step, self.rows))

    def head(self, h):
        return slice(h * HEAD, (h + 1) * HEAD)

    def pump(self, c):
        self.hop_one(c).wait_recv()
        self.hop_two(c).start()

        @pl.when(c + self.ahead < self.chunks)
        def _():
            self.hop_one(c + self.ahead).start()

    def own(self, c):
        heads = []
        for h in range(self.per_chunk):
            cols = self.cols(c, h)
            value_t = self.v_in[:, cols].T
            self.v_t[cols, :] = value_t
            heads.append((self.q_own[c, :, self.head(h)], self.k_in[:, cols], value_t, self.bias_own[...]))
        for h, (part, lse) in enumerate(window_parts(heads)):
            self.o_own[c, self.head(h), :] = part
            self.l_own[c, self.lse_at(h), :] = self.spread(lse)

    def two(self, c):
        self.hop_two(c).wait_recv()
        heads = [
            (self.q_two[c, :, self.head(h)], self.k_in[:, self.cols(c, h)], self.v_t[self.cols(c, h), :], self.bias_two[...])
            for h in range(self.per_chunk)
        ]
        for h, (part, lse) in enumerate(window_parts(heads)):
            self.o_snd2[c, self.head(h), :] = part.astype(BF16)
            self.l_snd2[c, self.lse_at(h), :] = self.spread(lse)
        for each in self.back_two(c):
            each.start()

    def incoming(self, got, h, c):
        first = h * self.lse_step
        return jnp.where(self.shard == 0, LOW, got[c, first : first + 1, :])

    def one(self, c):
        parts = window_parts([
            (self.q_one[c, :, self.head(h)], self.k_in[:, self.cols(c, h)], self.v_t[self.cols(c, h), :], None)
            for h in range(self.per_chunk)
        ])
        for each in self.back_two(c):
            each.wait_recv()
        for h in range(self.per_chunk):
            part, lse = merged(
                *parts[h], self.o_got2[c, self.head(h), :].astype(F32), self.incoming(self.l_got2, h, c)
            )
            self.o_snd1[c, self.head(h), :] = part.astype(BF16)
            self.l_snd1[c, self.lse_at(h), :] = self.spread(lse)
        for each in self.back_one(c):
            each.start()

    def final(self, c):
        for each in self.back_one(c):
            each.wait_recv()
        for h in range(self.per_chunk):
            first = h * self.lse_step
            part, _ = merged(
                self.o_own[c, self.head(h), :], self.l_own[c, first : first + 1, :],
                self.o_got1[c, self.head(h), :].astype(F32), self.incoming(self.l_got1, h, c),
            )
            self.store(c, h, part.T.astype(BF16))

    def store(self, c, h, value):
        self.out[:, self.cols(c, h)] = value

    def step(self, t, lag):
        def stage(late, *calls):
            @pl.when((t >= late) & (t < self.chunks + late))
            def _():
                for call in calls:
                    call(t - late)

        stage(0, self.pump, self.own)
        stage(lag, self.two)
        stage(2 * lag, self.one)
        stage(3 * lag, self.final)

    def drain(self):
        def body(c, carry):
            self.hop_one(c).wait_send()
            self.hop_two(c).wait_send()
            for each in self.back_two(c) + self.back_one(c):
                each.wait_send()
            return carry

        lax.fori_loop(0, self.chunks, body, 0)

    @staticmethod
    def scratch(rows, tok, full, per_chunk):
        width = per_chunk * HEAD
        chunks = full // width
        queries = pltpu.VMEM((chunks, rows, width), BF16)
        outs = pltpu.VMEM((chunks, width, rows), BF16)
        lses = pltpu.VMEM((chunks, 8, rows), F32)
        return [
            queries, queries, queries, pltpu.VMEM((full, tok), BF16), pltpu.VMEM((chunks, width, rows), F32), lses,
            outs, lses, outs, lses, outs, lses, outs, lses,
            pltpu.VMEM((tok, rows), F32), pltpu.VMEM((tok, rows), F32),
            pltpu.SemaphoreType.DMA((6, chunks)), pltpu.SemaphoreType.DMA((6, chunks)),
        ]


SIDE = 4


class Spread:
    OFFSETS = (0, 1, SIDE - 1, 2)

    def __init__(self, got, send_sem, recv_sem):
        self.got, self.send_sem, self.recv_sem = got, send_sem, recv_sem
        shard = lax.axis_index(SEQ)
        row, col = shard // SIDE, lax.rem(shard, SIDE)
        self.here = ((col, row), (row, col))

    @staticmethod
    def turn(at, by):
        return lax.rem(at + by + SIDE, SIDE)

    @staticmethod
    def slot(kind, place):
        a, b = place
        return b * SIDE + a if kind == 0 else a * SIDE + b

    def neighbours(self):
        a, b = self.here[0]
        return [self.slot(0, (self.turn(a, by), b)) for by in (1, -1)] + [
            self.slot(0, (a, self.turn(b, by))) for by in (1, -1)
        ]

    def message(self, c, kind, group, place, half, target):
        slot = self.slot(kind, place)
        ref = self.got.at[c, kind, slot] if half is None else self.got.at[c, kind, slot, half]
        return pltpu.make_async_remote_copy(
            src_ref=ref, dst_ref=ref, send_sem=self.send_sem.at[c, kind], recv_sem=self.recv_sem.at[c, kind, group],
            device_id={SEQ: self.slot(kind, target)}, device_id_type=MESH,
        )

    def whole(self, c, kind, group, pieces):
        a, b = self.here[kind]
        ref = self.got.at[c, kind, pl.ds(0, pieces)]
        return pltpu.make_async_remote_copy(
            src_ref=ref, dst_ref=ref, send_sem=self.send_sem.at[c, kind], recv_sem=self.recv_sem.at[c, kind, group],
            device_id={SEQ: self.slot(kind, (self.turn(a, 1), b))}, device_id_type=MESH,
        )

    def ring(self, c, kind, group, here, up, down, to_up, to_down):
        if group % 2 == 0:
            pairs = ((here, None, to_up), (here, None, to_down))
        else:
            pairs = ((down, 0, to_up), (up, 1, to_down))
        for pair in pairs:
            self.message(c, kind, group, *pair).start()

    def first(self, c, kind, group):
        a, b = self.here[kind]
        up, down = (self.turn(a, 1), b), (self.turn(a, -1), b)
        self.ring(c, kind, group, (a, b), up, down, up, down)

    def second(self, c, kind, group, k):
        a, b = self.here[kind]
        origin = self.turn(a, self.OFFSETS[k])
        up, down = self.turn(b, 1), self.turn(b, -1)
        self.ring(c, kind, group, (origin, b), (origin, up), (origin, down), (a, up), (a, down))

    def launch(self, c):
        for kind in range(2):
            self.first(c, kind, 0)

    def relay(self, c):
        for kind in range(2):
            self.whole(c, kind, 0, 2).wait_recv()
            self.first(c, kind, 1)
            for k in range(3):
                self.second(c, kind, 2, k)

    def relay_far(self, c):
        for kind in range(2):
            self.whole(c, kind, 1, 1).wait_recv()
            self.second(c, kind, 2, 3)

    def second_relay(self, c):
        for kind in range(2):
            self.whole(c, kind, 2, 8).wait_recv()
            for k in range(4):
                self.second(c, kind, 3, k)

    def settle(self, c):
        for kind in range(2):
            self.whole(c, kind, 3, 4).wait_recv()

    def drain(self, c):
        for kind in range(2):
            self.whole(c, kind, 0, 15).wait_send()


def front_kernel(
    keep, q_in, k_in, v_in, three, out, rows_out, projected, scale_out, table,
    weights, got, held, staged, staged_sem, total, squares, spread_send, spread_recv, *scratch,
):
    kept = keep.shape[1]
    per_shard = q_in.shape[0]
    ranks = near_ranks(keep, per_shard)
    half = per_shard // 2
    sel = [at for each in ranks for at in picked(each, range(half))]
    for b in range(per_shard):
        late = jnp.where(ranks[0][b] >= half, 1, 0)
        table[3 * b] = late
        table[3 * b + 1] = ranks[0][b] * (1 - late)
        table[3 * b + 2] = (ranks[0][b] - half) * late
    owner = [keep[0, j] // per_shard for j in range(kept)]
    nth = [0] + [jnp.where(owner[j] == owner[j - 1], 1, 0) for j in range(1, kept)]
    flow = Flow(sel, q_in, k_in, v_in, out, scratch)
    spread = Spread(got, spread_send, spread_recv)
    chunks, width = flow.chunks, flow.width
    total_rows, local = projected.shape
    full = k_in.shape[1]
    block = 512
    per_kind = flow.per_chunk // 2

    def store(c, h, value):
        out[:, flow.cols(c, h)] = value
        for a in range(flow.rows // BLK):
            got[c, h // per_kind, flow.shard, a, :, flow.head(h % per_kind)] = value[a * BLK : (a + 1) * BLK, :]

    flow.store = store
    flow.begin(3, spread.neighbours())
    for which in range(3):
        weights[:, which * HEAD : (which + 1) * HEAD] = three[which]
    total[...] = jnp.zeros_like(total)
    squares[...] = jnp.zeros_like(squares)

    def staged_copy(c):
        which = lax.rem(c, 2)
        return pltpu.make_async_copy(staged.at[which], rows_out.at[c], staged_sem.at[which])

    def project_chunk(c):
        which = lax.rem(c, 2)

        @pl.when(c >= 2)
        def _():
            staged_copy(c - 2).wait()

        def hold(i, carry):
            for kind in range(2):
                held[i, :, :, kind * width // 2 : (kind + 1) * width // 2] = got[c, kind, i]
            return carry

        lax.fori_loop(0, SIDE * SIDE, hold, 0)

        for j in range(kept):
            staged[which, j * BLK : (j + 1) * BLK, :] = held[owner[j], nth[j]]
        staged_copy(c).start()
        weight = weights[pl.ds(pl.multiple_of(c * width, width), width), :]

        def multiply(r, carry):
            at = pl.ds(pl.multiple_of(r * block, block), block)
            rows = staged[which, at, :]
            total[at, :] += jnp.dot(rows, weight, preferred_element_type=F32)
            wide = rows.astype(F32)
            square = wide * wide
            squares[at, :] += sum(square[:, h * HEAD : (h + 1) * HEAD] for h in range(flow.per_chunk))
            return carry

        lax.fori_loop(0, total_rows // block, multiply, 0)

    def step(t, carry):
        flow.step(t, 1)

        def stage(late, call):
            @pl.when((t >= late) & (t < chunks + late))
            def _():
                call(t - late)

        stage(3, spread.launch)
        stage(4, spread.relay)
        stage(5, spread.relay_far)
        stage(6, spread.second_relay)

        @pl.when(t >= 7)
        def _():
            spread.settle(t - 7)
            project_chunk(t - 7)

        return carry

    lax.fori_loop(0, chunks + 7, step, 0)

    def finish(r, carry):
        at = pl.ds(pl.multiple_of(r * block, block), block)
        square = squares[at, :]
        inv = lax.rsqrt(jnp.sum(square, axis=1, keepdims=True) * (1.0 / full) + 1e-06)
        projected[at, :] = (total[at, :] * inv).astype(BF16)
        scale_out[:, at] = lax.rsqrt(jnp.sum(square.T, axis=0, keepdims=True) * (1.0 / full) + 1e-06)
        return carry

    lax.fori_loop(0, total_rows // block, finish, 0)

    def drain(c, carry):
        spread.drain(c)
        return carry

    lax.fori_loop(0, chunks, drain, 0)
    for c in (chunks - 2, chunks - 1):
        staged_copy(c).wait()
    flow.drain()


def front(keep, query, key, value, weights, per_chunk, ident):
    tok, full = key.shape
    local = 3 * HEAD
    rows = query.shape[0] // 2 * BLK
    total_rows = keep.shape[1] * BLK
    width = per_chunk * HEAD
    chunks = full // width
    vmem = pl.BlockSpec(memory_space=pltpu.VMEM)
    smem = pl.BlockSpec(memory_space=pltpu.SMEM)
    return pl.pallas_call(
        front_kernel,
        out_shape=(
            jax.ShapeDtypeStruct((rows, full), BF16),
            jax.ShapeDtypeStruct((chunks, total_rows, width), BF16),
            jax.ShapeDtypeStruct((total_rows, local), BF16),
            jax.ShapeDtypeStruct((1, total_rows), F32),
            jax.ShapeDtypeStruct((3 * query.shape[0],), jnp.int32),
        ),
        in_specs=[smem, vmem, vmem, vmem, vmem],
        out_specs=[vmem, pl.BlockSpec(memory_space=pl.ANY), vmem, vmem, smem],
        scratch_shapes=[
            pltpu.VMEM((full, local), BF16),
            pltpu.VMEM((chunks, 2, SIDE * SIDE, rows // BLK, BLK, width // 2), BF16),
            pltpu.VMEM((SIDE * SIDE, rows // BLK, BLK, width), BF16),
            pltpu.VMEM((2, total_rows, width), BF16),
            pltpu.SemaphoreType.DMA((2,)),
            pltpu.VMEM((total_rows, local), F32),
            pltpu.VMEM((total_rows, HEAD), F32),
            pltpu.SemaphoreType.DMA((chunks, 2)),
            pltpu.SemaphoreType.DMA((chunks, 2, 4)),
            *Flow.scratch(rows, tok, full, per_chunk),
        ],
        compiler_params=pltpu.CompilerParams(
            collective_id=ident, has_side_effects=True, vmem_limit_bytes=VMEM_LIMIT
        ),
        name="front",
    )(keep, query, key, value, weights)


QB = 256
KB = 512


def causal_kernel(
    dest, keep, qkv, scale, cot, gathered, q_in, k_in, v_in, out, d_all, grads, rest,
    rows_in, rows_sem, d_all_t, v_t, k_t, do_own, do_t, p_buf, dk_acc, dv_acc, dq_t, *scratch,
):
    kept = dest.shape[1]
    total_rows = qkv.shape[0]
    per_shard = q_in.shape[0]
    sel = [at for each in near_ranks(keep, per_shard) for at in picked(each, range(per_shard // 2, per_shard))]
    blocks = total_rows // QB
    rows_copy = pltpu.make_async_copy(gathered, rows_in, rows_sem)
    rows_copy.start()
    flow = Flow(sel, q_in, k_in, v_in, rest, scratch)
    flow.begin(2)

    for j in range(kept):
        do_own[j * BLK : (j + 1) * BLK, :] = cot[dest[0, j]]

    def prepare(c, carry):
        at = pl.ds(pl.multiple_of(c * QB, QB), QB)
        k_t[:, at] = qkv[at, HEAD : 2 * HEAD].T
        v_t[:, at] = qkv[at, 2 * HEAD : 3 * HEAD].T
        do_t[:, at] = do_own[at, :].T
        return carry

    lax.fori_loop(0, blocks, prepare, 0)
    dk_acc[...] = jnp.zeros_like(dk_acc)
    dv_acc[...] = jnp.zeros_like(dv_acc)

    def query_block(i):
        rows = pl.ds(pl.multiple_of(i * QB, QB), QB)
        chunks = (i * QB + QB + KB - 1) // KB
        q_i = qkv[rows, :HEAD]
        do_i = do_own[rows, :]

        def scores_of(c, masked):
            keys = pl.ds(pl.multiple_of(c * KB, KB), KB)
            scores = lax.dot_general(qkv[keys, HEAD : 2 * HEAD], q_i, NT, preferred_element_type=F32)
            if masked:
                key_at = lax.broadcasted_iota(jnp.int32, (KB, QB), 0)
                row_at = lax.broadcasted_iota(jnp.int32, (KB, QB), 1)
                scores = jnp.where(key_at - row_at <= i * QB - (chunks - 1) * KB, scores, LOW)
            p_buf[keys, :] = scores
            return jnp.max(scores, axis=0, keepdims=True)

        top = lax.fori_loop(
            0, chunks - 1, lambda c, m: jnp.maximum(m, scores_of(c, False)), scores_of(chunks - 1, True)
        )

        def weigh(c, carry):
            total, acc = carry
            keys = pl.ds(pl.multiple_of(c * KB, KB), KB)
            weight = jnp.exp2((p_buf[keys, :] - top) * SCALE2)
            p_buf[keys, :] = weight
            total = total + jnp.sum(weight, axis=0, keepdims=True)
            acc = acc + jnp.dot(v_t[:, keys], weight.astype(BF16), preferred_element_type=F32)
            return total, acc

        total, acc = lax.fori_loop(
            0, chunks, weigh, (jnp.zeros((1, QB), F32), jnp.zeros((HEAD, QB), F32))
        )
        inv = 1.0 / total
        o_t = acc * inv
        delta = jnp.sum(o_t * do_t[:, rows].astype(F32), axis=0, keepdims=True)
        out[rows, :] = o_t.T.astype(BF16)

        def back(c, acc):
            keys = pl.ds(pl.multiple_of(c * KB, KB), KB)
            soft = p_buf[keys, :] * inv
            dv_acc[keys, :] += jnp.dot(soft.astype(BF16), do_i, preferred_element_type=F32)
            d_probs = lax.dot_general(qkv[keys, 2 * HEAD :], do_i, NT, preferred_element_type=F32)
            d_scores = (soft * (d_probs - delta) * SCALE).astype(BF16)
            dk_acc[keys, :] += jnp.dot(d_scores, q_i, preferred_element_type=F32)
            return acc + jnp.dot(k_t[:, keys], d_scores, preferred_element_type=F32)

        dq_t[:, rows] = lax.fori_loop(0, chunks, back, jnp.zeros((HEAD, QB), F32))

    def finish(c, carry):
        at = pl.ds(pl.multiple_of(c * QB, QB), QB)
        d_q = dq_t[:, at]
        d_all_t[:HEAD, at] = (d_q * scale[:, at]).astype(BF16)
        d_all[at, :HEAD] = d_q.T.astype(BF16)
        for which, acc in ((1, dk_acc), (2, dv_acc)):
            value = acc[at, :]
            d_all[at, which * HEAD : (which + 1) * HEAD] = value.astype(BF16)
            d_all_t[which * HEAD : (which + 1) * HEAD, at] = (value.T * scale[:, at]).astype(BF16)
        return carry

    def weight_block(g, carry):
        wide = rows_in.shape[2]
        at = pl.ds(pl.multiple_of(g * wide, wide), wide)
        value = jnp.dot(d_all_t[...], rows_in[g], preferred_element_type=F32)
        for which in range(3):
            grads[which, at, :] = value[which * HEAD : (which + 1) * HEAD, :].T.astype(BF16)
        return carry

    col_blocks = rows_in.shape[0]
    halves = blocks // flow.chunks
    share = (col_blocks + 2 * halves - 1) // (2 * halves)

    def step(u, carry):
        t, r = u // halves, lax.rem(u, halves)

        def stage(at, late, *calls):
            @pl.when((r == at) & (t >= late) & (t < flow.chunks + late))
            def _():
                for call in calls:
                    call(t - late)

        stage(0, 0, flow.own)

        @pl.when(u < blocks)
        def _():
            query_block(blocks - 1 - u)

        stage(0, 0, flow.pump)
        stage(0, 1, flow.two)
        stage(halves - 1, 2, flow.one)
        stage(halves - 1, 3, flow.final)

        @pl.when(u == blocks)
        def _():
            lax.fori_loop(0, blocks, finish, 0)
            rows_copy.wait()

        @pl.when(u >= blocks)
        def _():
            low = (u - blocks) * share
            lax.fori_loop(low, jnp.minimum(low + share, col_blocks), weight_block, 0)

        return carry

    lax.fori_loop(0, (flow.chunks + 3) * halves, step, 0)
    flow.drain()


def causal(dest, keep, qkv, scale, cot, gathered, query, key, value, per_chunk, ident):
    total_rows, local = qkv.shape
    tok, full = key.shape
    rows = query.shape[0] // 2 * BLK
    vmem = pl.BlockSpec(memory_space=pltpu.VMEM)
    smem = pl.BlockSpec(memory_space=pltpu.SMEM)
    return pl.pallas_call(
        causal_kernel,
        out_shape=(
            jax.ShapeDtypeStruct((total_rows, HEAD), BF16),
            jax.ShapeDtypeStruct((total_rows, local), BF16),
            jax.ShapeDtypeStruct((3, full, HEAD), BF16),
            jax.ShapeDtypeStruct((rows, full), BF16),
        ),
        in_specs=[smem, smem, vmem, vmem, vmem, pl.BlockSpec(memory_space=pl.ANY), vmem, vmem, vmem],
        out_specs=[vmem, vmem, vmem, vmem],
        scratch_shapes=[
            pltpu.VMEM(gathered.shape, BF16),
            pltpu.SemaphoreType.DMA,
            pltpu.VMEM((local, total_rows), BF16),
            pltpu.VMEM((HEAD, total_rows), BF16),
            pltpu.VMEM((HEAD, total_rows), BF16),
            pltpu.VMEM((total_rows, HEAD), BF16),
            pltpu.VMEM((HEAD, total_rows), BF16),
            pltpu.VMEM((total_rows, QB), F32),
            pltpu.VMEM((total_rows, HEAD), F32),
            pltpu.VMEM((total_rows, HEAD), F32),
            pltpu.VMEM((HEAD, total_rows), F32),
            *Flow.scratch(rows, tok, full, per_chunk),
        ],
        compiler_params=pltpu.CompilerParams(
            collective_id=ident, has_side_effects=True, vmem_limit_bytes=VMEM_LIMIT
        ),
        cost_estimate=pl.CostEstimate(
            flops=20 * 10**9, bytes_accessed=32 * 1024 * 1024, transcendentals=0
        ),
        name="causal",
    )(dest, keep, qkv, scale, cot, gathered, query, key, value)


class Reduce:
    def __init__(self, value, pair_got, own, snd, got1, got2, whole, send_sem, recv_sem):
        self.value, self.pair_got, self.own, self.snd = value, pair_got, own, snd
        self.got1, self.got2, self.whole = got1, got2, whole
        self.send_sem, self.recv_sem = send_sem, recv_sem
        at = lax.axis_index("dp")
        self.y, self.core = at // 2, lax.rem(at, 2)
        self.partner = self.y * 2 + 1 - self.core
        self.next = [self.turn(by) * 2 + self.core for by in (1, -1)]
        middle = value.shape[3] // 2
        self.halves = (slice(0, middle), slice(middle, 2 * middle))

    def turn(self, by):
        return lax.rem(self.y + by + SIDE, SIDE)

    def copy(self, which, src, dst, target):
        return pltpu.make_async_remote_copy(
            src_ref=src, dst_ref=dst, send_sem=self.send_sem.at[which], recv_sem=self.recv_sem.at[which],
            device_id={"dp": target}, device_id_type=MESH,
        )

    def pair(self):
        return self.copy(0, self.value.at[:, 1 - self.core], self.pair_got, self.partner)

    def ring1(self, d):
        return self.copy(1 + d, self.snd.at[d, 0, :, self.halves[0]], self.got1.at[d], self.next[d])

    def ring2(self, d):
        return self.copy(3 + d, self.snd.at[d, 1], self.got2.at[d], self.next[d])

    def quarter(self, by, half=None):
        ref = self.whole.at[:, self.core, self.turn(by)]
        return ref if half is None else self.whole.at[:, self.core, self.turn(by), self.halves[half]]

    def spread1(self, d, by):
        return self.copy(5 + d, self.quarter(by), self.quarter(by), self.next[d])

    def spread2(self, d, by):
        return self.copy(7 + d, self.quarter(by, d), self.quarter(by, d), self.next[d])

    def back(self, core):
        return self.copy(9, self.whole.at[:, core], self.whole.at[:, core], self.partner)

    def stage1(self):
        self.pair().wait_recv()

        def add(q, carry):
            self.own[q] = self.value[:, self.core, q].astype(F32) + self.pair_got[:, q].astype(F32)
            return carry

        lax.fori_loop(0, SIDE, add, 0)
        for d in range(2):
            self.snd[d, 0, :, self.halves[0]] = self.own[self.turn(2), :, self.halves[d]].astype(BF16)
            self.ring1(d).start()

    def stage2(self):
        for d in range(2):
            self.ring1(d).wait_recv()
            near = self.turn(1 - 2 * d)
            self.snd[d, 1, :, self.halves[1 - d]] = self.own[near, :, self.halves[1 - d]].astype(BF16)
            self.snd[d, 1, :, self.halves[d]] = (
                self.own[near, :, self.halves[d]] + self.got1[d].astype(F32)
            ).astype(BF16)
            self.ring2(d).start()

    def stage3(self):
        for d in range(2):
            self.ring2(d).wait_recv()
        total = self.own[self.y] + self.got2[0].astype(F32) + self.got2[1].astype(F32)
        self.whole[:, self.core, self.y] = total.astype(BF16)
        for d in range(2):
            self.spread1(d, 0).start()

    def stage4(self):
        for d in range(2):
            self.spread1(d, 2 * d - 1).wait_recv()
            self.spread2(d, 2 * d - 1).start()

    def stage5(self):
        for d in range(2):
            self.spread2(d, 2).wait_recv()
        self.back(self.core).start()

    def stage6(self, out):
        self.back(1 - self.core).wait_recv()
        out[...] = self.whole[...]
        self.pair().wait_send()
        for d in range(2):
            self.ring1(d).wait_send()
            self.ring2(d).wait_send()
            self.spread1(d, 0).wait_send()
            self.spread2(d, 2 * d - 1).wait_send()
        self.back(self.core).wait_send()

    @staticmethod
    def scratch(shape):
        three, _, quarters, rows, width = shape
        return [
            pltpu.VMEM((three, quarters, rows, width), BF16),
            pltpu.VMEM((quarters, three, rows, width), F32),
            pltpu.VMEM((2, 2, three, rows, width), BF16),
            pltpu.VMEM((2, three, rows // 2, width), BF16),
            pltpu.VMEM((2, three, rows, width), BF16),
            pltpu.VMEM(shape, BF16),
            pltpu.SemaphoreType.DMA((10,)),
            pltpu.SemaphoreType.DMA((10,)),
        ]


def scatter_kernel(
    dest, d_all, three, value, out, summed, slot_at, weights, terms, got1, snd2, got2, sums, last1, lasts2, last2,
    send1, recv1, send2, recv2, send3, recv3, send4, recv4, *reduce_scratch,
):
    shard = lax.axis_index(SEQ)
    row, col = shard // SIDE, lax.rem(shard, SIDE)
    wide = out.shape[1] // 2
    part = wide // 2
    place = ((row, col), (col, row))
    halves = (slice(0, part), slice(part, wide))

    def turn(at, by):
        return lax.rem(at + by + SIDE, SIDE)

    def slot(h, a, b):
        return a * SIDE + b if h == 0 else b * SIDE + a

    barrier = pltpu.get_barrier_semaphore()
    for by in (1, -1):
        for h in range(2):
            a, b = place[h]
            pl.semaphore_signal(
                barrier, inc=1, device_id={SEQ: slot(h, turn(a, by), b)}, device_id_type=MESH
            )
    kept = dest.shape[1]
    for at in range(kept):
        slot_at[at] = functools.reduce(lambda got, j: jnp.where(dest[0, j] == at, j, got), range(kept), 0)
    reduce = Reduce(value, *reduce_scratch)
    for target in (reduce.partner, *reduce.next):
        pl.semaphore_signal(barrier, inc=1, device_id={"dp": target}, device_id_type=MESH)
    for which in range(3):
        weights[:, which * HEAD : (which + 1) * HEAD] = three[which]

    def group(h, a):
        slots = [jnp.where(h == 0, a * SIDE + s, s * SIDE + a) for s in range(SIDE)]
        rows = jnp.concatenate([d_all[slot_at[one]] for one in slots], axis=0)
        cols = pl.ds(pl.multiple_of(h * wide, wide), wide)
        value = lax.dot_general(rows, weights[cols, :], NT, preferred_element_type=F32).astype(BF16)
        for s in range(SIDE):
            terms[h, a, s] = value[s * BLK : (s + 1) * BLK, :]

    def first_send(h, d, s):
        a, b = place[h]
        return pltpu.make_async_remote_copy(
            src_ref=terms.at[h, turn(a, 2), s, :, halves[d]], dst_ref=got1.at[h, d, s],
            send_sem=send1.at[h, d, s], recv_sem=recv1.at[h, d, s],
            device_id={SEQ: slot(h, turn(a, 1 - 2 * d), b)}, device_id_type=MESH,
        )

    def second_send(h, d, s):
        a, b = place[h]
        return pltpu.make_async_remote_copy(
            src_ref=snd2.at[h, d, s], dst_ref=got2.at[h, d, s],
            send_sem=send2.at[h, d, s], recv_sem=recv2.at[h, d, s],
            device_id={SEQ: slot(h, turn(a, 1 - 2 * d), b)}, device_id_type=MESH,
        )

    def third_send(h, d):
        a, b = place[h]
        return pltpu.make_async_remote_copy(
            src_ref=sums.at[h, turn(b, 2), :, halves[d]], dst_ref=last1.at[h, d],
            send_sem=send3.at[h, d], recv_sem=recv3.at[h, d],
            device_id={SEQ: slot(h, a, turn(b, 1 - 2 * d))}, device_id_type=MESH,
        )

    def fourth_send(h, d):
        a, b = place[h]
        return pltpu.make_async_remote_copy(
            src_ref=lasts2.at[h, d], dst_ref=last2.at[h, d],
            send_sem=send4.at[h, d], recv_sem=recv4.at[h, d],
            device_id={SEQ: slot(h, a, turn(b, 1 - 2 * d))}, device_id_type=MESH,
        )

    def group_far(h, carry):
        group(h, turn(jnp.where(h == 0, row, col), 2))
        return carry

    def group_rest(g, carry):
        h, which = lax.rem(g, 2), g // 2
        by = jnp.where(which == 0, 1, jnp.where(which == 1, SIDE - 1, 0))
        group(h, turn(jnp.where(h == 0, row, col), by))
        return carry

    lax.fori_loop(0, 2, group_far, 0)
    pl.semaphore_wait(barrier, 7)
    reduce.pair().start()
    for k in (2, 1, 3, 0):
        for h in range(2):
            s = turn(place[h][1], k)
            for d in range(2):
                first_send(h, d, s).start()
    lax.fori_loop(0, 2, group_rest, 0)
    reduce.stage1()
    lax.fori_loop(2, 6, group_rest, 0)
    reduce.stage2()
    for k in (2, 1, 3, 0):
        for h in range(2):
            a, b = place[h]
            s = turn(b, k)
            for d in range(2):
                first_send(h, d, s).wait_recv()
                near = turn(a, 1 - 2 * d)
                other = halves[1 - d]
                snd2[h, d, s, :, other] = terms[h, near, s, :, other]
                snd2[h, d, s, :, halves[d]] = (
                    terms[h, near, s, :, halves[d]].astype(F32) + got1[h, d, s].astype(F32)
                ).astype(BF16)
                second_send(h, d, s).start()
    reduce.stage3()
    for k in (2, 1, 3, 0):
        for h in range(2):
            a, b = place[h]
            s = turn(b, k)
            for d in range(2):
                second_send(h, d, s).wait_recv()
            total = (
                terms[h, a, s].astype(F32) + got2[h, 0, s].astype(F32) + got2[h, 1, s].astype(F32)
            )
            if k != 0:
                sums[h, s] = total.astype(BF16)
            if k == 2:
                for d in range(2):
                    third_send(h, d).start()
            elif k != 0:
                d = 0 if k == 1 else 1
                third_send(h, d).wait_recv()
                other = halves[1 - d]
                lasts2[h, d, :, other] = sums[h, s, :, other]
                lasts2[h, d, :, halves[d]] = (total[:, halves[d]] + last1[h, d].astype(F32)).astype(BF16)
                fourth_send(h, d).start()
            else:
                for d in range(2):
                    fourth_send(h, d).wait_recv()
                out[:, h * wide : (h + 1) * wide] = (
                    total + last2[h, 0].astype(F32) + last2[h, 1].astype(F32)
                ).astype(BF16)
        if k == 2:
            reduce.stage4()
        elif k == 1:
            reduce.stage5()
        elif k == 3:
            reduce.stage6(summed)
    for h in range(2):
        for d in range(2):
            for s in range(SIDE):
                first_send(h, d, s).wait_send()
                second_send(h, d, s).wait_send()
            third_send(h, d).wait_send()
            fourth_send(h, d).wait_send()


def scatter_terms(dest, d_all, three, value, ident):
    blocks, _, local = d_all.shape
    full = three.shape[1]
    wide = full // 2
    part = wide // 2
    vmem = pl.BlockSpec(memory_space=pltpu.VMEM)
    four = pltpu.SemaphoreType.DMA((2, 2, SIDE))
    two = pltpu.SemaphoreType.DMA((2, 2))
    return pl.pallas_call(
        scatter_kernel,
        out_shape=(jax.ShapeDtypeStruct((BLK, full), BF16), jax.ShapeDtypeStruct(value.shape, BF16)),
        in_specs=[pl.BlockSpec(memory_space=pltpu.SMEM), vmem, vmem, vmem],
        out_specs=[vmem, vmem],
        scratch_shapes=[
            pltpu.SMEM((blocks,), jnp.int32),
            pltpu.VMEM((full, local), BF16),
            pltpu.VMEM((2, SIDE, SIDE, BLK, wide), BF16),
            pltpu.VMEM((2, 2, SIDE, BLK, part), BF16),
            pltpu.VMEM((2, 2, SIDE, BLK, wide), BF16),
            pltpu.VMEM((2, 2, SIDE, BLK, wide), BF16),
            pltpu.VMEM((2, SIDE, BLK, wide), BF16),
            pltpu.VMEM((2, 2, BLK, part), BF16),
            pltpu.VMEM((2, 2, BLK, wide), BF16),
            pltpu.VMEM((2, 2, BLK, wide), BF16),
            four, four, four, four, two, two, two, two,
            *Reduce.scratch(value.shape),
        ],
        compiler_params=pltpu.CompilerParams(
            collective_id=ident, has_side_effects=True, vmem_limit_bytes=VMEM_LIMIT
        ),
        cost_estimate=pl.CostEstimate(
            flops=2 * blocks * BLK * local * full, bytes_accessed=100 * 1024 * 1024, transcendentals=0
        ),
        name="scatter_terms",
    )(dest, d_all, three, value)


def assemble_kernel(dest, table, head, rest, sorted_out, summed, out, causal_out, grads):
    kept = sorted_out.shape[0] // BLK
    late = table[3 * pl.program_id(0)] == 1
    grads[...] = summed[...].astype(F32)

    @pl.when(pl.program_id(0) == 0)
    def _():
        for j in range(kept):
            causal_out[pl.ds(pl.multiple_of(dest[j] * BLK, BLK), BLK), :] = sorted_out[j * BLK : (j + 1) * BLK, :]

    @pl.when(late)
    def _():
        out[...] = rest[...]

    @pl.when(jnp.logical_not(late))
    def _():
        out[...] = head[...]


def assemble(dest, table, head, rest, sorted_out, summed):
    rows, full = head.shape
    steps = 2 * rows // BLK
    whole = pl.BlockSpec(sorted_out.shape, lambda g, d, t: (0, 0))
    part = pl.BlockSpec((3, full // steps, HEAD), lambda g, d, t: (0, g, 0))
    return pl.pallas_call(
        assemble_kernel,
        out_shape=(
            jax.ShapeDtypeStruct((2 * rows, full), BF16),
            jax.ShapeDtypeStruct(sorted_out.shape, BF16),
            jax.ShapeDtypeStruct(summed.shape, F32),
        ),
        grid_spec=pltpu.PrefetchScalarGridSpec(
            num_scalar_prefetch=2,
            grid=(steps,),
            in_specs=[
                pl.BlockSpec((BLK, full), lambda g, d, t: (t[3 * g + 1], 0)),
                pl.BlockSpec((BLK, full), lambda g, d, t: (t[3 * g + 2], 0)),
                whole,
                part,
            ],
            out_specs=[pl.BlockSpec((BLK, full), lambda g, d, t: (g, 0)), whole, part],
        ),
        compiler_params=pltpu.CompilerParams(vmem_limit_bytes=VMEM_LIMIT),
        name="assemble",
    )(dest, table, head, rest, sorted_out, summed)


def shards(query_input, key_input, value_input, keep_blocks, dest_slots, proj_weights, cotangent):
    tok, full = query_input.shape[1:]
    per_shard = tok // BLK
    kept = keep_blocks.shape[1]
    query = query_input.reshape(per_shard, BLK, full)
    key = key_input[0]
    value = value_input[0]
    first, gathered, qkv, scale, table = front(keep_blocks, query, key, value, proj_weights, 2, 0)
    sorted_out, d_all, local_grads, rest = causal(
        dest_slots, keep_blocks, qkv, scale, cotangent.reshape(kept, BLK, -1), gathered, query, key, value, 4, 1
    )
    row_grad, summed = scatter_terms(
        dest_slots, d_all.reshape(kept, BLK, -1), proj_weights,
        local_grads.reshape(3, 2, SIDE, full // 2 // SIDE, HEAD), 2,
    )
    window_out, causal_out, grads = assemble(
        dest_slots[0], table, first, rest, sorted_out, summed.reshape(proj_weights.shape)
    )
    return (window_out[None], causal_out[None], grads, row_grad[None])


def solution(mesh):
    return jax.shard_map(
        shards,
        mesh=mesh,
        in_specs=(
            P("dp", "seq", None),
            P("dp", "seq", None),
            P("dp", "seq", None),
            P("dp", None),
            P("dp", None),
            P(None, None, "seq"),
            P("dp", None, "seq"),
        ),
        out_specs=(
            P("dp", "seq", None),
            P("dp", None, "seq"),
            P(None, None, "seq"),
            P("dp", "seq", None),
        ),
        check_vma=False,
    )
```

```python
import functools

import jax
import jax.numpy as jnp
from jax import lax
from jax.experimental import pallas as pl
from jax.experimental.pallas import tpu as pltpu
from jax.sharding import PartitionSpec as P

HEAD = 128
BLK = 128
SEQ = "seq"
MESH = pl.DeviceIdType.MESH
SCALE = HEAD ** (-0.5)
LOG2E = 1.4426950408889634
SCALE2 = SCALE * LOG2E
LOW = -1e30
NT = (((1,), (1,)), ((), ()))
BF16 = jnp.bfloat16
F32 = jnp.float32
VMEM_LIMIT = 56 * 1024 * 1024


def window_parts(heads):
    def scores_of(query, key, value_t, bias):
        scores = lax.dot_general(key, query, NT, preferred_element_type=F32)
        if bias is not None:
            scores = scores + bias
        return scores, jnp.max(scores, axis=0, keepdims=True), value_t

    def rest_of(scores, top, value_t):
        weight = jnp.exp2((scores - top) * SCALE2)
        total = jnp.sum(weight, axis=0, keepdims=True)
        out = jnp.dot(value_t, weight.astype(BF16), preferred_element_type=F32)
        return out * (1.0 / total), top * SCALE2 + jnp.log2(total)

    done = []
    ahead = scores_of(*heads[0])
    for h in range(len(heads)):
        current = ahead
        if h + 1 < len(heads):
            ahead = scores_of(*heads[h + 1])
        done.append(rest_of(*current))
    return done


def merged(out_a, lse_a, out_b, lse_b):
    top = jnp.maximum(lse_a, lse_b)
    weight_a = jnp.exp2(lse_a - top)
    weight_b = jnp.exp2(lse_b - top)
    total = weight_a + weight_b
    return out_a * (weight_a / total) + out_b * (weight_b / total), top + jnp.log2(total)


def block_ranks(keep, shard, per_shard):
    kept = [
        functools.reduce(
            lambda found, j: jnp.where(keep[0, j] == shard * per_shard + b, 1, found), range(keep.shape[1]), 0
        )
        for b in range(per_shard)
    ]
    total = sum(kept)
    return [
        jnp.where(kept[b] == 1, sum(kept[:b], 0), total + b - sum(kept[:b], 0)) for b in range(per_shard)
    ]


def picked(ranks, places):
    return [functools.reduce(lambda got, b: jnp.where(ranks[b] == at, b, got), range(len(ranks)), 0) for at in places]


def near_ranks(keep, per_shard):
    shard, count = lax.axis_index(SEQ), lax.axis_size(SEQ)
    return [block_ranks(keep, lax.rem(shard + by, count), per_shard) for by in range(3)]


class Flow:
    def __init__(self, sel, q_in, k_in, v_in, out, scratch):
        (
            self.q_own, self.q_one, self.q_two, self.v_t, self.o_own, self.l_own, self.o_snd2, self.l_snd2,
            self.o_got2, self.l_got2, self.o_snd1, self.l_snd1, self.o_got1, self.l_got1,
            self.bias_own, self.bias_two, self.send_sem, self.recv_sem,
        ) = scratch
        self.sel, self.q_in, self.k_in, self.v_in, self.out = sel, q_in, k_in, v_in, out
        self.chunks, self.rows, self.width = self.q_own.shape
        self.per_chunk = self.width // HEAD
        self.lse_step = 8 // self.per_chunk
        self.shard = lax.axis_index(SEQ)
        count = lax.axis_size(SEQ)
        self.right = lax.rem(self.shard + 1, count)
        self.left = lax.rem(self.shard + count - 1, count)

    def copy(self, which, c, src, dst, target):
        return pltpu.make_async_remote_copy(
            src_ref=src.at[c], dst_ref=dst.at[c],
            send_sem=self.send_sem.at[which, c], recv_sem=self.recv_sem.at[which, c],
            device_id={SEQ: target}, device_id_type=MESH,
        )

    def hop_one(self, c):
        return self.copy(0, c, self.q_own, self.q_one, self.left)

    def hop_two(self, c):
        return self.copy(1, c, self.q_one, self.q_two, self.left)

    def back_two(self, c):
        return (
            self.copy(2, c, self.o_snd2, self.o_got2, self.right),
            self.copy(3, c, self.l_snd2, self.l_got2, self.right),
        )

    def back_one(self, c):
        return (
            self.copy(4, c, self.o_snd1, self.o_got1, self.right),
            self.copy(5, c, self.l_snd1, self.l_got1, self.right),
        )

    def begin(self, ahead, others=()):
        barrier = pltpu.get_barrier_semaphore()
        greeted = (self.left, self.right, *others)
        for neighbour in greeted:
            pl.semaphore_signal(barrier, inc=1, device_id={SEQ: neighbour}, device_id_type=MESH)
        picks = self.rows // BLK
        for a in range(picks):
            block = self.q_in[self.sel[a]]
            for c in range(self.chunks):
                self.q_own[c, a * BLK : (a + 1) * BLK, :] = block[:, c * self.width : (c + 1) * self.width]
        pl.semaphore_wait(barrier, len(greeted))
        for c in range(ahead):
            self.hop_one(c).start()
        self.ahead = ahead
        lane = lax.broadcasted_iota(jnp.int32, (1, self.rows), 1)
        key_at = lax.broadcasted_iota(jnp.int32, self.bias_own.shape, 0)
        for base, ref in ((0, self.bias_own), (2 * picks, self.bias_two)):
            place = lane
            for a in range(picks):
                place = jnp.where(lane // BLK == a, (lane - a * BLK) + self.sel[base + a] * BLK, place)
            seen = (key_at <= place) if base == 0 else (key_at > place)
            ref[...] = jnp.where(seen, 0.0, LOW)

    def cols(self, c, h):
        return pl.ds(pl.multiple_of(c * self.width + h * HEAD, HEAD), HEAD)

    def lse_at(self, h):
        return slice(h * self.lse_step, (h + 1) * self.lse_step)

    def spread(self, row):
        return jnp.broadcast_to(row, (self.lse_step, self.rows))

    def head(self, h):
        return slice(h * HEAD, (h + 1) * HEAD)

    def pump(self, c):
        self.hop_one(c).wait_recv()
        self.hop_two(c).start()

        @pl.when(c + self.ahead < self.chunks)
        def _():
            self.hop_one(c + self.ahead).start()

    def own(self, c):
        heads = []
        for h in range(self.per_chunk):
            cols = self.cols(c, h)
            value_t = self.v_in[:, cols].T
            self.v_t[cols, :] = value_t
            heads.append((self.q_own[c, :, self.head(h)], self.k_in[:, cols], value_t, self.bias_own[...]))
        for h, (part, lse) in enumerate(window_parts(heads)):
            self.o_own[c, self.head(h), :] = part
            self.l_own[c, self.lse_at(h), :] = self.spread(lse)

    def two(self, c):
        self.hop_two(c).wait_recv()
        heads = [
            (self.q_two[c, :, self.head(h)], self.k_in[:, self.cols(c, h)], self.v_t[self.cols(c, h), :], self.bias_two[...])
            for h in range(self.per_chunk)
        ]
        for h, (part, lse) in enumerate(window_parts(heads)):
            self.o_snd2[c, self.head(h), :] = part.astype(BF16)
            self.l_snd2[c, self.lse_at(h), :] = self.spread(lse)
        for each in self.back_two(c):
            each.start()

    def incoming(self, got, h, c):
        first = h * self.lse_step
        return jnp.where(self.shard == 0, LOW, got[c, first : first + 1, :])

    def one(self, c):
        parts = window_parts([
            (self.q_one[c, :, self.head(h)], self.k_in[:, self.cols(c, h)], self.v_t[self.cols(c, h), :], None)
            for h in range(self.per_chunk)
        ])
        for each in self.back_two(c):
            each.wait_recv()
        for h in range(self.per_chunk):
            part, lse = merged(
                *parts[h], self.o_got2[c, self.head(h), :].astype(F32), self.incoming(self.l_got2, h, c)
            )
            self.o_snd1[c, self.head(h), :] = part.astype(BF16)
            self.l_snd1[c, self.lse_at(h), :] = self.spread(lse)
        for each in self.back_one(c):
            each.start()

    def final(self, c):
        for each in self.back_one(c):
            each.wait_recv()
        for h in range(self.per_chunk):
            first = h * self.lse_step
            part, _ = merged(
                self.o_own[c, self.head(h), :], self.l_own[c, first : first + 1, :],
                self.o_got1[c, self.head(h), :].astype(F32), self.incoming(self.l_got1, h, c),
            )
            self.store(c, h, part.T.astype(BF16))

    def store(self, c, h, value):
        self.out[:, self.cols(c, h)] = value

    def step(self, t, lag):
        def stage(late, *calls):
            @pl.when((t >= late) & (t < self.chunks + late))
            def _():
                for call in calls:
                    call(t - late)

        stage(0, self.pump, self.own)
        stage(lag, self.two)
        stage(2 * lag, self.one)
        stage(3 * lag, self.final)

    def drain(self):
        def body(c, carry):
            self.hop_one(c).wait_send()
            self.hop_two(c).wait_send()
            for each in self.back_two(c) + self.back_one(c):
                each.wait_send()
            return carry

        lax.fori_loop(0, self.chunks, body, 0)

    @staticmethod
    def scratch(rows, tok, full, per_chunk):
        width = per_chunk * HEAD
        chunks = full // width
        queries = pltpu.VMEM((chunks, rows, width), BF16)
        outs = pltpu.VMEM((chunks, width, rows), BF16)
        lses = pltpu.VMEM((chunks, 8, rows), F32)
        return [
            queries, queries, queries, pltpu.VMEM((full, tok), BF16), pltpu.VMEM((chunks, width, rows), F32), lses,
            outs, lses, outs, lses, outs, lses, outs, lses,
            pltpu.VMEM((tok, rows), F32), pltpu.VMEM((tok, rows), F32),
            pltpu.SemaphoreType.DMA((6, chunks)), pltpu.SemaphoreType.DMA((6, chunks)),
        ]


SIDE = 4


class Spread:
    OFFSETS = (0, 1, SIDE - 1, 2)

    def __init__(self, got, send_sem, recv_sem):
        self.got, self.send_sem, self.recv_sem = got, send_sem, recv_sem
        shard = lax.axis_index(SEQ)
        row, col = shard // SIDE, lax.rem(shard, SIDE)
        self.here = ((col, row), (row, col))

    @staticmethod
    def turn(at, by):
        return lax.rem(at + by + SIDE, SIDE)

    @staticmethod
    def slot(kind, place):
        a, b = place
        return b * SIDE + a if kind == 0 else a * SIDE + b

    def neighbours(self):
        a, b = self.here[0]
        return [self.slot(0, (self.turn(a, by), b)) for by in (1, -1)] + [
            self.slot(0, (a, self.turn(b, by))) for by in (1, -1)
        ]

    def message(self, c, kind, group, place, half, target):
        slot = self.slot(kind, place)
        ref = self.got.at[c, kind, slot] if half is None else self.got.at[c, kind, slot, half]
        return pltpu.make_async_remote_copy(
            src_ref=ref, dst_ref=ref, send_sem=self.send_sem.at[c, kind], recv_sem=self.recv_sem.at[c, kind, group],
            device_id={SEQ: self.slot(kind, target)}, device_id_type=MESH,
        )

    def whole(self, c, kind, group, pieces):
        a, b = self.here[kind]
        ref = self.got.at[c, kind, pl.ds(0, pieces)]
        return pltpu.make_async_remote_copy(
            src_ref=ref, dst_ref=ref, send_sem=self.send_sem.at[c, kind], recv_sem=self.recv_sem.at[c, kind, group],
            device_id={SEQ: self.slot(kind, (self.turn(a, 1), b))}, device_id_type=MESH,
        )

    def ring(self, c, kind, group, here, up, down, to_up, to_down):
        if group % 2 == 0:
            pairs = ((here, None, to_up), (here, None, to_down))
        else:
            pairs = ((down, 0, to_up), (up, 1, to_down))
        for pair in pairs:
            self.message(c, kind, group, *pair).start()

    def first(self, c, kind, group):
        a, b = self.here[kind]
        up, down = (self.turn(a, 1), b), (self.turn(a, -1), b)
        self.ring(c, kind, group, (a, b), up, down, up, down)

    def second(self, c, kind, group, k):
        a, b = self.here[kind]
        origin = self.turn(a, self.OFFSETS[k])
        up, down = self.turn(b, 1), self.turn(b, -1)
        self.ring(c, kind, group, (origin, b), (origin, up), (origin, down), (a, up), (a, down))

    def launch(self, c):
        for kind in range(2):
            self.first(c, kind, 0)

    def relay(self, c):
        for kind in range(2):
            self.whole(c, kind, 0, 2).wait_recv()
            self.first(c, kind, 1)
            for k in range(3):
                self.second(c, kind, 2, k)

    def relay_far(self, c):
        for kind in range(2):
            self.whole(c, kind, 1, 1).wait_recv()
            self.second(c, kind, 2, 3)

    def second_relay(self, c):
        for kind in range(2):
            self.whole(c, kind, 2, 8).wait_recv()
            for k in range(4):
                self.second(c, kind, 3, k)

    def settle(self, c):
        for kind in range(2):
            self.whole(c, kind, 3, 4).wait_recv()

    def drain(self, c):
        for kind in range(2):
            self.whole(c, kind, 0, 15).wait_send()


def front_kernel(
    keep, q_in, k_in, v_in, three, out, rows_out, projected, scale_out, table,
    weights, got, held, staged, staged_sem, total, squares, spread_send, spread_recv, *scratch,
):
    kept = keep.shape[1]
    per_shard = q_in.shape[0]
    ranks = near_ranks(keep, per_shard)
    half = per_shard // 2
    sel = [at for each in ranks for at in picked(each, range(half))]
    for b in range(per_shard):
        late = jnp.where(ranks[0][b] >= half, 1, 0)
        table[3 * b] = late
        table[3 * b + 1] = ranks[0][b] * (1 - late)
        table[3 * b + 2] = (ranks[0][b] - half) * late
    owner = [keep[0, j] // per_shard for j in range(kept)]
    nth = [0] + [jnp.where(owner[j] == owner[j - 1], 1, 0) for j in range(1, kept)]
    flow = Flow(sel, q_in, k_in, v_in, out, scratch)
    spread = Spread(got, spread_send, spread_recv)
    chunks, width = flow.chunks, flow.width
    total_rows, local = projected.shape
    full = k_in.shape[1]
    block = 512
    per_kind = flow.per_chunk // 2

    def store(c, h, value):
        out[:, flow.cols(c, h)] = value
        for a in range(flow.rows // BLK):
            got[c, h // per_kind, flow.shard, a, :, flow.head(h % per_kind)] = value[a * BLK : (a + 1) * BLK, :]

    flow.store = store
    flow.begin(3, spread.neighbours())
    for which in range(3):
        weights[:, which * HEAD : (which + 1) * HEAD] = three[which]
    total[...] = jnp.zeros_like(total)
    squares[...] = jnp.zeros_like(squares)

    def staged_copy(c):
        which = lax.rem(c, 2)
        return pltpu.make_async_copy(staged.at[which], rows_out.at[c], staged_sem.at[which])

    def project_chunk(c):
        which = lax.rem(c, 2)

        @pl.when(c >= 2)
        def _():
            staged_copy(c - 2).wait()

        def hold(i, carry):
            for kind in range(2):
                held[i, :, :, kind * width // 2 : (kind + 1) * width // 2] = got[c, kind, i]
            return carry

        lax.fori_loop(0, SIDE * SIDE, hold, 0)

        for j in range(kept):
            staged[which, j * BLK : (j + 1) * BLK, :] = held[owner[j], nth[j]]
        staged_copy(c).start()
        weight = weights[pl.ds(pl.multiple_of(c * width, width), width), :]

        def multiply(r, carry):
            at = pl.ds(pl.multiple_of(r * block, block), block)
            rows = staged[which, at, :]
            total[at, :] += jnp.dot(rows, weight, preferred_element_type=F32)
            wide = rows.astype(F32)
            square = wide * wide
            squares[at, :] += sum(square[:, h * HEAD : (h + 1) * HEAD] for h in range(flow.per_chunk))
            return carry

        lax.fori_loop(0, total_rows // block, multiply, 0)

    def step(t, carry):
        flow.step(t, 1)

        def stage(late, call):
            @pl.when((t >= late) & (t < chunks + late))
            def _():
                call(t - late)

        stage(3, spread.launch)
        stage(4, spread.relay)
        stage(5, spread.relay_far)
        stage(6, spread.second_relay)

        @pl.when(t >= 7)
        def _():
            spread.settle(t - 7)
            project_chunk(t - 7)

        return carry

    lax.fori_loop(0, chunks + 7, step, 0)

    def finish(r, carry):
        at = pl.ds(pl.multiple_of(r * block, block), block)
        square = squares[at, :]
        inv = lax.rsqrt(jnp.sum(square, axis=1, keepdims=True) * (1.0 / full) + 1e-06)
        projected[at, :] = (total[at, :] * inv).astype(BF16)
        scale_out[:, at] = lax.rsqrt(jnp.sum(square.T, axis=0, keepdims=True) * (1.0 / full) + 1e-06)
        return carry

    lax.fori_loop(0, total_rows // block, finish, 0)

    def drain(c, carry):
        spread.drain(c)
        return carry

    lax.fori_loop(0, chunks, drain, 0)
    for c in (chunks - 2, chunks - 1):
        staged_copy(c).wait()
    flow.drain()


def front(keep, query, key, value, weights, per_chunk, ident):
    tok, full = key.shape
    local = 3 * HEAD
    rows = query.shape[0] // 2 * BLK
    total_rows = keep.shape[1] * BLK
    width = per_chunk * HEAD
    chunks = full // width
    vmem = pl.BlockSpec(memory_space=pltpu.VMEM)
    smem = pl.BlockSpec(memory_space=pltpu.SMEM)
    return pl.pallas_call(
        front_kernel,
        out_shape=(
            jax.ShapeDtypeStruct((rows, full), BF16),
            jax.ShapeDtypeStruct((chunks, total_rows, width), BF16),
            jax.ShapeDtypeStruct((total_rows, local), BF16),
            jax.ShapeDtypeStruct((1, total_rows), F32),
            jax.ShapeDtypeStruct((3 * query.shape[0],), jnp.int32),
        ),
        in_specs=[smem, vmem, vmem, vmem, vmem],
        out_specs=[vmem, pl.BlockSpec(memory_space=pl.ANY), vmem, vmem, smem],
        scratch_shapes=[
            pltpu.VMEM((full, local), BF16),
            pltpu.VMEM((chunks, 2, SIDE * SIDE, rows // BLK, BLK, width // 2), BF16),
            pltpu.VMEM((SIDE * SIDE, rows // BLK, BLK, width), BF16),
            pltpu.VMEM((2, total_rows, width), BF16),
            pltpu.SemaphoreType.DMA((2,)),
            pltpu.VMEM((total_rows, local), F32),
            pltpu.VMEM((total_rows, HEAD), F32),
            pltpu.SemaphoreType.DMA((chunks, 2)),
            pltpu.SemaphoreType.DMA((chunks, 2, 4)),
            *Flow.scratch(rows, tok, full, per_chunk),
        ],
        compiler_params=pltpu.CompilerParams(
            collective_id=ident, has_side_effects=True, vmem_limit_bytes=VMEM_LIMIT
        ),
        name="front",
    )(keep, query, key, value, weights)


QB = 256
KB = 512


def causal_kernel(
    dest, keep, qkv, scale, cot, gathered, q_in, k_in, v_in, out, d_all, grads, rest,
    rows_in, rows_sem, d_all_t, v_t, k_t, do_own, do_t, p_buf, dk_acc, dv_acc, dq_t, *scratch,
):
    kept = dest.shape[1]
    total_rows = qkv.shape[0]
    per_shard = q_in.shape[0]
    sel = [at for each in near_ranks(keep, per_shard) for at in picked(each, range(per_shard // 2, per_shard))]
    blocks = total_rows // QB
    rows_copy = pltpu.make_async_copy(gathered, rows_in, rows_sem)
    rows_copy.start()
    flow = Flow(sel, q_in, k_in, v_in, rest, scratch)
    flow.begin(3)

    for j in range(kept):
        do_own[j * BLK : (j + 1) * BLK, :] = cot[dest[0, j]]

    def prepare(c, carry):
        at = pl.ds(pl.multiple_of(c * QB, QB), QB)
        k_t[:, at] = qkv[at, HEAD : 2 * HEAD].T
        v_t[:, at] = qkv[at, 2 * HEAD : 3 * HEAD].T
        do_t[:, at] = do_own[at, :].T
        return carry

    lax.fori_loop(0, blocks, prepare, 0)
    dk_acc[...] = jnp.zeros_like(dk_acc)
    dv_acc[...] = jnp.zeros_like(dv_acc)

    def query_block(i):
        rows = pl.ds(pl.multiple_of(i * QB, QB), QB)
        chunks = (i * QB + QB + KB - 1) // KB
        q_i = qkv[rows, :HEAD]
        do_i = do_own[rows, :]

        def scores_of(c, masked):
            keys = pl.ds(pl.multiple_of(c * KB, KB), KB)
            scores = lax.dot_general(qkv[keys, HEAD : 2 * HEAD], q_i, NT, preferred_element_type=F32)
            if masked:
                key_at = lax.broadcasted_iota(jnp.int32, (KB, QB), 0)
                row_at = lax.broadcasted_iota(jnp.int32, (KB, QB), 1)
                scores = jnp.where(key_at - row_at <= i * QB - (chunks - 1) * KB, scores, LOW)
            p_buf[keys, :] = scores
            return jnp.max(scores, axis=0, keepdims=True)

        top = lax.fori_loop(
            0, chunks - 1, lambda c, m: jnp.maximum(m, scores_of(c, False)), scores_of(chunks - 1, True)
        )

        def weigh(c, carry):
            total, acc = carry
            keys = pl.ds(pl.multiple_of(c * KB, KB), KB)
            weight = jnp.exp2((p_buf[keys, :] - top) * SCALE2)
            p_buf[keys, :] = weight
            total = total + jnp.sum(weight, axis=0, keepdims=True)
            acc = acc + jnp.dot(v_t[:, keys], weight.astype(BF16), preferred_element_type=F32)
            return total, acc

        total, acc = lax.fori_loop(
            0, chunks, weigh, (jnp.zeros((1, QB), F32), jnp.zeros((HEAD, QB), F32))
        )
        inv = 1.0 / total
        o_t = acc * inv
        delta = jnp.sum(o_t * do_t[:, rows].astype(F32), axis=0, keepdims=True)
        out[rows, :] = o_t.T.astype(BF16)

        def back(c, acc):
            keys = pl.ds(pl.multiple_of(c * KB, KB), KB)
            soft = p_buf[keys, :] * inv
            dv_acc[keys, :] += jnp.dot(soft.astype(BF16), do_i, preferred_element_type=F32)
            d_probs = lax.dot_general(qkv[keys, 2 * HEAD :], do_i, NT, preferred_element_type=F32)
            d_scores = (soft * (d_probs - delta) * SCALE).astype(BF16)
            dk_acc[keys, :] += jnp.dot(d_scores, q_i, preferred_element_type=F32)
            return acc + jnp.dot(k_t[:, keys], d_scores, preferred_element_type=F32)

        dq_t[:, rows] = lax.fori_loop(0, chunks, back, jnp.zeros((HEAD, QB), F32))

    def finish(c, carry):
        at = pl.ds(pl.multiple_of(c * QB, QB), QB)
        d_q = dq_t[:, at]
        d_all_t[:HEAD, at] = (d_q * scale[:, at]).astype(BF16)
        d_all[at, :HEAD] = d_q.T.astype(BF16)
        for which, acc in ((1, dk_acc), (2, dv_acc)):
            value = acc[at, :]
            d_all[at, which * HEAD : (which + 1) * HEAD] = value.astype(BF16)
            d_all_t[which * HEAD : (which + 1) * HEAD, at] = (value.T * scale[:, at]).astype(BF16)
        return carry

    def weight_block(g, carry):
        wide = rows_in.shape[2]
        at = pl.ds(pl.multiple_of(g * wide, wide), wide)
        value = jnp.dot(d_all_t[...], rows_in[g], preferred_element_type=F32)
        for which in range(3):
            grads[which, at, :] = value[which * HEAD : (which + 1) * HEAD, :].T.astype(BF16)
        return carry

    col_blocks = rows_in.shape[0]
    halves = blocks // flow.chunks
    share = (col_blocks + 2 * halves - 1) // (2 * halves)

    def step(u, carry):
        t, r = u // halves, lax.rem(u, halves)

        def stage(at, late, *calls):
            @pl.when((r == at) & (t >= late) & (t < flow.chunks + late))
            def _():
                for call in calls:
                    call(t - late)

        stage(0, 0, flow.own)

        @pl.when(u < blocks)
        def _():
            query_block(blocks - 1 - u)

        stage(0, 0, flow.pump)
        stage(0, 1, flow.two)
        stage(halves - 1, 2, flow.one)
        stage(halves - 1, 3, flow.final)

        @pl.when(u == blocks)
        def _():
            lax.fori_loop(0, blocks, finish, 0)
            rows_copy.wait()

        @pl.when(u >= blocks)
        def _():
            low = (u - blocks) * share
            lax.fori_loop(low, jnp.minimum(low + share, col_blocks), weight_block, 0)

        return carry

    lax.fori_loop(0, (flow.chunks + 3) * halves, step, 0)
    flow.drain()


def causal(dest, keep, qkv, scale, cot, gathered, query, key, value, per_chunk, ident):
    total_rows, local = qkv.shape
    tok, full = key.shape
    rows = query.shape[0] // 2 * BLK
    vmem = pl.BlockSpec(memory_space=pltpu.VMEM)
    smem = pl.BlockSpec(memory_space=pltpu.SMEM)
    return pl.pallas_call(
        causal_kernel,
        out_shape=(
            jax.ShapeDtypeStruct((total_rows, HEAD), BF16),
            jax.ShapeDtypeStruct((total_rows, local), BF16),
            jax.ShapeDtypeStruct((3, full, HEAD), BF16),
            jax.ShapeDtypeStruct((rows, full), BF16),
        ),
        in_specs=[smem, smem, vmem, vmem, vmem, pl.BlockSpec(memory_space=pl.ANY), vmem, vmem, vmem],
        out_specs=[vmem, vmem, vmem, vmem],
        scratch_shapes=[
            pltpu.VMEM(gathered.shape, BF16),
            pltpu.SemaphoreType.DMA,
            pltpu.VMEM((local, total_rows), BF16),
            pltpu.VMEM((HEAD, total_rows), BF16),
            pltpu.VMEM((HEAD, total_rows), BF16),
            pltpu.VMEM((total_rows, HEAD), BF16),
            pltpu.VMEM((HEAD, total_rows), BF16),
            pltpu.VMEM((total_rows, QB), F32),
            pltpu.VMEM((total_rows, HEAD), F32),
            pltpu.VMEM((total_rows, HEAD), F32),
            pltpu.VMEM((HEAD, total_rows), F32),
            *Flow.scratch(rows, tok, full, per_chunk),
        ],
        compiler_params=pltpu.CompilerParams(
            collective_id=ident, has_side_effects=True, vmem_limit_bytes=VMEM_LIMIT
        ),
        cost_estimate=pl.CostEstimate(
            flops=20 * 10**9, bytes_accessed=32 * 1024 * 1024, transcendentals=0
        ),
        name="causal",
    )(dest, keep, qkv, scale, cot, gathered, query, key, value)


class Reduce:
    def __init__(self, value, pair_got, own, snd, got1, got2, whole, send_sem, recv_sem):
        self.value, self.pair_got, self.own, self.snd = value, pair_got, own, snd
        self.got1, self.got2, self.whole = got1, got2, whole
        self.send_sem, self.recv_sem = send_sem, recv_sem
        at = lax.axis_index("dp")
        self.y, self.core = at // 2, lax.rem(at, 2)
        self.partner = self.y * 2 + 1 - self.core
        self.next = [self.turn(by) * 2 + self.core for by in (1, -1)]
        middle = value.shape[3] // 2
        self.halves = (slice(0, middle), slice(middle, 2 * middle))

    def turn(self, by):
        return lax.rem(self.y + by + SIDE, SIDE)

    def copy(self, which, src, dst, target):
        return pltpu.make_async_remote_copy(
            src_ref=src, dst_ref=dst, send_sem=self.send_sem.at[which], recv_sem=self.recv_sem.at[which],
            device_id={"dp": target}, device_id_type=MESH,
        )

    def pair(self):
        return self.copy(0, self.value.at[:, 1 - self.core], self.pair_got, self.partner)

    def ring1(self, d):
        return self.copy(1 + d, self.snd.at[d, 0, :, self.halves[0]], self.got1.at[d], self.next[d])

    def ring2(self, d):
        return self.copy(3 + d, self.snd.at[d, 1], self.got2.at[d], self.next[d])

    def quarter(self, by, half=None):
        ref = self.whole.at[:, self.core, self.turn(by)]
        return ref if half is None else self.whole.at[:, self.core, self.turn(by), self.halves[half]]

    def spread1(self, d, by):
        return self.copy(5 + d, self.quarter(by), self.quarter(by), self.next[d])

    def spread2(self, d, by):
        return self.copy(7 + d, self.quarter(by, d), self.quarter(by, d), self.next[d])

    def back(self, core):
        return self.copy(9, self.whole.at[:, core], self.whole.at[:, core], self.partner)

    def stage1(self):
        self.pair().wait_recv()

        def add(q, carry):
            self.own[q] = self.value[:, self.core, q].astype(F32) + self.pair_got[:, q].astype(F32)
            return carry

        lax.fori_loop(0, SIDE, add, 0)
        for d in range(2):
            self.snd[d, 0, :, self.halves[0]] = self.own[self.turn(2), :, self.halves[d]].astype(BF16)
            self.ring1(d).start()

    def stage2(self):
        for d in range(2):
            self.ring1(d).wait_recv()
            near = self.turn(1 - 2 * d)
            self.snd[d, 1, :, self.halves[1 - d]] = self.own[near, :, self.halves[1 - d]].astype(BF16)
            self.snd[d, 1, :, self.halves[d]] = (
                self.own[near, :, self.halves[d]] + self.got1[d].astype(F32)
            ).astype(BF16)
            self.ring2(d).start()

    def stage3(self):
        for d in range(2):
            self.ring2(d).wait_recv()
        total = self.own[self.y] + self.got2[0].astype(F32) + self.got2[1].astype(F32)
        self.whole[:, self.core, self.y] = total.astype(BF16)
        for d in range(2):
            self.spread1(d, 0).start()

    def stage4(self):
        for d in range(2):
            self.spread1(d, 2 * d - 1).wait_recv()
            self.spread2(d, 2 * d - 1).start()

    def stage5(self):
        for d in range(2):
            self.spread2(d, 2).wait_recv()
        self.back(self.core).start()

    def stage6(self, out):
        self.back(1 - self.core).wait_recv()
        out[...] = self.whole[...]
        self.pair().wait_send()
        for d in range(2):
            self.ring1(d).wait_send()
            self.ring2(d).wait_send()
            self.spread1(d, 0).wait_send()
            self.spread2(d, 2 * d - 1).wait_send()
        self.back(self.core).wait_send()

    @staticmethod
    def scratch(shape):
        three, _, quarters, rows, width = shape
        return [
            pltpu.VMEM((three, quarters, rows, width), BF16),
            pltpu.VMEM((quarters, three, rows, width), F32),
            pltpu.VMEM((2, 2, three, rows, width), BF16),
            pltpu.VMEM((2, three, rows // 2, width), BF16),
            pltpu.VMEM((2, three, rows, width), BF16),
            pltpu.VMEM(shape, BF16),
            pltpu.SemaphoreType.DMA((10,)),
            pltpu.SemaphoreType.DMA((10,)),
        ]


def scatter_kernel(
    dest, d_all, three, value, out, summed, slot_at, weights, terms, got1, snd2, got2, sums, last1, lasts2, last2,
    send1, recv1, send2, recv2, send3, recv3, send4, recv4, *reduce_scratch,
):
    shard = lax.axis_index(SEQ)
    row, col = shard // SIDE, lax.rem(shard, SIDE)
    wide = out.shape[1] // 2
    part = wide // 2
    place = ((row, col), (col, row))
    halves = (slice(0, part), slice(part, wide))

    def turn(at, by):
        return lax.rem(at + by + SIDE, SIDE)

    def slot(h, a, b):
        return a * SIDE + b if h == 0 else b * SIDE + a

    barrier = pltpu.get_barrier_semaphore()
    for by in (1, -1):
        for h in range(2):
            a, b = place[h]
            pl.semaphore_signal(
                barrier, inc=1, device_id={SEQ: slot(h, turn(a, by), b)}, device_id_type=MESH
            )
    kept = dest.shape[1]
    for at in range(kept):
        slot_at[at] = functools.reduce(lambda got, j: jnp.where(dest[0, j] == at, j, got), range(kept), 0)
    reduce = Reduce(value, *reduce_scratch)
    for target in (reduce.partner, *reduce.next):
        pl.semaphore_signal(barrier, inc=1, device_id={"dp": target}, device_id_type=MESH)
    for which in range(3):
        weights[:, which * HEAD : (which + 1) * HEAD] = three[which]

    def group(h, a):
        slots = [jnp.where(h == 0, a * SIDE + s, s * SIDE + a) for s in range(SIDE)]
        rows = jnp.concatenate([d_all[slot_at[one]] for one in slots], axis=0)
        cols = pl.ds(pl.multiple_of(h * wide, wide), wide)
        value = lax.dot_general(rows, weights[cols, :], NT, preferred_element_type=F32).astype(BF16)
        for s in range(SIDE):
            terms[h, a, s] = value[s * BLK : (s + 1) * BLK, :]

    def first_send(h, d, s):
        a, b = place[h]
        return pltpu.make_async_remote_copy(
            src_ref=terms.at[h, turn(a, 2), s, :, halves[d]], dst_ref=got1.at[h, d, s],
            send_sem=send1.at[h, d, s], recv_sem=recv1.at[h, d, s],
            device_id={SEQ: slot(h, turn(a, 1 - 2 * d), b)}, device_id_type=MESH,
        )

    def second_send(h, d, s):
        a, b = place[h]
        return pltpu.make_async_remote_copy(
            src_ref=snd2.at[h, d, s], dst_ref=got2.at[h, d, s],
            send_sem=send2.at[h, d, s], recv_sem=recv2.at[h, d, s],
            device_id={SEQ: slot(h, turn(a, 1 - 2 * d), b)}, device_id_type=MESH,
        )

    def third_send(h, d):
        a, b = place[h]
        return pltpu.make_async_remote_copy(
            src_ref=sums.at[h, turn(b, 2), :, halves[d]], dst_ref=last1.at[h, d],
            send_sem=send3.at[h, d], recv_sem=recv3.at[h, d],
            device_id={SEQ: slot(h, a, turn(b, 1 - 2 * d))}, device_id_type=MESH,
        )

    def fourth_send(h, d):
        a, b = place[h]
        return pltpu.make_async_remote_copy(
            src_ref=lasts2.at[h, d], dst_ref=last2.at[h, d],
            send_sem=send4.at[h, d], recv_sem=recv4.at[h, d],
            device_id={SEQ: slot(h, a, turn(b, 1 - 2 * d))}, device_id_type=MESH,
        )

    def group_far(h, carry):
        group(h, turn(jnp.where(h == 0, row, col), 2))
        return carry

    def group_rest(g, carry):
        h, which = lax.rem(g, 2), g // 2
        by = jnp.where(which == 0, 1, jnp.where(which == 1, SIDE - 1, 0))
        group(h, turn(jnp.where(h == 0, row, col), by))
        return carry

    lax.fori_loop(0, 2, group_far, 0)
    pl.semaphore_wait(barrier, 7)
    reduce.pair().start()
    for k in (2, 1, 3, 0):
        for h in range(2):
            s = turn(place[h][1], k)
            for d in range(2):
                first_send(h, d, s).start()
    lax.fori_loop(0, 2, group_rest, 0)
    reduce.stage1()
    lax.fori_loop(2, 6, group_rest, 0)
    reduce.stage2()
    for k in (2, 1, 3, 0):
        for h in range(2):
            a, b = place[h]
            s = turn(b, k)
            for d in range(2):
                first_send(h, d, s).wait_recv()
                near = turn(a, 1 - 2 * d)
                other = halves[1 - d]
                snd2[h, d, s, :, other] = terms[h, near, s, :, other]
                snd2[h, d, s, :, halves[d]] = (
                    terms[h, near, s, :, halves[d]].astype(F32) + got1[h, d, s].astype(F32)
                ).astype(BF16)
                second_send(h, d, s).start()
    reduce.stage3()
    for k in (2, 1, 3, 0):
        for h in range(2):
            a, b = place[h]
            s = turn(b, k)
            for d in range(2):
                second_send(h, d, s).wait_recv()
            total = (
                terms[h, a, s].astype(F32) + got2[h, 0, s].astype(F32) + got2[h, 1, s].astype(F32)
            )
            if k != 0:
                sums[h, s] = total.astype(BF16)
            if k == 2:
                for d in range(2):
                    third_send(h, d).start()
            elif k != 0:
                d = 0 if k == 1 else 1
                third_send(h, d).wait_recv()
                other = halves[1 - d]
                lasts2[h, d, :, other] = sums[h, s, :, other]
                lasts2[h, d, :, halves[d]] = (total[:, halves[d]] + last1[h, d].astype(F32)).astype(BF16)
                fourth_send(h, d).start()
            else:
                for d in range(2):
                    fourth_send(h, d).wait_recv()
                out[:, h * wide : (h + 1) * wide] = (
                    total + last2[h, 0].astype(F32) + last2[h, 1].astype(F32)
                ).astype(BF16)
        if k == 2:
            reduce.stage4()
        elif k == 1:
            reduce.stage5()
        elif k == 3:
            reduce.stage6(summed)
    for h in range(2):
        for d in range(2):
            for s in range(SIDE):
                first_send(h, d, s).wait_send()
                second_send(h, d, s).wait_send()
            third_send(h, d).wait_send()
            fourth_send(h, d).wait_send()


def scatter_terms(dest, d_all, three, value, ident):
    blocks, _, local = d_all.shape
    full = three.shape[1]
    wide = full // 2
    part = wide // 2
    vmem = pl.BlockSpec(memory_space=pltpu.VMEM)
    four = pltpu.SemaphoreType.DMA((2, 2, SIDE))
    two = pltpu.SemaphoreType.DMA((2, 2))
    return pl.pallas_call(
        scatter_kernel,
        out_shape=(jax.ShapeDtypeStruct((BLK, full), BF16), jax.ShapeDtypeStruct(value.shape, BF16)),
        in_specs=[pl.BlockSpec(memory_space=pltpu.SMEM), vmem, vmem, vmem],
        out_specs=[vmem, vmem],
        scratch_shapes=[
            pltpu.SMEM((blocks,), jnp.int32),
            pltpu.VMEM((full, local), BF16),
            pltpu.VMEM((2, SIDE, SIDE, BLK, wide), BF16),
            pltpu.VMEM((2, 2, SIDE, BLK, part), BF16),
            pltpu.VMEM((2, 2, SIDE, BLK, wide), BF16),
            pltpu.VMEM((2, 2, SIDE, BLK, wide), BF16),
            pltpu.VMEM((2, SIDE, BLK, wide), BF16),
            pltpu.VMEM((2, 2, BLK, part), BF16),
            pltpu.VMEM((2, 2, BLK, wide), BF16),
            pltpu.VMEM((2, 2, BLK, wide), BF16),
            four, four, four, four, two, two, two, two,
            *Reduce.scratch(value.shape),
        ],
        compiler_params=pltpu.CompilerParams(
            collective_id=ident, has_side_effects=True, vmem_limit_bytes=VMEM_LIMIT
        ),
        cost_estimate=pl.CostEstimate(
            flops=2 * blocks * BLK * local * full, bytes_accessed=100 * 1024 * 1024, transcendentals=0
        ),
        name="scatter_terms",
    )(dest, d_all, three, value)


def assemble_kernel(dest, table, head, rest, sorted_out, summed, out, causal_out, grads):
    kept = sorted_out.shape[0] // BLK
    late = table[3 * pl.program_id(0)] == 1
    grads[...] = summed[...].astype(F32)

    @pl.when(pl.program_id(0) == 0)
    def _():
        for j in range(kept):
            causal_out[pl.ds(pl.multiple_of(dest[j] * BLK, BLK), BLK), :] = sorted_out[j * BLK : (j + 1) * BLK, :]

    @pl.when(late)
    def _():
        out[...] = rest[...]

    @pl.when(jnp.logical_not(late))
    def _():
        out[...] = head[...]


def assemble(dest, table, head, rest, sorted_out, summed):
    rows, full = head.shape
    steps = 2 * rows // BLK
    whole = pl.BlockSpec(sorted_out.shape, lambda g, d, t: (0, 0))
    part = pl.BlockSpec((3, full // steps, HEAD), lambda g, d, t: (0, g, 0))
    return pl.pallas_call(
        assemble_kernel,
        out_shape=(
            jax.ShapeDtypeStruct((2 * rows, full), BF16),
            jax.ShapeDtypeStruct(sorted_out.shape, BF16),
            jax.ShapeDtypeStruct(summed.shape, F32),
        ),
        grid_spec=pltpu.PrefetchScalarGridSpec(
            num_scalar_prefetch=2,
            grid=(steps,),
            in_specs=[
                pl.BlockSpec((BLK, full), lambda g, d, t: (t[3 * g + 1], 0)),
                pl.BlockSpec((BLK, full), lambda g, d, t: (t[3 * g + 2], 0)),
                whole,
                part,
            ],
            out_specs=[pl.BlockSpec((BLK, full), lambda g, d, t: (g, 0)), whole, part],
        ),
        compiler_params=pltpu.CompilerParams(vmem_limit_bytes=VMEM_LIMIT),
        name="assemble",
    )(dest, table, head, rest, sorted_out, summed)


def shards(query_input, key_input, value_input, keep_blocks, dest_slots, proj_weights, cotangent):
    tok, full = query_input.shape[1:]
    per_shard = tok // BLK
    kept = keep_blocks.shape[1]
    query = query_input.reshape(per_shard, BLK, full)
    key = key_input[0]
    value = value_input[0]
    first, gathered, qkv, scale, table = front(keep_blocks, query, key, value, proj_weights, 2, 0)
    sorted_out, d_all, local_grads, rest = causal(
        dest_slots, keep_blocks, qkv, scale, cotangent.reshape(kept, BLK, -1), gathered, query, key, value, 2, 1
    )
    row_grad, summed = scatter_terms(
        dest_slots, d_all.reshape(kept, BLK, -1), proj_weights,
        local_grads.reshape(3, 2, SIDE, full // 2 // SIDE, HEAD), 2,
    )
    window_out, causal_out, grads = assemble(
        dest_slots[0], table, first, rest, sorted_out, summed.reshape(proj_weights.shape)
    )
    return (window_out[None], causal_out[None], grads, row_grad[None])


def solution(mesh):
    return jax.shard_map(
        shards,
        mesh=mesh,
        in_specs=(
            P("dp", "seq", None),
            P("dp", "seq", None),
            P("dp", "seq", None),
            P("dp", None),
            P("dp", None),
            P(None, None, "seq"),
            P("dp", None, "seq"),
        ),
        out_specs=(
            P("dp", "seq", None),
            P("dp", None, "seq"),
            P(None, None, "seq"),
            P("dp", "seq", None),
        ),
        check_vma=False,
    )
```
